32 devices in a mesh: dp: 4 (over y, x), tensor: 8 (over z, core).
Axes of the slice: x: 2, y: 2, z: 4, core: 2. Of those that a mesh axis runs over, the one named last changes fastest.
Arguments:
- hidden_in: bfloat16 [8192, 2048], P(('dp', 'tensor')), parts along dimension 0, may hold values from -6 to 6
- attn_gain: float32 [2048], replicated, may hold values from 0.1 to 1.9
- attn_shift: float32 [2048], replicated, may hold values from -3 to 3
- qkv_weight: bfloat16 [2048, 6144], P(None, 'tensor'), may hold values from -4 to 4
- qkv_bias: bfloat16 [6144], P('tensor'), may hold values from -3 to 3
- out_weight: bfloat16 [2048, 2048], P('tensor'), may hold values from -0.125 to 0.125
- out_bias: float32 [2048], replicated, may hold values from -3 to 3
- mlp_gain: float32 [2048], replicated, may hold values from 0.1 to 1.9
- mlp_shift: float32 [2048], replicated, may hold values from -3 to 3
- up_weight: bfloat16 [2048, 8192], P(None, 'tensor'), may hold values from -0.125 to 0.125
- up_bias: float32 [8192], P('tensor'), may hold values from -3 to 3
- down_weight: bfloat16 [8192, 2048], P('tensor'), may hold values from -0.0625 to 0.0625
- down_bias: float32 [2048], replicated, may hold values from -3 to 3
- segment_ids: int32 [4, 2048], P('dp'), parts along dimension 0, may hold values from 0 to 7, never falling along the last dimension, each value on 1 to 1024 neighbouring positions
- prompt_lengths: int32 [4], P('dp'), parts along dimension 0, may hold values from 1024 to 2048
- page_table: int32 [512, 1], P('dp'), parts along dimension 0, may hold values from 0 to 7; in each aligned block of 128 rows (0 to 127, 128 to 255, ...) at most 32 rows name the same one
Outputs:
- layer_out: bfloat16 [8192, 2048], P(('dp', 'tensor')), parts along dimension 0
- kv_pages: bfloat16 [1024, 16, 4096], P(('dp', 'tensor')), parts along dimension 0
The draws below stay inside these ranges and needn't reach their ends.
There are 4 independent parts, one for each index of `dp`. The reference program is written for one: setup_inputs(seed, part) draws one part's arguments, and reference() takes and returns one part's arrays. A program takes and returns all parts, laid end to end along the dimension named above; an argument that names none is the same for every part. Nothing has to cross between parts.
Inputs may be any that keep to these rules, and one draw needn't show every extreme that they name: `segment_ids`: along a stream document numbers never fall; a document has at most 1024 tokens. `page_table`: no device owns more than 32 pages of a part, and one owns exactly 32.
All inputs are finite; a program needn't handle non-finite values.
Results may differ from the reference program's by a relative error of at most 0.014.
Values may be sent and summed in bfloat16 or wider, within the bound.
A program may use at most 128 MiB of HBM per device.

```python
import math
import jax
import jax.numpy as jnp
import numpy as np
from jax import lax

D = 2048
H = 16
HD = 128
FF = 8192
LEN = 2048
STREAMS = 1
PAGE = 16
DOCS = 8
TOKENS = 2048
PAIRS = 4
HPD = 4
FF_DEV = 1024
BLOCKS = 128
CAP = 32
N_TENSOR = 8


def draw_qkv_weight(key, part):
    first_key = jax.random.fold_in(key, 0)
    drawn_all = jax.random.normal(first_key, (D, H, 3, HD), jnp.float32) / math.sqrt(D)
    return jnp.clip(drawn_all, -4.0, 4.0).reshape(D, H * 3 * HD).astype(jnp.bfloat16)


def steps_of(key, extent, shards, least, high):
    gain, own = 1.0, jax.random.fold_in(key, 6)
    for axis_at, parts in shards:
        steps = jnp.exp(jax.random.uniform(jax.random.fold_in(own, axis_at), (parts,), jnp.float32, least / len(shards), high / len(shards)))
        gain = gain * jnp.repeat(steps, extent[axis_at] // parts).reshape([-1 if axis == axis_at else 1 for axis in range(len(extent))])
    return gain


def length_profile(number_of, total, most, lean):
    portions = [(1 << 20) // math.isqrt(grade ** lean) + 1 for grade in range(2, number_of + 1)]
    spare, given = total - most - (number_of - 1), [1] * (number_of - 1)
    while spare > 0:
        candidates = [i for i in range(number_of - 1) if given[i] < most]
        pool, remaining = sum([portions[i] for i in candidates]), spare
        for i in candidates:
            more = min(most - given[i], max(1, remaining * portions[i] // pool), spare)
            given[i] = given[i] + more
            spare = spare - more
    return np.array([most] + given)


def uneven(stream_key, number_of, total, most, skew):
    if number_of == 2:
        one = jax.random.randint(stream_key, (), max(1, total - most), min(most, total - 1) + 1)
        return jnp.stack([one, total - one])
    tallies = jnp.asarray(length_profile(number_of, total, most, skew), jnp.int32)
    pairs = (number_of - 1) // 2
    giver, taker = tallies[1:1 + 2 * pairs:2], tallies[2:2 + 2 * pairs:2]
    margin = jnp.minimum(giver - 1, most - taker)
    moved = jax.random.randint(jax.random.fold_in(stream_key, 1), (pairs,), 0, 1 << 20) % (margin + 1)
    tallies = tallies.at[1:1 + 2 * pairs:2].set(giver - moved).at[2:2 + 2 * pairs:2].set(taker + moved)
    return tallies[jax.random.permutation(jax.random.fold_in(stream_key, 2), number_of)]


def shared_out(rng, own, number, rows, amount, top, reach, lean):
    order = jax.random.permutation(rng, amount)
    packed, ordinary = load_shares(amount, rows * top, reach, lean, True), load_shares(amount, rows * top, reach, lean, False)
    places = jnp.arange(amount)

    def named(sizes, rotation):
        used = int((sizes > 0).sum())
        fixed = max(1, used // 4)
        shifted = fixed + (places - fixed + rotation * (used - fixed)) % max(1, amount - fixed)
        return jnp.zeros((amount,), jnp.int32).at[order[jnp.where(places < fixed, places, shifted)]].set(jnp.asarray(sizes, jnp.int32))

    sizes = jnp.where(number % 4 == 0, named(packed, number // 4), named(ordinary, number - number // 4 - 1))
    mixed = jax.random.permutation(jax.random.fold_in(own, 3), amount)
    giver, taker = mixed[0:amount // 2 * 2:2], mixed[1:amount // 2 * 2:2]
    room = jnp.minimum(sizes[giver] - 1, reach - sizes[taker]) // 2
    room = jnp.where((giver == order[0]) | (taker == order[0]) | (sizes[taker] == 0), 0, jnp.maximum(room, 0))
    shifted = jax.random.randint(jax.random.fold_in(own, 4), (amount // 2,), 0, 1 << 20) % (room + 1)
    sizes = sizes.at[giver].add(-shifted).at[taker].add(shifted)
    items = jnp.searchsorted(jnp.cumsum(sizes), jnp.arange(rows * top), side="right").astype(jnp.int32)
    table = items.reshape(top, rows).T
    table = table[jax.random.permutation(jax.random.fold_in(own, 1), rows)]
    rotation = jax.random.randint(jax.random.fold_in(own, 2), (rows, 1), 0, top)
    return jnp.take_along_axis(table, (jnp.arange(top)[None, :] + rotation) % top, axis=1)


def load_shares(number_of, total, most, skew, full):
    portions = [(1 << 20) // math.isqrt(rank ** skew) + 1 for rank in range(1, number_of + 1)]
    largest = most if full else min(most, max(-(-total // number_of), total * portions[0] // sum(portions)))
    least = 1 if total - largest >= number_of - 1 else 0
    given, surplus = [largest] + [least] * (number_of - 1), total - largest - least * (number_of - 1)
    while surplus > 0:
        movable = [i for i in range(1, number_of) if given[i] < largest] or [i for i in range(1, number_of) if given[i] < most]
        pool, left = sum([portions[i] for i in movable]), surplus
        for i in movable:
            extra = min(most - given[i], max(1, left * portions[i] // pool), surplus)
            given[i] = given[i] + extra
            surplus = surplus - extra
    return np.array(given)


def noise(own_key, shape, scale, limit, cuts=(), held_as=jnp.bfloat16):
    entries = jax.random.normal(own_key, shape, jnp.float32) * scale
    if len(cuts) > 0:
        entries = steps_of(own_key, shape, cuts, -0.22, 0.18) * entries
    return jnp.clip(entries, min=-limit, max=limit).astype(held_as)


def setup_inputs(seed: int = 0, part: int = 0) -> dict:
    splits = jax.random.split(jax.random.key(seed), 17)
    own_keys = jax.random.split(jax.random.fold_in(splits[16], part), 17)
    hidden_in = noise(own_keys[0], (TOKENS, D), 1.0, 6.0, ((0, 8),))
    attn_gain = jnp.clip(1.0 + 0.18 * jax.random.normal(splits[1], (D,), jnp.float32), 0.1, 1.9)
    attn_shift = noise(splits[2], (D,), 0.5, 3.0, (), jnp.float32)
    qkv_weight = draw_qkv_weight(jax.random.fold_in(splits[16], 71), part)
    qkv_bias = noise(splits[4], (3 * H * HD,), 0.5, 3.0, ((0, 8),))
    out_weight = noise(splits[5], (H * HD, D), (H * HD) ** -0.5, 0.125, ((0, 8),))
    out_bias = noise(splits[6], (D,), 0.5, 3.0, (), jnp.float32)
    mlp_gain = jnp.clip(1.0 + 0.18 * jax.random.normal(splits[7], (D,), jnp.float32), 0.1, 1.9)
    mlp_shift = noise(splits[8], (D,), 0.5, 3.0, (), jnp.float32)
    up_weight = noise(splits[9], (D, FF), D ** -0.5, 0.125, ((1, 8),))
    up_bias = noise(splits[10], (FF,), 0.5, 3.0, ((0, 8),), jnp.float32)
    down_weight = noise(splits[11], (FF, D), FF ** -0.5, 0.0625, ((0, 8),))
    down_bias = noise(splits[12], (D,), 0.5, 3.0, (), jnp.float32)
    segment_ids = jax.vmap(lambda own: jnp.searchsorted(jnp.cumsum(uneven(own, DOCS, LEN, LEN // 2, 2)), jnp.arange(LEN), side="right"))(jax.random.split(own_keys[13], STREAMS)).reshape((STREAMS, LEN)).astype(jnp.int32)
    prompt_lengths = jax.random.randint(own_keys[14], (STREAMS,), LEN // 2, LEN + 1).astype(jnp.int32)
    page_table_keys = jax.random.split(jax.random.fold_in(own_keys[15], 1), BLOCKS // BLOCKS)
    page_table_turns = jax.random.permutation(jax.random.fold_in(own_keys[15], 3), BLOCKS // BLOCKS)
    page_table = jax.vmap(lambda own, number: shared_out(jax.random.fold_in(own_keys[15], 2), own, number, BLOCKS, N_TENSOR, 1, CAP, 2))(page_table_keys, page_table_turns).reshape((BLOCKS, 1))
    return dict(hidden_in=hidden_in, attn_gain=attn_gain, attn_shift=attn_shift, qkv_weight=qkv_weight, qkv_bias=qkv_bias, out_weight=out_weight, out_bias=out_bias, mlp_gain=mlp_gain, mlp_shift=mlp_shift, up_weight=up_weight, up_bias=up_bias, down_weight=down_weight, down_bias=down_bias, segment_ids=segment_ids, prompt_lengths=prompt_lengths, page_table=page_table)


def normalize(values, norm_gain, norm_shift):
    widened = values.astype(jnp.float32)
    center = lax.optimization_barrier(jnp.mean(widened, axis=-1, keepdims=True))
    spread = lax.optimization_barrier(jnp.mean(jnp.square(widened - center), axis=-1, keepdims=True))
    return (widened - center) * lax.rsqrt(spread + 1e-05) * norm_gain + norm_shift

def attend_head(queries, keys_here, values_here, segments):
    raw_scores = jnp.dot(queries, keys_here.T, preferred_element_type=jnp.float32) * (1.0 / math.sqrt(HD))
    position = jnp.arange(LEN, dtype=jnp.int32)
    allowed = (position[None, :] <= position[:, None]) & (segments[None, :] == segments[:, None])
    raw_scores = jnp.where(allowed, raw_scores, -jnp.inf)
    row_max = lax.optimization_barrier(jnp.max(raw_scores, axis=1, keepdims=True))
    expo = jnp.exp(raw_scores - row_max)
    weights = (expo / lax.optimization_barrier(jnp.sum(expo, axis=1, keepdims=True))).astype(jnp.bfloat16)
    return jnp.dot(weights, values_here, preferred_element_type=jnp.float32).astype(jnp.bfloat16)

def reference(hidden_in, attn_gain, attn_shift, qkv_weight, qkv_bias, out_weight, out_bias, mlp_gain, mlp_shift, up_weight, up_bias, down_weight, down_bias, segment_ids, prompt_lengths, page_table):
    normed = normalize(hidden_in, attn_gain, attn_shift).astype(jnp.bfloat16)
    projected = (jnp.dot(normed, qkv_weight, preferred_element_type=jnp.float32) + qkv_bias.astype(jnp.float32)).astype(jnp.bfloat16)
    grid = projected.reshape(STREAMS, LEN, H, 3, HD)

    def one_head(flat_index):
        stream_id = flat_index // H
        head_id = flat_index % H
        stream_block = lax.dynamic_index_in_dim(grid, stream_id, 0, keepdims=False)
        head_block = lax.dynamic_index_in_dim(stream_block, head_id, 1, keepdims=False)
        segments = lax.dynamic_index_in_dim(segment_ids, stream_id, 0, keepdims=False)
        return attend_head(head_block[:, 0], head_block[:, 1], head_block[:, 2], segments)
    attended = lax.map(one_head, jnp.arange(STREAMS * H, dtype=jnp.int32))
    attended = attended.reshape(STREAMS, H, LEN, HD).transpose(0, 2, 1, 3).reshape(TOKENS, H * HD)

    def head_group(running, group):
        columns = lax.dynamic_slice_in_dim(attended, group * (HPD * HD), HPD * HD, 1)
        rows_part = lax.dynamic_slice_in_dim(out_weight, group * (HPD * HD), HPD * HD, 0)
        term = jnp.dot(columns, rows_part, preferred_element_type=jnp.float32).astype(jnp.bfloat16)
        term = lax.optimization_barrier(term)
        return (running + term.astype(jnp.float32), None)
    attn_sum, _unused = lax.scan(head_group, jnp.zeros((TOKENS, D), jnp.float32), jnp.arange(PAIRS, dtype=jnp.int32))
    residual_mid = (hidden_in.astype(jnp.float32) + attn_sum + out_bias).astype(jnp.bfloat16)
    normed_mid = normalize(residual_mid, mlp_gain, mlp_shift).astype(jnp.bfloat16)
    expanded = jax.nn.gelu(jnp.dot(normed_mid, up_weight, preferred_element_type=jnp.float32) + up_bias.astype(jnp.float32), approximate=False).astype(jnp.bfloat16)

    def unit_group(running, group):
        columns = lax.dynamic_slice_in_dim(expanded, group * FF_DEV, FF_DEV, 1)
        rows_part = lax.dynamic_slice_in_dim(down_weight, group * FF_DEV, FF_DEV, 0)
        term = jnp.dot(columns, rows_part, preferred_element_type=jnp.float32).astype(jnp.bfloat16)
        term = lax.optimization_barrier(term)
        return (running + term.astype(jnp.float32), None)
    mlp_sum, _unused = lax.scan(unit_group, jnp.zeros((TOKENS, D), jnp.float32), jnp.arange(FF // FF_DEV, dtype=jnp.int32))
    layer_out = (residual_mid.astype(jnp.float32) + mlp_sum + down_bias).astype(jnp.bfloat16)
    position = jnp.arange(LEN, dtype=jnp.int32)
    live_mask = (position[None, :] < prompt_lengths[:, None]).astype(jnp.bfloat16)
    kept_rows = grid[:, :, :, 1:, :] * live_mask[:, :, None, None, None]
    page_rows = kept_rows.reshape(BLOCKS, PAGE, H * 2 * HD)
    owners = page_table[:, 0].astype(jnp.int32)
    onehot = (owners[:, None] == jnp.arange(N_TENSOR, dtype=jnp.int32)[None, :]).astype(jnp.int32)
    earlier = jnp.cumsum(onehot, axis=0) - onehot
    slot_ids = owners * CAP + lax.optimization_barrier(jnp.sum(earlier * onehot, axis=1))
    kv_pages = jnp.zeros((N_TENSOR * CAP, PAGE, H * 2 * HD), jnp.bfloat16).at[slot_ids].set(page_rows)
    return (layer_out, kv_pages)
```

```python
import functools
import math

import jax
import jax.numpy as jnp
from jax import lax
from jax.experimental import pallas as pl
from jax.experimental.pallas import tpu as pltpu
from jax.sharding import PartitionSpec as P

HD = 128
PAGE = 16
MAX_DOC = 1024
Q_BLOCK = 256
CHUNKS = 2


def normalize(values, norm_gain, norm_shift):
    widened = values.astype(jnp.float32)
    center = jnp.mean(widened, axis=-1, keepdims=True)
    spread = jnp.mean(jnp.square(widened - center), axis=-1, keepdims=True)
    return (widened - center) * lax.rsqrt(spread + 1e-05) * norm_gain + norm_shift


def attend_kernel(window, seq_len, q_ref, k_ref, v_ref, qseg_ref, kseg_ref, out_ref):
    block = pl.program_id(2)
    rows = q_ref.shape[0]
    start = jnp.clip(block * rows - MAX_DOC, 0, seq_len - window)
    start = pl.multiple_of(start, 128)
    keys = k_ref[pl.ds(start, window), :]
    values = v_ref[pl.ds(start, window), :]
    scores = lax.dot_general(
        q_ref[...], keys, (((1,), (1,)), ((), ())), preferred_element_type=jnp.float32
    ) * (1.0 / math.sqrt(HD))
    query_pos = block * rows + lax.broadcasted_iota(jnp.int32, (rows, window), 0)
    key_pos = start + lax.broadcasted_iota(jnp.int32, (rows, window), 1)
    allowed = (key_pos <= query_pos) & (qseg_ref[...] == kseg_ref[0, :, pl.ds(start, window)])
    scores = jnp.where(allowed, scores, -1e30)
    expo = jnp.exp(scores - jnp.max(scores, axis=1, keepdims=True))
    weights = (expo * (1.0 / jnp.sum(expo, axis=1, keepdims=True))).astype(jnp.bfloat16)
    out_ref[...] = jnp.dot(weights, values, preferred_element_type=jnp.float32).astype(
        jnp.bfloat16
    )


def attend(projected, segment_ids):
    streams, seq_len = segment_ids.shape
    heads = projected.shape[1] // (3 * HD)
    blocks = seq_len // Q_BLOCK
    window = min(seq_len, MAX_DOC + Q_BLOCK)
    pairs = streams * heads * seq_len * window
    return pl.pallas_call(
        functools.partial(attend_kernel, window, seq_len),
        grid=(streams, heads, blocks),
        in_specs=[
            pl.BlockSpec((Q_BLOCK, HD), lambda s, n, i: (s * blocks + i, 3 * n)),
            pl.BlockSpec((seq_len, HD), lambda s, n, i: (s, 3 * n + 1)),
            pl.BlockSpec((seq_len, HD), lambda s, n, i: (s, 3 * n + 2)),
            pl.BlockSpec((Q_BLOCK, 1), lambda s, n, i: (s * blocks + i, 0)),
            pl.BlockSpec((1, 1, seq_len), lambda s, n, i: (s, 0, 0)),
        ],
        out_specs=pl.BlockSpec((Q_BLOCK, HD), lambda s, n, i: (s * blocks + i, n)),
        out_shape=jax.ShapeDtypeStruct((streams * seq_len, heads * HD), jnp.bfloat16),
        compiler_params=pltpu.CompilerParams(vmem_limit_bytes=24 << 20),
        cost_estimate=pl.CostEstimate(
            flops=4 * pairs * HD,
            bytes_accessed=2 * projected.size * 2,
            transcendentals=pairs,
        ),
    )(
        projected,
        projected,
        projected,
        segment_ids.reshape(streams * seq_len, 1),
        segment_ids.reshape(streams, 1, seq_len),
    )


def join_pair(value, axis, position):
    devices = lax.axis_size("tensor")
    other = lax.ppermute(value, "tensor", [(source, source ^ 1) for source in range(devices)])
    first = jnp.where(position % 2 == 0, value, other)
    second = jnp.where(position % 2 == 0, other, value)
    return jnp.concatenate([first, second], axis=axis)


def copy_page(index_ref, page_ref, out_ref):
    out_ref[...] = page_ref[...]


def take_pages(page_rows, index):
    block = (1,) + page_rows.shape[1:]
    return pl.pallas_call(
        copy_page,
        grid_spec=pltpu.PrefetchScalarGridSpec(
            num_scalar_prefetch=1,
            grid=(index.shape[0],),
            in_specs=[pl.BlockSpec(block, lambda i, index: (index[i], 0, 0))],
            out_specs=pl.BlockSpec(block, lambda i, index: (i, 0, 0)),
        ),
        out_shape=jax.ShapeDtypeStruct(index.shape + page_rows.shape[1:], page_rows.dtype),
    )(index, page_rows)


def pack_pages(keys_vals, live, page_table, capacity, position):
    devices = lax.axis_size("tensor")
    pages = keys_vals.shape[0] // PAGE
    owners = page_table[:, 0]
    numbers = jnp.arange(pages, dtype=jnp.int32)
    earlier = (owners[None, :] == owners[:, None]) & (numbers[None, :] < numbers[:, None])
    ranks = jnp.sum(earlier.astype(jnp.int32), axis=1)
    slot_ids = owners * capacity + ranks
    owner_order = position ^ jnp.arange(devices, dtype=jnp.int32)
    slots = owner_order[:, None] * capacity + jnp.arange(capacity, dtype=jnp.int32)[None, :]
    hits = slot_ids[None, :] == slots.reshape(-1)[:, None]
    source_page = jnp.sum(jnp.where(hits, numbers[None, :], 0), axis=1)
    live_pages = live.reshape(pages, PAGE).astype(jnp.int32)
    kept = jnp.sum(jnp.where(hits[:, :, None], live_pages[None], 0), axis=1) > 0
    page_rows = keys_vals.reshape(pages, PAGE, -1)
    taken = take_pages(page_rows, source_page)
    outgoing = jnp.where(kept[:, :, None], taken, 0).astype(jnp.bfloat16)
    return [
        lax.slice_in_dim(outgoing, apart * capacity, (apart + 1) * capacity, axis=0)
        for apart in range(devices)
    ]


def send_pages(pieces):
    devices = len(pieces)
    received = [pieces[0]]
    for apart in range(1, devices):
        hops = [(source, source ^ apart) for source in range(devices)]
        received.append(lax.ppermute(pieces[apart], "tensor", hops))
    return received


def lay_out_pages(received, position):
    devices = len(received)
    slots, page, width = received[0].shape
    laid = jnp.zeros((slots, page, devices * width), received[0].dtype)
    for apart in range(devices):
        laid = lax.dynamic_update_slice_in_dim(
            laid, received[apart], (position ^ apart) * width, axis=2
        )
    return laid


MESH = pl.DeviceIdType.MESH
LINE = 8
CHUNK = 32


def layer_norm(values, gain, shift):
    widened = values.astype(jnp.float32)
    center = jnp.mean(widened, axis=-1, keepdims=True)
    moved = widened - center
    spread = jnp.mean(moved * moved, axis=-1, keepdims=True)
    return moved * lax.rsqrt(spread + 1e-05) * gain + shift


def greet(me, chips):
    z, c = me // 2, lax.rem(me, 2)
    barrier = pltpu.get_barrier_semaphore()
    pl.semaphore_signal(barrier, inc=1, device_id={"tensor": 2 * z + 1 - c}, device_id_type=MESH)

    @pl.when(z > 0)
    def _():
        pl.semaphore_signal(barrier, inc=1, device_id={"tensor": me - 2}, device_id_type=MESH)

    @pl.when(z < chips - 1)
    def _():
        pl.semaphore_signal(barrier, inc=1, device_id={"tensor": me + 2}, device_id_type=MESH)

    peers = 1 + (z > 0).astype(jnp.int32) + (z < chips - 1).astype(jnp.int32)
    pl.semaphore_wait(barrier, peers)


def gather_project_kernel(
    chips, hid, w_hbm, b_ref, gain_ref, shift_ref, hall_out, proj_out,
    buf, w_ref, nrm, pbuf, ssem, rsem, lsem, psem, wsem,
):
    me = lax.axis_index("tensor")
    z, c = me // 2, lax.rem(me, 2)
    twin = 2 * z + 1 - c
    rows, width = hid.shape
    cols = w_ref.shape[1]
    load = pltpu.make_async_copy(w_hbm, w_ref, wsem.at[0])
    load.start()
    own = pltpu.make_async_copy(hid, buf.at[me], wsem.at[1])
    own.start()
    greet(me, chips)
    own.wait()

    def send(slot, device, way):
        pltpu.make_async_remote_copy(
            src_ref=buf.at[slot], dst_ref=buf.at[slot], send_sem=ssem.at[slot, way],
            recv_sem=rsem.at[slot], device_id={"tensor": device}, device_id_type=MESH,
        ).start()

    def sent(slot, way):
        pltpu.make_async_remote_copy(
            src_ref=buf.at[slot], dst_ref=buf.at[slot], send_sem=ssem.at[slot, way],
            recv_sem=rsem.at[slot], device_id={"tensor": twin}, device_id_type=MESH,
        ).wait_send()

    def arrived(slot):
        pltpu.make_async_copy(hid, buf.at[slot], rsem.at[slot]).wait()

    def compute(slot):
        pltpu.make_async_copy(buf.at[slot], hall_out.at[slot], lsem.at[slot]).start()

        @pl.loop(0, rows // 32)
        def _(i):
            part = pl.ds(pl.multiple_of(i * 32, 32), 32)
            nrm[part, :] = layer_norm(buf[slot, part, :], gain_ref[...], shift_ref[...]).astype(
                jnp.bfloat16
            )

        @pl.loop(0, cols // 256)
        def _(i):
            part = pl.ds(pl.multiple_of(i * 256, 256), 256)
            pbuf[slot, :, part] = (
                jnp.dot(nrm[...], w_ref[:, part], preferred_element_type=jnp.float32)
                + b_ref[:, part].astype(jnp.float32)
            ).astype(jnp.bfloat16)

        pltpu.make_async_copy(pbuf.at[slot], proj_out.at[slot], psem.at[slot]).start()

    @pl.when(z > 0)
    def _():
        send(me, me - 2, 0)

    @pl.when(z < chips - 1)
    def _():
        send(me, me + 2, 1)

    send(me, twin, 2)
    load.wait()
    compute(me)
    arrived(twin)
    compute(twin)
    for hop in range(1, chips):

        @pl.when(z - hop >= 0)
        def _():
            slot = me - 2 * hop
            arrived(slot)

            @pl.when(z < chips - 1)
            def _():
                send(slot, me + 2, 1)

            send(slot, twin, 2)

        @pl.when(z + hop < chips)
        def _():
            slot = me + 2 * hop
            arrived(slot)

            @pl.when(z > 0)
            def _():
                send(slot, me - 2, 0)

            send(slot, twin, 2)

        @pl.when(z - hop >= 0)
        def _():
            compute(me - 2 * hop)
            arrived(twin - 2 * hop)
            compute(twin - 2 * hop)

        @pl.when(z + hop < chips)
        def _():
            compute(me + 2 * hop)
            arrived(twin + 2 * hop)
            compute(twin + 2 * hop)

    for slot in range(2 * chips):
        pltpu.make_async_copy(buf.at[slot], hall_out.at[slot], lsem.at[slot]).wait()
        pltpu.make_async_copy(pbuf.at[slot], proj_out.at[slot], psem.at[slot]).wait()
    for origin in range(chips):
        slot = 2 * origin + c
        sent(slot, 2)

        @pl.when((origin >= z) & (z > 0))
        def _():
            sent(slot, 0)

        @pl.when((origin <= z) & (z < chips - 1))
        def _():
            sent(slot, 1)


def gather_project(hidden_in, qkv_weight, qkv_bias, gain, shift, devices):
    rows, width = hidden_in.shape
    cols = qkv_weight.shape[1]
    hbm, vmem = pl.BlockSpec(memory_space=pl.ANY), pl.BlockSpec(memory_space=pltpu.VMEM)
    total = rows * devices
    hall, proj = pl.pallas_call(
        functools.partial(gather_project_kernel, devices // 2),
        in_specs=[hbm, hbm, vmem, vmem, vmem],
        out_specs=[hbm, hbm],
        out_shape=[
            jax.ShapeDtypeStruct((devices, rows, width), jnp.bfloat16),
            jax.ShapeDtypeStruct((devices, rows, cols), jnp.bfloat16),
        ],
        scratch_shapes=[
            pltpu.VMEM((devices, rows, width), jnp.bfloat16),
            pltpu.VMEM((width, cols), jnp.bfloat16),
            pltpu.VMEM((rows, width), jnp.bfloat16),
            pltpu.VMEM((devices, rows, cols), jnp.bfloat16),
            pltpu.SemaphoreType.DMA((devices, 3)),
            pltpu.SemaphoreType.DMA((devices,)),
            pltpu.SemaphoreType.DMA((devices,)),
            pltpu.SemaphoreType.DMA((devices,)),
            pltpu.SemaphoreType.DMA((2,)),
        ],
        compiler_params=pltpu.CompilerParams(
            collective_id=0, has_side_effects=True, vmem_limit_bytes=32 << 20
        ),
        cost_estimate=pl.CostEstimate(
            flops=2 * total * width * cols,
            bytes_accessed=2 * (total * (width + cols) + width * cols),
            transcendentals=0,
        ),
        name="gather_project",
    )(
        hidden_in, qkv_weight, qkv_bias.reshape(1, cols), gain.reshape(1, width),
        shift.reshape(1, width),
    )
    return hall, proj


def mlp_kernel(
    chips, att, hall, outw_hbm, upw_hbm, dnw_hbm, outb_ref, gain_ref, shift_ref, upb_ref, dnb_ref,
    out_ref,
    ag, outw, upw, dnw, hbuf, res, nrm, exp_, own_res, par, tw, lin, rin,
    wsem, osem, hsem, ag_s, ag_r, tw_s, tw_r, rs_s, rs_r,
):
    me = lax.axis_index("tensor")
    z, c = me // 2, lax.rem(me, 2)
    twin = 2 * z + 1 - c
    devices = 2 * chips
    chunks = ag.shape[0]
    width = outw.shape[1]
    piece = att.shape[-1]
    hidden_units = upw.shape[1]
    rows = devices * CHUNK

    loads = [
        pltpu.make_async_copy(outw_hbm, outw, wsem.at[0]),
        pltpu.make_async_copy(upw_hbm, upw, wsem.at[1]),
        pltpu.make_async_copy(dnw_hbm, dnw, wsem.at[2]),
    ]

    def place(k, device):
        return ag.at[k, :, :, pl.ds(pl.multiple_of(device * piece, piece), piece)]

    def own_piece(k):
        part = pl.ds(pl.multiple_of(k * CHUNK, CHUNK), CHUNK)
        return pltpu.make_async_copy(att.at[:, part, :], place(k, me), osem.at[k])

    def hidden_part(k):
        part = pl.ds(pl.multiple_of(k * CHUNK, CHUNK), CHUNK)
        return pltpu.make_async_copy(hall.at[:, part, :], hbuf.at[lax.rem(k, 2)], hsem.at[lax.rem(k, 2)])

    @pl.loop(0, chunks)
    def _(k):
        own_piece(k).start()

    for load in loads:
        load.start()
    greet(me, chips)

    def piece_copy(k, origin, device, way):
        return pltpu.make_async_remote_copy(
            src_ref=place(k, origin), dst_ref=place(k, origin), send_sem=ag_s.at[k, origin, way],
            recv_sem=ag_r.at[k, origin], device_id={"tensor": device}, device_id_type=MESH,
        )

    def piece_wait(k, origin):
        piece_copy(k, origin, twin, 2).wait_recv()

    def twin_copy(k):
        return pltpu.make_async_remote_copy(
            src_ref=par.at[k, :, 1 - c], dst_ref=tw.at[k], send_sem=tw_s.at[k], recv_sem=tw_r.at[k],
            device_id={"tensor": twin}, device_id_type=MESH,
        )

    def right_copy(k, at):
        count = chips - 1 - at
        return pltpu.make_async_remote_copy(
            src_ref=par.at[k, pl.ds(at + 1, count), c], dst_ref=lin.at[k, pl.ds(chips - 1 - count, count)],
            send_sem=rs_s.at[k, 0], recv_sem=rs_r.at[k, 0],
            device_id={"tensor": me + 2}, device_id_type=MESH,
        )

    def left_copy(k, at):
        return pltpu.make_async_remote_copy(
            src_ref=par.at[k, pl.ds(0, at), c], dst_ref=rin.at[k, pl.ds(0, at)],
            send_sem=rs_s.at[k, 1], recv_sem=rs_r.at[k, 1],
            device_id={"tensor": me - 2}, device_id_type=MESH,
        )

    def lin_at(k, chip):
        return lin[k, chip - 1].astype(jnp.float32)

    def rin_at(k, chip):
        return rin[k, chip].astype(jnp.float32)

    def at_chunk(k, run):
        pl.when((k >= 0) & (k < chunks))(lambda: run(k))

    def first_hop(k):
        own_piece(k).wait()

        @pl.when(z > 0)
        def _():
            piece_copy(k, me, me - 2, 0).start()

        @pl.when(z < chips - 1)
        def _():
            piece_copy(k, me, me + 2, 1).start()

        piece_copy(k, me, twin, 2).start()

    def later_hop(hop, k):
        @pl.when(z - hop >= 0)
        def _():
            origin = me - 2 * hop
            piece_wait(k, origin)

            @pl.when(z < chips - 1)
            def _():
                piece_copy(k, origin, me + 2, 1).start()

            piece_copy(k, origin, twin, 2).start()

        @pl.when(z + hop < chips)
        def _():
            origin = me + 2 * hop
            piece_wait(k, origin)

            @pl.when(z > 0)
            def _():
                piece_copy(k, origin, me - 2, 0).start()

            piece_copy(k, origin, twin, 2).start()

    def join_twins(k):
        twin_copy(k).wait_recv()
        for chip in range(chips):
            par[k, chip, c] = (
                par[k, chip, c].astype(jnp.float32) + tw[k, chip].astype(jnp.float32)
            ).astype(jnp.bfloat16)

        @pl.when(z == 0)
        def _():
            right_copy(k, 0).start()

        @pl.when(z == chips - 1)
        def _():
            left_copy(k, chips - 1).start()

    def add_left(k, at):
        right_copy(k, at - 1).wait_recv()
        for chip in range(at, chips):
            par[k, chip, c] = (par[k, chip, c].astype(jnp.float32) + lin_at(k, chip)).astype(jnp.bfloat16)
        if at < chips - 1:
            right_copy(k, at).start()

    def add_right(k, at):
        left_copy(k, at + 1).wait_recv()
        for chip in range(0, at + 1):
            par[k, chip, c] = (par[k, chip, c].astype(jnp.float32) + rin_at(k, chip)).astype(jnp.bfloat16)
        if at > 0:
            left_copy(k, at).start()

    def pass_on(hop, k):
        for at in range(1, chips):
            if at == hop:

                @pl.when(z == at)
                def _():
                    add_left(k, at)

                @pl.when(z == chips - 1 - at)
                def _():
                    add_right(k, chips - 1 - at)

    def finish(k):
        part = pl.ds(pl.multiple_of(k * CHUNK, CHUNK), CHUNK)
        out_ref[part, :] = (
            own_res[part, :].astype(jnp.float32) + par[k, z, c].astype(jnp.float32) + dnb_ref[...]
        ).astype(jnp.bfloat16)

    def compute(k):
        for hop in range(1, chips):

            @pl.when(z - hop >= 0)
            def _():
                piece_wait(k, twin - 2 * hop)

            @pl.when(z + hop < chips)
            def _():
                piece_wait(k, twin + 2 * hop)

        piece_wait(k, twin)
        hidden_part(k).wait()
        slot = lax.rem(k, 2)

        @pl.when(k + 1 < chunks)
        def _():
            hidden_part(k + 1).start()

        @pl.when(k == 0)
        def _():
            for load in loads:
                load.wait()

        @pl.loop(0, width // 256)
        def _(i):
            part = pl.ds(pl.multiple_of(i * 256, 256), 256)
            terms = jnp.dot(
                ag[k].reshape(rows, width), outw[:, part], preferred_element_type=jnp.float32
            )
            res[:, :, part] = (
                hbuf[slot, :, :, part].astype(jnp.float32)
                + terms.reshape(devices, CHUNK, 256)
                + outb_ref[:, part].reshape(1, 1, 256)
            ).astype(jnp.bfloat16)

        @pl.loop(0, devices)
        def _(d):
            nrm[pl.ds(pl.multiple_of(d * CHUNK, CHUNK), CHUNK), :] = layer_norm(
                res[d], gain_ref[...], shift_ref[...]
            ).astype(jnp.bfloat16)

        own_res[pl.ds(pl.multiple_of(k * CHUNK, CHUNK), CHUNK), :] = res[me]

        @pl.loop(0, hidden_units // 256)
        def _(i):
            part = pl.ds(pl.multiple_of(i * 256, 256), 256)
            lifted = (
                jnp.dot(nrm[...], upw[:, part], preferred_element_type=jnp.float32) + upb_ref[:, part]
            )
            exp_[:, part] = (0.5 * lifted * (1.0 + lax.erf(lifted * math.sqrt(0.5)))).astype(
                jnp.bfloat16
            )

        @pl.loop(0, width // 256)
        def _(i):
            part = pl.ds(pl.multiple_of(i * 256, 256), 256)
            par[k, :, :, :, part] = (
                jnp.dot(exp_[...], dnw[:, part], preferred_element_type=jnp.float32)
                .astype(jnp.bfloat16)
                .reshape(chips, 2, CHUNK, 256)
            )

        twin_copy(k).start()

    hidden_part(0).start()

    @pl.loop(0, chunks + 2 * chips - 1)
    def _(s):
        at_chunk(s, first_hop)
        for hop in range(1, chips):
            at_chunk(s - hop, functools.partial(later_hop, hop))
        at_chunk(s - chips, join_twins)
        for hop in range(1, chips):
            at_chunk(s - chips - hop, functools.partial(pass_on, hop))
        at_chunk(s - 2 * chips + 1, finish)
        at_chunk(s - chips + 1, compute)

    @pl.loop(0, chunks)
    def _(k):
        for origin in range(chips):
            slot = 2 * origin + c
            piece_copy(k, slot, twin, 2).wait_send()

            @pl.when((origin >= z) & (z > 0))
            def _():
                piece_copy(k, slot, twin, 0).wait_send()

            @pl.when((origin <= z) & (z < chips - 1))
            def _():
                piece_copy(k, slot, twin, 1).wait_send()

        twin_copy(k).wait_send()
        for at in range(chips):

            @pl.when(z == at)
            def _():
                if at < chips - 1:
                    right_copy(k, at).wait_send()
                if at > 0:
                    left_copy(k, at).wait_send()


def mlp_layer(
    attended, hall, out_weight, up_weight, down_weight, out_bias, gain, shift, up_bias, down_bias
):
    devices, tok_rows, width = hall.shape
    chips, chunks = devices // 2, tok_rows // CHUNK
    piece, units = attended.shape[1], up_weight.shape[1]
    total = devices * tok_rows
    hbm, vmem = pl.BlockSpec(memory_space=pl.ANY), pl.BlockSpec(memory_space=pltpu.VMEM)
    dma = pltpu.SemaphoreType.DMA
    bf16 = jnp.bfloat16
    return pl.pallas_call(
        functools.partial(mlp_kernel, chips),
        in_specs=[hbm] * 5 + [vmem] * 5,
        out_specs=vmem,
        out_shape=jax.ShapeDtypeStruct((tok_rows, width), bf16),
        scratch_shapes=[
            pltpu.VMEM((chunks, devices, CHUNK, width), bf16),
            pltpu.VMEM((width, width), bf16),
            pltpu.VMEM((width, units), bf16),
            pltpu.VMEM((units, width), bf16),
            pltpu.VMEM((2, devices, CHUNK, width), bf16),
            pltpu.VMEM((devices, CHUNK, width), bf16),
            pltpu.VMEM((devices * CHUNK, width), bf16),
            pltpu.VMEM((devices * CHUNK, units), bf16),
            pltpu.VMEM((tok_rows, width), bf16),
            pltpu.VMEM((chunks, chips, 2, CHUNK, width), bf16),
            pltpu.VMEM((chunks, chips, CHUNK, width), bf16),
            pltpu.VMEM((chunks, chips - 1, CHUNK, width), bf16),
            pltpu.VMEM((chunks, chips - 1, CHUNK, width), bf16),
            dma((3,)),
            dma((chunks,)),
            dma((2,)),
            dma((chunks, devices, 3)),
            dma((chunks, devices)),
            dma((chunks,)),
            dma((chunks,)),
            dma((chunks, 2)),
            dma((chunks, 2)),
        ],
        compiler_params=pltpu.CompilerParams(
            collective_id=1, has_side_effects=True, vmem_limit_bytes=60 << 20
        ),
        cost_estimate=pl.CostEstimate(
            flops=2 * total * width * (width + 2 * units),
            bytes_accessed=2 * (2 * total * width + width * (width + 2 * units)),
            transcendentals=total * units,
        ),
        name="mlp_layer",
    )(
        attended.reshape(devices, tok_rows, piece),
        hall,
        out_weight,
        up_weight,
        down_weight,
        out_bias.reshape(1, width),
        gain.reshape(1, width),
        shift.reshape(1, width),
        up_bias.reshape(1, units),
        down_bias.reshape(1, width),
    )


def page_kernel(src_ref, hall, w_ref, gain_ref, shift_ref, live_ref, out_ref, raw, nrm, sem):
    slots = raw.shape[0]

    @pl.when(pl.program_id(0) == 0)
    def _():
        copies = [
            pltpu.make_async_copy(hall.at[src_ref[i]], raw.at[i], sem.at[i]) for i in range(slots)
        ]
        for copy in copies:
            copy.start()
        for copy in copies:
            copy.wait()

        @pl.loop(0, slots // 2)
        def _(i):
            nrm[pl.ds(pl.multiple_of(i * 2 * PAGE, 2 * PAGE), 2 * PAGE), :] = layer_norm(
                raw[pl.ds(2 * i, 2)].reshape(2 * PAGE, -1), gain_ref[...], shift_ref[...]
            ).astype(jnp.bfloat16)

    parts, depth = w_ref.shape[0], nrm.shape[1] // w_ref.shape[0]
    half = nrm.shape[0] // 2
    bias = w_ref[0, depth : depth + 1, :].astype(jnp.float32)
    for j in range(2):
        rows = slice(j * half, (j + 1) * half)
        sums = sum(
            jnp.dot(
                nrm[rows, p * depth : (p + 1) * depth],
                w_ref[p, :depth, :],
                preferred_element_type=jnp.float32,
            )
            for p in range(parts)
        )
        made = jnp.where(live_ref[rows, :] > 0, sums + bias, 0.0).astype(jnp.bfloat16)
        out_ref[slice(j * slots // 2, (j + 1) * slots // 2)] = made.reshape(slots // 2, PAGE, -1)


def own_pages(hall, kv_weights, gain, shift, page_table, prompt_lengths, seq_len, position):
    devices, tok_rows, width = hall.shape
    pages = devices * tok_rows // PAGE
    capacity = 2 * pages // devices
    owners = page_table[:, 0]
    numbers = jnp.arange(pages, dtype=jnp.int32)
    earlier = (owners[None, :] == owners[:, None]) & (numbers[None, :] < numbers[:, None])
    ranks = jnp.sum(earlier.astype(jnp.int32), axis=1)
    slots = jnp.arange(capacity, dtype=jnp.int32)
    hits = (owners[None, :] == position) & (ranks[None, :] == slots[:, None])
    source = jnp.sum(jnp.where(hits, numbers[None, :], 0), axis=1)
    taken = jnp.sum(hits.astype(jnp.int32), axis=1) > 0
    tokens = source[:, None] * PAGE + jnp.arange(PAGE, dtype=jnp.int32)[None, :]
    stream = tokens // seq_len
    limits = jnp.sum(
        jnp.where(
            stream[:, :, None] == jnp.arange(prompt_lengths.shape[0], dtype=jnp.int32),
            prompt_lengths, 0,
        ),
        axis=2,
    )
    live = (taken[:, None] & (tokens - stream * seq_len < limits)).astype(jnp.int32)
    shards, parts, depth, cols = kv_weights.shape
    total = capacity * PAGE
    return pl.pallas_call(
        page_kernel,
        grid_spec=pltpu.PrefetchScalarGridSpec(
            num_scalar_prefetch=1,
            grid=(shards,),
            in_specs=[
                pl.BlockSpec(memory_space=pl.ANY),
                pl.BlockSpec((None, parts, depth, cols), lambda t, src: (t, 0, 0, 0)),
                pl.BlockSpec((1, width), lambda t, src: (0, 0)),
                pl.BlockSpec((1, width), lambda t, src: (0, 0)),
                pl.BlockSpec((total, 1), lambda t, src: (0, 0)),
            ],
            out_specs=pl.BlockSpec((capacity, PAGE, cols), lambda t, src: (0, 0, t)),
            scratch_shapes=[
                pltpu.VMEM((capacity, PAGE, width), jnp.bfloat16),
                pltpu.VMEM((total, width), jnp.bfloat16),
                pltpu.SemaphoreType.DMA((capacity,)),
            ],
        ),
        out_shape=jax.ShapeDtypeStruct((capacity, PAGE, shards * cols), jnp.bfloat16),
        compiler_params=pltpu.CompilerParams(vmem_limit_bytes=32 << 20),
        cost_estimate=pl.CostEstimate(
            flops=2 * total * width * shards * cols,
            bytes_accessed=2 * (total * (width + shards * cols) + width * shards * cols),
            transcendentals=0,
        ),
        name="own_pages",
    )(
        source,
        hall.reshape(pages, PAGE, width),
        kv_weights,
        gain.reshape(1, width),
        shift.reshape(1, width),
        live.reshape(total, 1),
    )


def on_line(
    hidden_in, attn_gain, attn_shift, qkv_weight, qkv_bias, out_weight, out_bias, mlp_gain,
    mlp_shift, up_weight, up_bias, down_weight, down_bias, segment_ids, prompt_lengths, page_table,
):
    devices = lax.axis_size("tensor")
    columns = lax.axis_size("dp")
    position, column = lax.axis_index("tensor"), lax.axis_index("dp")
    width = hidden_in.shape[1]
    heads = qkv_weight.shape[1] // (3 * HD)

    out_rows = out_weight.shape[0] // columns
    out_share = lax.dynamic_slice_in_dim(out_weight, column * out_rows, out_rows, 0)
    out_whole = lax.all_gather(out_share, ("tensor", "dp"), axis=0, tiled=True)
    kv_rows = width // columns
    share = lax.dynamic_slice_in_dim(qkv_weight, column * kv_rows, kv_rows, 0)
    share = jnp.concatenate(
        [share, jnp.broadcast_to(qkv_bias[None, :], (PAGE, qkv_bias.shape[0]))], axis=0
    )
    share = jnp.concatenate(
        [share[:, (3 * n + 1) * HD : (3 * n + 3) * HD] for n in range(heads)], axis=1
    )
    kv_whole = lax.all_gather(share, ("tensor", "dp"), axis=0, tiled=True)
    kv_whole = kv_whole.reshape(devices, columns, kv_rows + PAGE, heads * 2 * HD)

    hall, projected = gather_project(
        hidden_in, qkv_weight, qkv_bias, attn_gain, attn_shift, devices
    )
    attended = attend(projected.reshape(-1, projected.shape[2]), segment_ids)
    layer_out = mlp_layer(
        attended, hall, out_whole, up_weight, down_weight, out_bias, mlp_gain, mlp_shift, up_bias,
        down_bias,
    )
    kv_pages = own_pages(
        hall, kv_whole, attn_gain, attn_shift, page_table, prompt_lengths, segment_ids.shape[1],
        position,
    )
    return (layer_out, kv_pages)


def on_device(
    hidden_in,
    attn_gain,
    attn_shift,
    qkv_weight,
    qkv_bias,
    out_weight,
    out_bias,
    mlp_gain,
    mlp_shift,
    up_weight,
    up_bias,
    down_weight,
    down_bias,
    segment_ids,
    prompt_lengths,
    page_table,
):
    devices = lax.axis_size("tensor")
    position = lax.axis_index("tensor")
    tok_rows, width = hidden_in.shape
    total_rows = tok_rows * devices
    streams, seq_len = segment_ids.shape
    whole_heads = qkv_weight.shape[1] % (3 * HD) == 0

    normed = normalize(hidden_in, attn_gain, attn_shift).astype(jnp.bfloat16)
    if not whole_heads:
        qkv_weight = join_pair(qkv_weight, 1, position)
        qkv_bias = join_pair(qkv_bias, 0, position)
    gathered = lax.all_gather(normed, "tensor", axis=0, tiled=True)
    projected = (
        jnp.dot(gathered, qkv_weight, preferred_element_type=jnp.float32)
        + qkv_bias.astype(jnp.float32)
    ).astype(jnp.bfloat16)
    heads_here = projected.shape[1] // (3 * HD)
    keys_vals = jnp.concatenate(
        [
            lax.slice_in_dim(projected, (3 * n + 1) * HD, (3 * n + 3) * HD, axis=1)
            for n in range(heads_here)
        ],
        axis=1,
    )
    if not whole_heads:
        half = keys_vals.shape[1] // 2
        keys_vals = lax.dynamic_slice_in_dim(keys_vals, position % 2 * half, half, 1)
    live = jnp.arange(seq_len, dtype=jnp.int32)[None, :] < prompt_lengths[:, None]
    pieces = pack_pages(
        keys_vals, live, page_table, 2 * (total_rows // PAGE) // devices, position
    )
    projected, pieces = lax.optimization_barrier((projected, pieces))
    received = send_pages(pieces)
    far, step = devices // 2, devices // 8
    attended = attend(projected, segment_ids)
    if not whole_heads:
        half = attended.shape[1] // 2
        attended = lax.dynamic_slice_in_dim(attended, position % 2 * half, half, 1)
    attended, received[far : far + step] = lax.optimization_barrier(
        (attended, received[far : far + step])
    )

    part = tok_rows // CHUNKS
    shaped = attended.reshape(devices, CHUNKS, part, attended.shape[1])
    sums = []
    for chunk in range(CHUNKS):
        rows = shaped[:, chunk].reshape(devices * part, -1)
        terms = jnp.dot(rows, out_weight, preferred_element_type=jnp.float32)
        sums.append(
            lax.psum_scatter(
                terms.astype(jnp.bfloat16), "tensor", scatter_dimension=0, tiled=True
            )
        )
    residuals, gathers = [], []
    for chunk in range(CHUNKS):
        hidden = lax.slice_in_dim(hidden_in, chunk * part, (chunk + 1) * part, axis=0)
        attn_sum = sums[chunk]
        if chunk == 0:
            attn_sum, received[far + step : far + 3 * step] = lax.optimization_barrier(
                (attn_sum, received[far + step : far + 3 * step])
            )
        else:
            attn_sum, residuals[-1], received, _ = lax.optimization_barrier(
                (attn_sum, residuals[-1], received, normed_mid)
            )
        residual_mid = (
            hidden.astype(jnp.float32) + attn_sum.astype(jnp.float32) + out_bias
        ).astype(jnp.bfloat16)
        normed_mid = normalize(residual_mid, mlp_gain, mlp_shift).astype(jnp.bfloat16)
        residuals.append(residual_mid)
        gathers.append(lax.all_gather(normed_mid, "tensor", axis=0, tiled=True))
    sums = []
    for chunk in range(CHUNKS):
        lifted = jnp.dot(gathers[chunk], up_weight, preferred_element_type=jnp.float32) + up_bias
        expanded = jax.nn.gelu(lifted, approximate=False).astype(jnp.bfloat16)
        expanded = lax.optimization_barrier(expanded)
        terms = jnp.dot(expanded, down_weight, preferred_element_type=jnp.float32)
        sums.append(
            lax.psum_scatter(
                terms.astype(jnp.bfloat16), "tensor", scatter_dimension=0, tiled=True
            )
        )
    kv_pages = lay_out_pages(received, position)
    outs = [
        (residual_mid.astype(jnp.float32) + mlp_sum.astype(jnp.float32) + down_bias).astype(
            jnp.bfloat16
        )
        for residual_mid, mlp_sum in zip(residuals, sums)
    ]
    layer_out = outs[0] if CHUNKS == 1 else jnp.concatenate(outs, axis=0)
    return (layer_out, kv_pages)


def solution(mesh):
    in_specs = (
        P(("dp", "tensor"), None),
        P(),
        P(),
        P(None, "tensor"),
        P("tensor"),
        P("tensor", None),
        P(),
        P(),
        P(),
        P(None, "tensor"),
        P("tensor"),
        P("tensor", None),
        P(),
        P("dp", None),
        P("dp"),
        P("dp", None),
    )
    out_specs = (P(("dp", "tensor"), None), P(("dp", "tensor"), None, None))
    body = on_line if mesh.shape["tensor"] == LINE else on_device
    return jax.shard_map(
        body, mesh=mesh, in_specs=in_specs, out_specs=out_specs, check_vma=False
    )
```

```python
import functools
import math

import jax
import jax.numpy as jnp
from jax import lax
from jax.experimental import pallas as pl
from jax.experimental.pallas import tpu as pltpu
from jax.sharding import PartitionSpec as P

HD = 128
PAGE = 16
MAX_DOC = 1024
Q_BLOCK = 256
CHUNKS = 2


def normalize(values, norm_gain, norm_shift):
    widened = values.astype(jnp.float32)
    center = jnp.mean(widened, axis=-1, keepdims=True)
    spread = jnp.mean(jnp.square(widened - center), axis=-1, keepdims=True)
    return (widened - center) * lax.rsqrt(spread + 1e-05) * norm_gain + norm_shift


def attend_kernel(most, count_ref, q_ref, k_ref, v_ref, qseg_ref, kseg_ref, out_ref):
    stream, block = pl.program_id(0), pl.program_id(2)
    rows = q_ref.shape[0]
    count = count_ref[stream * pl.num_programs(2) + block]

    def over(blocks):
        window = blocks * rows
        start = pl.multiple_of((block - blocks + 1) * rows, rows)
        keys = k_ref[pl.ds(start, window), :]
        values = v_ref[pl.ds(start, window), :]
        scores = lax.dot_general(
            q_ref[...], keys, (((1,), (1,)), ((), ())), preferred_element_type=jnp.float32
        ) * (1.0 / math.sqrt(HD))
        ahead = lax.broadcasted_iota(jnp.int32, (rows, window), 1) - lax.broadcasted_iota(
            jnp.int32, (rows, window), 0
        )
        allowed = (ahead <= window - rows) & (
            qseg_ref[...] == kseg_ref[0, :, pl.ds(start, window)]
        )
        scores = jnp.where(allowed, scores, -1e30)
        expo = jnp.exp(scores - jnp.max(scores, axis=1, keepdims=True))
        weights = (expo * (1.0 / jnp.sum(expo, axis=1, keepdims=True))).astype(jnp.bfloat16)
        out_ref[...] = jnp.dot(weights, values, preferred_element_type=jnp.float32).astype(
            jnp.bfloat16
        )

    for blocks in range(1, most + 1):
        pl.when(count == blocks)(functools.partial(over, blocks))


def attend(projected, segment_ids):
    streams, seq_len = segment_ids.shape
    heads = projected.shape[1] // (3 * HD)
    blocks = seq_len // Q_BLOCK
    most = min(blocks, MAX_DOC // Q_BLOCK + 1)
    pairs = streams * heads * seq_len * 2 * Q_BLOCK
    firsts = segment_ids[:, ::Q_BLOCK]
    begins = jnp.sum((segment_ids[:, None, :] < firsts[:, :, None]).astype(jnp.int32), axis=2)
    counts = jnp.arange(blocks, dtype=jnp.int32)[None, :] - begins // Q_BLOCK + 1
    counts = jnp.clip(counts, 1, most).reshape(-1)
    return pl.pallas_call(
        functools.partial(attend_kernel, most),
        grid_spec=pltpu.PrefetchScalarGridSpec(
            num_scalar_prefetch=1,
            grid=(streams, heads, blocks),
            in_specs=[
                pl.BlockSpec((Q_BLOCK, HD), lambda s, n, i, counts: (s * blocks + i, 3 * n)),
                pl.BlockSpec((seq_len, HD), lambda s, n, i, counts: (s, 3 * n + 1)),
                pl.BlockSpec((seq_len, HD), lambda s, n, i, counts: (s, 3 * n + 2)),
                pl.BlockSpec((Q_BLOCK, 1), lambda s, n, i, counts: (s * blocks + i, 0)),
                pl.BlockSpec((1, 1, seq_len), lambda s, n, i, counts: (s, 0, 0)),
            ],
            out_specs=pl.BlockSpec((Q_BLOCK, HD), lambda s, n, i, counts: (s * blocks + i, n)),
        ),
        out_shape=jax.ShapeDtypeStruct((streams * seq_len, heads * HD), jnp.bfloat16),
        compiler_params=pltpu.CompilerParams(vmem_limit_bytes=60 << 20),
        cost_estimate=pl.CostEstimate(
            flops=4 * pairs * HD,
            bytes_accessed=2 * projected.size * 2,
            transcendentals=pairs,
        ),
        name="attend",
    )(
        counts,
        projected,
        projected,
        projected,
        segment_ids.reshape(streams * seq_len, 1),
        segment_ids.reshape(streams, 1, seq_len),
    )


def join_pair(value, axis, position):
    devices = lax.axis_size("tensor")
    other = lax.ppermute(value, "tensor", [(source, source ^ 1) for source in range(devices)])
    first = jnp.where(position % 2 == 0, value, other)
    second = jnp.where(position % 2 == 0, other, value)
    return jnp.concatenate([first, second], axis=axis)


def copy_page(index_ref, page_ref, out_ref):
    out_ref[...] = page_ref[...]


def take_pages(page_rows, index):
    block = (1,) + page_rows.shape[1:]
    return pl.pallas_call(
        copy_page,
        grid_spec=pltpu.PrefetchScalarGridSpec(
            num_scalar_prefetch=1,
            grid=(index.shape[0],),
            in_specs=[pl.BlockSpec(block, lambda i, index: (index[i], 0, 0))],
            out_specs=pl.BlockSpec(block, lambda i, index: (i, 0, 0)),
        ),
        out_shape=jax.ShapeDtypeStruct(index.shape + page_rows.shape[1:], page_rows.dtype),
    )(index, page_rows)


def pack_pages(keys_vals, live, page_table, capacity, position):
    devices = lax.axis_size("tensor")
    pages = keys_vals.shape[0] // PAGE
    owners = page_table[:, 0]
    numbers = jnp.arange(pages, dtype=jnp.int32)
    earlier = (owners[None, :] == owners[:, None]) & (numbers[None, :] < numbers[:, None])
    ranks = jnp.sum(earlier.astype(jnp.int32), axis=1)
    slot_ids = owners * capacity + ranks
    owner_order = position ^ jnp.arange(devices, dtype=jnp.int32)
    slots = owner_order[:, None] * capacity + jnp.arange(capacity, dtype=jnp.int32)[None, :]
    hits = slot_ids[None, :] == slots.reshape(-1)[:, None]
    source_page = jnp.sum(jnp.where(hits, numbers[None, :], 0), axis=1)
    live_pages = live.reshape(pages, PAGE).astype(jnp.int32)
    kept = jnp.sum(jnp.where(hits[:, :, None], live_pages[None], 0), axis=1) > 0
    page_rows = keys_vals.reshape(pages, PAGE, -1)
    taken = take_pages(page_rows, source_page)
    outgoing = jnp.where(kept[:, :, None], taken, 0).astype(jnp.bfloat16)
    return [
        lax.slice_in_dim(outgoing, apart * capacity, (apart + 1) * capacity, axis=0)
        for apart in range(devices)
    ]


def send_pages(pieces):
    devices = len(pieces)
    received = [pieces[0]]
    for apart in range(1, devices):
        hops = [(source, source ^ apart) for source in range(devices)]
        received.append(lax.ppermute(pieces[apart], "tensor", hops))
    return received


def lay_out_pages(received, position):
    devices = len(received)
    slots, page, width = received[0].shape
    laid = jnp.zeros((slots, page, devices * width), received[0].dtype)
    for apart in range(devices):
        laid = lax.dynamic_update_slice_in_dim(
            laid, received[apart], (position ^ apart) * width, axis=2
        )
    return laid


MESH = pl.DeviceIdType.MESH
SQUARE_LINE = (4, 8)
CHUNK = 32


def layer_norm(values, gain, shift):
    widened = values.astype(jnp.float32)
    center = jnp.mean(widened, axis=-1, keepdims=True)
    moved = widened - center
    spread = jnp.mean(moved * moved, axis=-1, keepdims=True)
    return moved * lax.rsqrt(spread + 1e-05) * gain + shift


def norm_rows(load, out, rows, gain_ref, shift_ref):
    @pl.loop(0, rows // 16, unroll=4)
    def _(i):
        part = pl.ds(pl.multiple_of(i * 16, 16), 16)
        out[part, :] = layer_norm(load(part), gain_ref[...], shift_ref[...]).astype(jnp.bfloat16)


def greet(me, chips, across=()):
    z, c = me // 2, lax.rem(me, 2)
    barrier = pltpu.get_barrier_semaphore()
    pl.semaphore_signal(barrier, inc=1, device_id={"tensor": 2 * z + 1 - c}, device_id_type=MESH)
    for column in across:
        pl.semaphore_signal(barrier, inc=1, device_id={"dp": column}, device_id_type=MESH)

    @pl.when(z > 0)
    def _():
        pl.semaphore_signal(barrier, inc=1, device_id={"tensor": me - 2}, device_id_type=MESH)

    @pl.when(z < chips - 1)
    def _():
        pl.semaphore_signal(barrier, inc=1, device_id={"tensor": me + 2}, device_id_type=MESH)

    peers = 1 + len(across) + (z > 0).astype(jnp.int32) + (z < chips - 1).astype(jnp.int32)
    pl.semaphore_wait(barrier, peers)


def gather_project_kernel(
    chips, hid, w_hbm, oshare, kshare, b_ref, gain_ref, shift_ref, hall_out, proj_out, oall, kall,
    buf, w_ref, nrm, pbuf, ssem, rsem, lsem, psem, wsem, share_s, share_r,
):
    me, p = lax.axis_index("tensor"), lax.axis_index("dp")
    z, c = me // 2, lax.rem(me, 2)
    twin = 2 * z + 1 - c
    beside, over, corner = p + 1 - 2 * lax.rem(p, 2), lax.rem(p + 2, 4), 3 - p
    rows, width = hid.shape
    cols = w_ref.shape[1]
    pair, own_share = (oall, kall), (oshare, kshare)
    load = pltpu.make_async_copy(w_hbm, w_ref, wsem.at[0])
    own = pltpu.make_async_copy(hid, buf.at[me], wsem.at[1])
    own_shares = [
        pltpu.make_async_copy(oshare, oall.at[p, me], wsem.at[2]),
        pltpu.make_async_copy(kshare, kall.at[p, me], wsem.at[3]),
    ]
    for copy in own_shares:
        copy.start()
    own.start()
    load.start()
    greet(me, chips, (beside, over))

    def share_copy(a, q, slot, way, own_from=False):
        device = [
            {"tensor": me - 2}, {"tensor": me + 2}, {"tensor": twin}, {"dp": beside}, {"dp": over},
        ][way]
        source = own_share[a] if own_from else pair[a].at[q, slot]
        return pltpu.make_async_remote_copy(
            src_ref=source, dst_ref=pair[a].at[q, slot],
            send_sem=share_s.at[a, q, slot, way], recv_sem=share_r.at[a, q, slot],
            device_id=device, device_id_type=MESH,
        )

    def share_send(q, slot, *ways):
        for a in range(2):
            for way in ways:
                share_copy(a, q, slot, way).start()

    def own_share_send(*ways):
        for a in range(2):
            for way in ways:
                share_copy(a, p, me, way, True).start()

    def share_arrived(q, slot):
        for a in range(2):
            share_copy(a, q, slot, 2).wait_recv()

    def share_line(hop):
        @pl.when(z - hop >= 0)
        def _():
            slot = me - 2 * hop
            share_arrived(p, slot)

            @pl.when(z < chips - 1)
            def _():
                share_send(p, slot, 1)

            share_send(p, slot, 3, 4, 2)

        @pl.when(z + hop < chips)
        def _():
            slot = me + 2 * hop
            share_arrived(p, slot)

            @pl.when(z > 0)
            def _():
                share_send(p, slot, 0)

            share_send(p, slot, 3, 4, 2)

    def at_slots(hop, run):
        if hop == 0:
            run(me)
        else:
            pl.when(z - hop >= 0)(lambda: run(me - 2 * hop))
            pl.when(z + hop < chips)(lambda: run(me + 2 * hop))

    def share_across(slot):
        share_arrived(over, slot)
        pl.when(c == 0)(lambda: share_send(over, slot, 3))
        share_arrived(beside, slot)
        pl.when(c == 1)(lambda: share_send(beside, slot, 4))
        share_send(over, slot, 2)
        share_send(beside, slot, 2)

    def share_corner(slot):
        share_arrived(corner, slot)
        share_send(corner, slot, 2)

    def send(slot, device, way):
        pltpu.make_async_remote_copy(
            src_ref=buf.at[slot], dst_ref=buf.at[slot], send_sem=ssem.at[slot, way],
            recv_sem=rsem.at[slot], device_id={"tensor": device}, device_id_type=MESH,
        ).start()

    def sent(slot, way):
        pltpu.make_async_remote_copy(
            src_ref=buf.at[slot], dst_ref=buf.at[slot], send_sem=ssem.at[slot, way],
            recv_sem=rsem.at[slot], device_id={"tensor": twin}, device_id_type=MESH,
        ).wait_send()

    def arrived(slot):
        pltpu.make_async_copy(hid, buf.at[slot], rsem.at[slot]).wait()

    def compute(slot):
        pltpu.make_async_copy(buf.at[slot], hall_out.at[slot], lsem.at[slot]).start()

        norm_rows(lambda part: buf[slot, part, :], nrm, rows, gain_ref, shift_ref)

        @pl.loop(0, cols // 256)
        def _(i):
            part = pl.ds(pl.multiple_of(i * 256, 256), 256)
            pbuf[slot, :, part] = (
                jnp.dot(nrm[...], w_ref[:, part], preferred_element_type=jnp.float32)
                + b_ref[:, part].astype(jnp.float32)
            ).astype(jnp.bfloat16)

        pltpu.make_async_copy(pbuf.at[slot], proj_out.at[slot], psem.at[slot]).start()

    def token_line(hop):
        @pl.when(z - hop >= 0)
        def _():
            slot = me - 2 * hop
            arrived(slot)

            @pl.when(z < chips - 1)
            def _():
                send(slot, me + 2, 1)

            send(slot, twin, 2)

        @pl.when(z + hop < chips)
        def _():
            slot = me + 2 * hop
            arrived(slot)

            @pl.when(z > 0)
            def _():
                send(slot, me - 2, 0)

            send(slot, twin, 2)

    def token_compute(hop):
        @pl.when(z - hop >= 0)
        def _():
            compute(me - 2 * hop)
            arrived(twin - 2 * hop)
            compute(twin - 2 * hop)

        @pl.when(z + hop < chips)
        def _():
            compute(me + 2 * hop)
            arrived(twin + 2 * hop)
            compute(twin + 2 * hop)

    pl.when(z > 0)(lambda: own_share_send(0))
    pl.when(z < chips - 1)(lambda: own_share_send(1))
    own_share_send(3, 4, 2)
    own.wait()
    load.wait()
    compute(me)
    for hop in range(1, chips - 1):
        share_line(hop)
        if hop == 1:
            at_slots(0, share_across)
    pl.when(z > 0)(lambda: send(me, me - 2, 0))
    pl.when(z < chips - 1)(lambda: send(me, me + 2, 1))
    send(me, twin, 2)
    share_line(chips - 1)
    arrived(twin)
    compute(twin)
    for hop in range(1, chips):
        at_slots(hop, share_across)
        at_slots(hop - 1, share_corner)
        token_line(hop)
        token_compute(hop)
    at_slots(chips - 1, share_corner)

    for copy in own_shares:
        copy.wait()
    for slot in range(2 * chips):
        pltpu.make_async_copy(buf.at[slot], hall_out.at[slot], lsem.at[slot]).wait()
        pltpu.make_async_copy(pbuf.at[slot], proj_out.at[slot], psem.at[slot]).wait()
    for origin in range(chips):
        slot = 2 * origin + c
        sent(slot, 2)
        for q in (beside, over, corner):
            share_arrived(q, 2 * origin + 1 - c)

        share_arrived(p, 2 * origin + 1 - c)

        @pl.when((origin >= z) & (z > 0))
        def _():
            sent(slot, 0)
            for a in range(2):
                share_copy(a, p, slot, 0).wait_send()

        @pl.when((origin <= z) & (z < chips - 1))
        def _():
            sent(slot, 1)
            for a in range(2):
                share_copy(a, p, slot, 1).wait_send()

        for a in range(2):
            for q in (p, beside, over, corner):
                share_copy(a, q, slot, 2).wait_send()
            share_copy(a, p, slot, 3).wait_send()
            share_copy(a, p, slot, 4).wait_send()

            @pl.when(c == 0)
            def _():
                share_copy(a, over, slot, 3).wait_send()

            @pl.when(c == 1)
            def _():
                share_copy(a, beside, slot, 4).wait_send()


def gather_project(
    hidden_in, qkv_weight, out_share, kv_share, qkv_bias, gain, shift, devices, columns
):
    rows, width = hidden_in.shape
    cols = qkv_weight.shape[1]
    hbm, vmem = pl.BlockSpec(memory_space=pl.ANY), pl.BlockSpec(memory_space=pltpu.VMEM)
    total = rows * devices
    dma = pltpu.SemaphoreType.DMA
    return pl.pallas_call(
        functools.partial(gather_project_kernel, devices // 2),
        in_specs=[hbm] * 4 + [vmem] * 3,
        out_specs=[hbm] * 4,
        out_shape=[
            jax.ShapeDtypeStruct((devices, rows, width), jnp.bfloat16),
            jax.ShapeDtypeStruct((devices, rows, cols), jnp.bfloat16),
            jax.ShapeDtypeStruct((columns, devices) + out_share.shape, jnp.bfloat16),
            jax.ShapeDtypeStruct((columns, devices) + kv_share.shape, jnp.bfloat16),
        ],
        scratch_shapes=[
            pltpu.VMEM((devices, rows, width), jnp.bfloat16),
            pltpu.VMEM((width, cols), jnp.bfloat16),
            pltpu.VMEM((rows, width), jnp.bfloat16),
            pltpu.VMEM((devices, rows, cols), jnp.bfloat16),
            dma((devices, 3)),
            dma((devices,)),
            dma((devices,)),
            dma((devices,)),
            dma((4,)),
            dma((2, columns, devices, 5)),
            dma((2, columns, devices)),
        ],
        compiler_params=pltpu.CompilerParams(
            collective_id=0, has_side_effects=True, vmem_limit_bytes=60 << 20
        ),
        cost_estimate=pl.CostEstimate(
            flops=2 * total * width * cols,
            bytes_accessed=2 * (total * (width + cols) + width * cols),
            transcendentals=0,
        ),
        name="gather_project",
    )(
        hidden_in, qkv_weight, out_share, kv_share, qkv_bias.reshape(1, cols),
        gain.reshape(1, width), shift.reshape(1, width),
    )


def mlp_kernel(
    chips, att, hall, outw_hbm, upw_hbm, dnw_hbm, outb_ref, gain_ref, shift_ref, upb_ref, dnb_ref,
    out_ref,
    ag, outw, upw, dnw, hbuf, res, nrm, exp_, own_res, par, tw, lin, rin,
    wsem, osem, hsem, ag_s, ag_r, tw_s, tw_r, rs_s, rs_r,
):
    me = lax.axis_index("tensor")
    z, c = me // 2, lax.rem(me, 2)
    twin = 2 * z + 1 - c
    devices = 2 * chips
    chunks = ag.shape[0]
    width = outw.shape[1]
    piece = att.shape[-1]
    hidden_units = upw.shape[1]
    rows = devices * CHUNK

    columns, _, out_rows, _ = outw_hbm.shape
    loads = [
        pltpu.make_async_copy(
            outw_hbm.at[p, d], outw.at[pl.ds((d * columns + p) * out_rows, out_rows)], wsem.at[2 + d * columns + p]
        )
        for d in range(devices)
        for p in range(columns)
    ] + [
        pltpu.make_async_copy(upw_hbm, upw, wsem.at[0]),
        pltpu.make_async_copy(dnw_hbm, dnw, wsem.at[1]),
    ]

    def place(k, device):
        return ag.at[k, :, :, pl.ds(pl.multiple_of(device * piece, piece), piece)]

    def own_piece(k):
        part = pl.ds(pl.multiple_of(k * CHUNK, CHUNK), CHUNK)
        return pltpu.make_async_copy(att.at[:, part, :], place(k, me), osem.at[k])

    def hidden_part(k):
        part = pl.ds(pl.multiple_of(k * CHUNK, CHUNK), CHUNK)
        return pltpu.make_async_copy(hall.at[:, part, :], hbuf.at[lax.rem(k, 2)], hsem.at[lax.rem(k, 2)])

    @pl.loop(0, chunks)
    def _(k):
        own_piece(k).start()

    for load in loads:
        load.start()
    greet(me, chips)

    def piece_copy(k, origin, device, way):
        return pltpu.make_async_remote_copy(
            src_ref=place(k, origin), dst_ref=place(k, origin), send_sem=ag_s.at[k, origin, way],
            recv_sem=ag_r.at[k, origin], device_id={"tensor": device}, device_id_type=MESH,
        )

    def piece_wait(k, origin):
        piece_copy(k, origin, twin, 2).wait_recv()

    def twin_copy(k):
        return pltpu.make_async_remote_copy(
            src_ref=par.at[k, :, 1 - c], dst_ref=tw.at[k], send_sem=tw_s.at[k], recv_sem=tw_r.at[k],
            device_id={"tensor": twin}, device_id_type=MESH,
        )

    def right_copy(k, at):
        count = chips - 1 - at
        return pltpu.make_async_remote_copy(
            src_ref=par.at[k, pl.ds(at + 1, count), c], dst_ref=lin.at[k, pl.ds(chips - 1 - count, count)],
            send_sem=rs_s.at[k, 0], recv_sem=rs_r.at[k, 0],
            device_id={"tensor": me + 2}, device_id_type=MESH,
        )

    def left_copy(k, at):
        return pltpu.make_async_remote_copy(
            src_ref=par.at[k, pl.ds(0, at), c], dst_ref=rin.at[k, pl.ds(0, at)],
            send_sem=rs_s.at[k, 1], recv_sem=rs_r.at[k, 1],
            device_id={"tensor": me - 2}, device_id_type=MESH,
        )

    def lin_at(k, chip):
        return lin[k, chip - 1].astype(jnp.float32)

    def rin_at(k, chip):
        return rin[k, chip].astype(jnp.float32)

    def at_chunk(k, run):
        pl.when((k >= 0) & (k < chunks))(lambda: run(k))

    def first_hop(k):
        own_piece(k).wait()

        @pl.when(z > 0)
        def _():
            piece_copy(k, me, me - 2, 0).start()

        @pl.when(z < chips - 1)
        def _():
            piece_copy(k, me, me + 2, 1).start()

        piece_copy(k, me, twin, 2).start()

    def later_hop(hop, k):
        @pl.when(z - hop >= 0)
        def _():
            origin = me - 2 * hop
            piece_wait(k, origin)

            @pl.when(z < chips - 1)
            def _():
                piece_copy(k, origin, me + 2, 1).start()

            piece_copy(k, origin, twin, 2).start()

        @pl.when(z + hop < chips)
        def _():
            origin = me + 2 * hop
            piece_wait(k, origin)

            @pl.when(z > 0)
            def _():
                piece_copy(k, origin, me - 2, 0).start()

            piece_copy(k, origin, twin, 2).start()

    def join_twins(k):
        twin_copy(k).wait_recv()
        for chip in range(chips):
            par[k, chip, c] = (
                par[k, chip, c].astype(jnp.float32) + tw[k, chip].astype(jnp.float32)
            ).astype(jnp.bfloat16)

        @pl.when(z == 0)
        def _():
            right_copy(k, 0).start()

        @pl.when(z == chips - 1)
        def _():
            left_copy(k, chips - 1).start()

    def add_left(k, at):
        right_copy(k, at - 1).wait_recv()
        for chip in range(at, chips):
            par[k, chip, c] = (par[k, chip, c].astype(jnp.float32) + lin_at(k, chip)).astype(jnp.bfloat16)
        if at < chips - 1:
            right_copy(k, at).start()

    def add_right(k, at):
        left_copy(k, at + 1).wait_recv()
        for chip in range(0, at + 1):
            par[k, chip, c] = (par[k, chip, c].astype(jnp.float32) + rin_at(k, chip)).astype(jnp.bfloat16)
        if at > 0:
            left_copy(k, at).start()

    def pass_on(hop, k):
        for at in range(1, chips):
            if at == hop:

                @pl.when(z == at)
                def _():
                    add_left(k, at)

                @pl.when(z == chips - 1 - at)
                def _():
                    add_right(k, chips - 1 - at)

    def finish(k):
        part = pl.ds(pl.multiple_of(k * CHUNK, CHUNK), CHUNK)
        out_ref[part, :] = (
            own_res[part, :].astype(jnp.float32) + par[k, z, c].astype(jnp.float32) + dnb_ref[...]
        ).astype(jnp.bfloat16)

    def compute(k):
        for hop in range(1, chips):

            @pl.when(z - hop >= 0)
            def _():
                piece_wait(k, twin - 2 * hop)

            @pl.when(z + hop < chips)
            def _():
                piece_wait(k, twin + 2 * hop)

        piece_wait(k, twin)
        hidden_part(k).wait()
        slot = lax.rem(k, 2)

        @pl.when(k + 1 < chunks)
        def _():
            hidden_part(k + 1).start()

        @pl.when(k == 0)
        def _():
            for load in loads:
                load.wait()

        @pl.loop(0, width // 256)
        def _(i):
            part = pl.ds(pl.multiple_of(i * 256, 256), 256)
            terms = jnp.dot(
                ag[k].reshape(rows, width), outw[:, part], preferred_element_type=jnp.float32
            )
            res[:, part] = (
                hbuf[slot, :, :, part].reshape(rows, 256).astype(jnp.float32)
                + terms
                + outb_ref[:, part]
            ).astype(jnp.bfloat16)

        norm_rows(lambda part: res[part, :], nrm, rows, gain_ref, shift_ref)
        own_res[pl.ds(pl.multiple_of(k * CHUNK, CHUNK), CHUNK), :] = res[
            pl.ds(pl.multiple_of(me * CHUNK, CHUNK), CHUNK), :
        ]

        for i in range(hidden_units // 256):
            part = slice(i * 256, (i + 1) * 256)
            lifted = (
                jnp.dot(nrm[...], upw[:, part], preferred_element_type=jnp.float32) + upb_ref[:, part]
            )
            exp_[:, part] = (0.5 * lifted * (1.0 + lax.erf(lifted * math.sqrt(0.5)))).astype(
                jnp.bfloat16
            )

        @pl.loop(0, width // 256)
        def _(i):
            part = pl.ds(pl.multiple_of(i * 256, 256), 256)
            par[k, :, :, :, part] = (
                jnp.dot(exp_[...], dnw[:, part], preferred_element_type=jnp.float32)
                .astype(jnp.bfloat16)
                .reshape(chips, 2, CHUNK, 256)
            )

        twin_copy(k).start()

    hidden_part(0).start()

    @pl.loop(0, chunks + 2 * chips - 1)
    def _(s):
        at_chunk(s, first_hop)
        for hop in range(1, chips):
            at_chunk(s - hop, functools.partial(later_hop, hop))
        at_chunk(s - chips, join_twins)
        for hop in range(1, chips):
            at_chunk(s - chips - hop, functools.partial(pass_on, hop))
        at_chunk(s - 2 * chips + 1, finish)
        at_chunk(s - chips + 1, compute)

    @pl.loop(0, chunks)
    def _(k):
        for origin in range(chips):
            slot = 2 * origin + c
            piece_copy(k, slot, twin, 2).wait_send()

            @pl.when((origin >= z) & (z > 0))
            def _():
                piece_copy(k, slot, twin, 0).wait_send()

            @pl.when((origin <= z) & (z < chips - 1))
            def _():
                piece_copy(k, slot, twin, 1).wait_send()

        twin_copy(k).wait_send()
        for at in range(chips):

            @pl.when(z == at)
            def _():
                if at < chips - 1:
                    right_copy(k, at).wait_send()
                if at > 0:
                    left_copy(k, at).wait_send()


def mlp_layer(
    attended, hall, out_weight, up_weight, down_weight, out_bias, gain, shift, up_bias, down_bias
):
    devices, tok_rows, width = hall.shape
    chips, chunks = devices // 2, tok_rows // CHUNK
    piece, units = attended.shape[1], up_weight.shape[1]
    total = devices * tok_rows
    hbm, vmem = pl.BlockSpec(memory_space=pl.ANY), pl.BlockSpec(memory_space=pltpu.VMEM)
    dma = pltpu.SemaphoreType.DMA
    bf16 = jnp.bfloat16
    return pl.pallas_call(
        functools.partial(mlp_kernel, chips),
        in_specs=[hbm] * 5 + [vmem] * 5,
        out_specs=vmem,
        out_shape=jax.ShapeDtypeStruct((tok_rows, width), bf16),
        scratch_shapes=[
            pltpu.VMEM((chunks, devices, CHUNK, width), bf16),
            pltpu.VMEM((width, width), bf16),
            pltpu.VMEM((width, units), bf16),
            pltpu.VMEM((units, width), bf16),
            pltpu.VMEM((2, devices, CHUNK, width), bf16),
            pltpu.VMEM((devices * CHUNK, width), bf16),
            pltpu.VMEM((devices * CHUNK, width), bf16),
            pltpu.VMEM((devices * CHUNK, units), bf16),
            pltpu.VMEM((tok_rows, width), bf16),
            pltpu.VMEM((chunks, chips, 2, CHUNK, width), bf16),
            pltpu.VMEM((chunks, chips, CHUNK, width), bf16),
            pltpu.VMEM((chunks, chips - 1, CHUNK, width), bf16),
            pltpu.VMEM((chunks, chips - 1, CHUNK, width), bf16),
            dma((2 + devices * out_weight.shape[0],)),
            dma((chunks,)),
            dma((2,)),
            dma((chunks, devices, 3)),
            dma((chunks, devices)),
            dma((chunks,)),
            dma((chunks,)),
            dma((chunks, 2)),
            dma((chunks, 2)),
        ],
        compiler_params=pltpu.CompilerParams(
            collective_id=1, has_side_effects=True, vmem_limit_bytes=60 << 20
        ),
        cost_estimate=pl.CostEstimate(
            flops=2 * total * width * (width + 2 * units),
            bytes_accessed=2 * (2 * total * width + width * (width + 2 * units)),
            transcendentals=total * units,
        ),
        name="mlp_layer",
    )(
        attended.reshape(devices, tok_rows, piece),
        hall,
        out_weight,
        up_weight,
        down_weight,
        out_bias.reshape(1, width),
        gain.reshape(1, width),
        shift.reshape(1, width),
        up_bias.reshape(1, units),
        down_bias.reshape(1, width),
    )


def page_kernel(src_ref, hall, w_ref, gain_ref, shift_ref, live_ref, out_ref, raw, nrm, sem):
    slots = raw.shape[0] // PAGE

    @pl.when(pl.program_id(0) == 0)
    def _():
        copies = [
            pltpu.make_async_copy(hall.at[src_ref[i]], raw.at[pl.ds(i * PAGE, PAGE)], sem.at[i])
            for i in range(slots)
        ]
        for copy in copies:
            copy.start()
        for copy in copies:
            copy.wait()

        norm_rows(
            lambda part: raw[part, :], nrm, slots * PAGE, gain_ref, shift_ref
        )

    parts, depth = w_ref.shape[0], nrm.shape[1] // w_ref.shape[0]

    @pl.loop(0, w_ref.shape[2] // 256)
    def _(i):
        part = pl.ds(pl.multiple_of(i * 256, 256), 256)
        bias = w_ref[0, depth : depth + 1, part].astype(jnp.float32)
        sums = jnp.dot(
            nrm[...],
            w_ref[:, :depth, part].reshape(parts * depth, 256),
            preferred_element_type=jnp.float32,
        )
        made = jnp.where(live_ref[...] > 0, sums + bias, 0.0).astype(jnp.bfloat16)
        out_ref[:, :, part] = made.reshape(slots, PAGE, 256)


def own_pages(hall, kv_weights, gain, shift, page_table, prompt_lengths, seq_len, position):
    devices, tok_rows, width = hall.shape
    pages = devices * tok_rows // PAGE
    capacity = 2 * pages // devices
    owners = page_table[:, 0]
    numbers = jnp.arange(pages, dtype=jnp.int32)
    earlier = (owners[None, :] == owners[:, None]) & (numbers[None, :] < numbers[:, None])
    ranks = jnp.sum(earlier.astype(jnp.int32), axis=1)
    slots = jnp.arange(capacity, dtype=jnp.int32)
    hits = (owners[None, :] == position) & (ranks[None, :] == slots[:, None])
    source = jnp.sum(jnp.where(hits, numbers[None, :], 0), axis=1)
    taken = jnp.sum(hits.astype(jnp.int32), axis=1) > 0
    tokens = source[:, None] * PAGE + jnp.arange(PAGE, dtype=jnp.int32)[None, :]
    stream = tokens // seq_len
    limits = jnp.sum(
        jnp.where(
            stream[:, :, None] == jnp.arange(prompt_lengths.shape[0], dtype=jnp.int32),
            prompt_lengths, 0,
        ),
        axis=2,
    )
    live = (taken[:, None] & (tokens - stream * seq_len < limits)).astype(jnp.int32)
    parts, shards, depth, cols = kv_weights.shape
    total = capacity * PAGE
    return pl.pallas_call(
        page_kernel,
        grid_spec=pltpu.PrefetchScalarGridSpec(
            num_scalar_prefetch=1,
            grid=(shards,),
            in_specs=[
                pl.BlockSpec(memory_space=pl.ANY),
                pl.BlockSpec((parts, None, depth, cols), lambda t, src: (0, t, 0, 0)),
                pl.BlockSpec((1, width), lambda t, src: (0, 0)),
                pl.BlockSpec((1, width), lambda t, src: (0, 0)),
                pl.BlockSpec((total, 1), lambda t, src: (0, 0)),
            ],
            out_specs=pl.BlockSpec((capacity, PAGE, cols), lambda t, src: (0, 0, t)),
            scratch_shapes=[
                pltpu.VMEM((total, width), jnp.bfloat16),
                pltpu.VMEM((total, width), jnp.bfloat16),
                pltpu.SemaphoreType.DMA((capacity,)),
            ],
        ),
        out_shape=jax.ShapeDtypeStruct((capacity, PAGE, shards * cols), jnp.bfloat16),
        compiler_params=pltpu.CompilerParams(vmem_limit_bytes=60 << 20),
        cost_estimate=pl.CostEstimate(
            flops=2 * total * width * shards * cols,
            bytes_accessed=2 * (total * (width + shards * cols) + width * shards * cols),
            transcendentals=0,
        ),
        name="own_pages",
    )(
        source,
        hall.reshape(pages, PAGE, width),
        kv_weights,
        gain.reshape(1, width),
        shift.reshape(1, width),
        live.reshape(total, 1),
    )


def on_line(
    hidden_in, attn_gain, attn_shift, qkv_weight, qkv_bias, out_weight, out_bias, mlp_gain,
    mlp_shift, up_weight, up_bias, down_weight, down_bias, segment_ids, prompt_lengths, page_table,
):
    devices = lax.axis_size("tensor")
    columns = lax.axis_size("dp")
    position, column = lax.axis_index("tensor"), lax.axis_index("dp")
    width = hidden_in.shape[1]
    heads = qkv_weight.shape[1] // (3 * HD)

    out_rows = out_weight.shape[0] // columns
    out_share = lax.dynamic_slice_in_dim(out_weight, column * out_rows, out_rows, 0)
    kv_rows = width // columns
    share = lax.dynamic_slice_in_dim(qkv_weight, column * kv_rows, kv_rows, 0)
    share = jnp.concatenate(
        [share, jnp.broadcast_to(qkv_bias[None, :], (PAGE, qkv_bias.shape[0]))], axis=0
    )
    share = jnp.concatenate(
        [share[:, (3 * n + 1) * HD : (3 * n + 3) * HD] for n in range(heads)], axis=1
    )
    hall, projected, out_whole, kv_whole = gather_project(
        hidden_in, qkv_weight, out_share, share, qkv_bias, attn_gain, attn_shift, devices, columns
    )
    attended = attend(projected.reshape(-1, projected.shape[2]), segment_ids)
    layer_out = mlp_layer(
        attended, hall, out_whole, up_weight, down_weight, out_bias, mlp_gain, mlp_shift, up_bias,
        down_bias,
    )
    kv_pages = own_pages(
        hall, kv_whole, attn_gain, attn_shift, page_table, prompt_lengths, segment_ids.shape[1],
        position,
    )
    return (layer_out, kv_pages)


def on_device(
    hidden_in,
    attn_gain,
    attn_shift,
    qkv_weight,
    qkv_bias,
    out_weight,
    out_bias,
    mlp_gain,
    mlp_shift,
    up_weight,
    up_bias,
    down_weight,
    down_bias,
    segment_ids,
    prompt_lengths,
    page_table,
):
    devices = lax.axis_size("tensor")
    position = lax.axis_index("tensor")
    tok_rows, width = hidden_in.shape
    total_rows = tok_rows * devices
    streams, seq_len = segment_ids.shape
    whole_heads = qkv_weight.shape[1] % (3 * HD) == 0

    normed = normalize(hidden_in, attn_gain, attn_shift).astype(jnp.bfloat16)
    if not whole_heads:
        qkv_weight = join_pair(qkv_weight, 1, position)
        qkv_bias = join_pair(qkv_bias, 0, position)
    gathered = lax.all_gather(normed, "tensor", axis=0, tiled=True)
    projected = (
        jnp.dot(gathered, qkv_weight, preferred_element_type=jnp.float32)
        + qkv_bias.astype(jnp.float32)
    ).astype(jnp.bfloat16)
    heads_here = projected.shape[1] // (3 * HD)
    keys_vals = jnp.concatenate(
        [
            lax.slice_in_dim(projected, (3 * n + 1) * HD, (3 * n + 3) * HD, axis=1)
            for n in range(heads_here)
        ],
        axis=1,
    )
    if not whole_heads:
        half = keys_vals.shape[1] // 2
        keys_vals = lax.dynamic_slice_in_dim(keys_vals, position % 2 * half, half, 1)
    live = jnp.arange(seq_len, dtype=jnp.int32)[None, :] < prompt_lengths[:, None]
    pieces = pack_pages(
        keys_vals, live, page_table, 2 * (total_rows // PAGE) // devices, position
    )
    projected, pieces = lax.optimization_barrier((projected, pieces))
    received = send_pages(pieces)
    far, step = devices // 2, devices // 8
    attended = attend(projected, segment_ids)
    if not whole_heads:
        half = attended.shape[1] // 2
        attended = lax.dynamic_slice_in_dim(attended, position % 2 * half, half, 1)
    attended, received[far : far + step] = lax.optimization_barrier(
        (attended, received[far : far + step])
    )

    part = tok_rows // CHUNKS
    shaped = attended.reshape(devices, CHUNKS, part, attended.shape[1])
    sums = []
    for chunk in range(CHUNKS):
        rows = shaped[:, chunk].reshape(devices * part, -1)
        terms = jnp.dot(rows, out_weight, preferred_element_type=jnp.float32)
        sums.append(
            lax.psum_scatter(
                terms.astype(jnp.bfloat16), "tensor", scatter_dimension=0, tiled=True
            )
        )
    residuals, gathers = [], []
    for chunk in range(CHUNKS):
        hidden = lax.slice_in_dim(hidden_in, chunk * part, (chunk + 1) * part, axis=0)
        attn_sum = sums[chunk]
        if chunk == 0:
            attn_sum, received[far + step : far + 3 * step] = lax.optimization_barrier(
                (attn_sum, received[far + step : far + 3 * step])
            )
        else:
            attn_sum, residuals[-1], received, _ = lax.optimization_barrier(
                (attn_sum, residuals[-1], received, normed_mid)
            )
        residual_mid = (
            hidden.astype(jnp.float32) + attn_sum.astype(jnp.float32) + out_bias
        ).astype(jnp.bfloat16)
        normed_mid = normalize(residual_mid, mlp_gain, mlp_shift).astype(jnp.bfloat16)
        residuals.append(residual_mid)
        gathers.append(lax.all_gather(normed_mid, "tensor", axis=0, tiled=True))
    sums = []
    for chunk in range(CHUNKS):
        lifted = jnp.dot(gathers[chunk], up_weight, preferred_element_type=jnp.float32) + up_bias
        expanded = jax.nn.gelu(lifted, approximate=False).astype(jnp.bfloat16)
        expanded = lax.optimization_barrier(expanded)
        terms = jnp.dot(expanded, down_weight, preferred_element_type=jnp.float32)
        sums.append(
            lax.psum_scatter(
                terms.astype(jnp.bfloat16), "tensor", scatter_dimension=0, tiled=True
            )
        )
    kv_pages = lay_out_pages(received, position)
    outs = [
        (residual_mid.astype(jnp.float32) + mlp_sum.astype(jnp.float32) + down_bias).astype(
            jnp.bfloat16
        )
        for residual_mid, mlp_sum in zip(residuals, sums)
    ]
    layer_out = outs[0] if CHUNKS == 1 else jnp.concatenate(outs, axis=0)
    return (layer_out, kv_pages)


def solution(mesh):
    in_specs = (
        P(("dp", "tensor"), None),
        P(),
        P(),
        P(None, "tensor"),
        P("tensor"),
        P("tensor", None),
        P(),
        P(),
        P(),
        P(None, "tensor"),
        P("tensor"),
        P("tensor", None),
        P(),
        P("dp", None),
        P("dp"),
        P("dp", None),
    )
    out_specs = (P(("dp", "tensor"), None), P(("dp", "tensor"), None, None))
    body = on_line if (mesh.shape["dp"], mesh.shape["tensor"]) == SQUARE_LINE else on_device
    return jax.shard_map(
        body, mesh=mesh, in_specs=in_specs, out_specs=out_specs, check_vma=False
    )
```

```python
import functools
import math

import jax
import jax.numpy as jnp
from jax import lax
from jax.experimental import pallas as pl
from jax.experimental.pallas import tpu as pltpu
from jax.sharding import PartitionSpec as P

HD = 128
PAGE = 16
MAX_DOC = 1024
Q_BLOCK = 256
CHUNKS = 2


def normalize(values, norm_gain, norm_shift):
    widened = values.astype(jnp.float32)
    center = jnp.mean(widened, axis=-1, keepdims=True)
    spread = jnp.mean(jnp.square(widened - center), axis=-1, keepdims=True)
    return (widened - center) * lax.rsqrt(spread + 1e-05) * norm_gain + norm_shift


def attend_kernel(most, count_ref, proj_ref, qseg_ref, kseg_ref, out_ref):
    stream, block = pl.program_id(0), pl.program_id(1)
    rows = out_ref.shape[0]
    heads = out_ref.shape[1] // HD
    count = count_ref[stream * pl.num_programs(1) + block]
    here = pl.ds(pl.multiple_of(block * rows, rows), rows)

    def over(blocks):
        window = blocks * rows
        start = pl.multiple_of((block - blocks + 1) * rows, rows)
        ahead = lax.broadcasted_iota(jnp.int32, (rows, window), 1) - lax.broadcasted_iota(
            jnp.int32, (rows, window), 0
        )
        allowed = (ahead <= window - rows) & (
            qseg_ref[...] == kseg_ref[0, :, pl.ds(start, window)]
        )
        scores = [
            lax.dot_general(
                proj_ref[here, 3 * n * HD : (3 * n + 1) * HD],
                proj_ref[pl.ds(start, window), (3 * n + 1) * HD : (3 * n + 2) * HD],
                (((1,), (1,)), ((), ())),
                preferred_element_type=jnp.float32,
            )
            for n in range(heads)
        ]
        for n in range(heads):
            masked = jnp.where(allowed, scores[n] * (1.0 / math.sqrt(HD)), -1e30)
            expo = jnp.exp(masked - jnp.max(masked, axis=1, keepdims=True))
            weights = (expo * (1.0 / jnp.sum(expo, axis=1, keepdims=True))).astype(jnp.bfloat16)
            values = proj_ref[pl.ds(start, window), (3 * n + 2) * HD : (3 * n + 3) * HD]
            out_ref[:, n * HD : (n + 1) * HD] = jnp.dot(
                weights, values, preferred_element_type=jnp.float32
            ).astype(jnp.bfloat16)

    for blocks in range(1, most + 1):
        pl.when(count == blocks)(functools.partial(over, blocks))


def attend(projected, segment_ids):
    streams, seq_len = segment_ids.shape
    heads = projected.shape[1] // (3 * HD)
    blocks = seq_len // Q_BLOCK
    most = min(blocks, MAX_DOC // Q_BLOCK + 1)
    pairs = streams * heads * seq_len * 2 * Q_BLOCK
    firsts = segment_ids[:, ::Q_BLOCK]
    begins = jnp.sum((segment_ids[:, None, :] < firsts[:, :, None]).astype(jnp.int32), axis=2)
    counts = jnp.arange(blocks, dtype=jnp.int32)[None, :] - begins // Q_BLOCK + 1
    counts = jnp.clip(counts, 1, most).reshape(-1)
    return pl.pallas_call(
        functools.partial(attend_kernel, most),
        grid_spec=pltpu.PrefetchScalarGridSpec(
            num_scalar_prefetch=1,
            grid=(streams, blocks),
            in_specs=[
                pl.BlockSpec((seq_len, 3 * heads * HD), lambda s, i, counts: (s, 0)),
                pl.BlockSpec((Q_BLOCK, 1), lambda s, i, counts: (s * blocks + i, 0)),
                pl.BlockSpec((1, 1, seq_len), lambda s, i, counts: (s, 0, 0)),
            ],
            out_specs=pl.BlockSpec((Q_BLOCK, heads * HD), lambda s, i, counts: (s * blocks + i, 0)),
        ),
        out_shape=jax.ShapeDtypeStruct((streams * seq_len, heads * HD), jnp.bfloat16),
        compiler_params=pltpu.CompilerParams(vmem_limit_bytes=60 << 20),
        cost_estimate=pl.CostEstimate(
            flops=4 * pairs * HD,
            bytes_accessed=2 * projected.size * 2,
            transcendentals=pairs,
        ),
        name="attend",
    )(
        counts,
        projected,
        segment_ids.reshape(streams * seq_len, 1),
        segment_ids.reshape(streams, 1, seq_len),
    )


def join_pair(value, axis, position):
    devices = lax.axis_size("tensor")
    other = lax.ppermute(value, "tensor", [(source, source ^ 1) for source in range(devices)])
    first = jnp.where(position % 2 == 0, value, other)
    second = jnp.where(position % 2 == 0, other, value)
    return jnp.concatenate([first, second], axis=axis)


def copy_page(index_ref, page_ref, out_ref):
    out_ref[...] = page_ref[...]


def take_pages(page_rows, index):
    block = (1,) + page_rows.shape[1:]
    return pl.pallas_call(
        copy_page,
        grid_spec=pltpu.PrefetchScalarGridSpec(
            num_scalar_prefetch=1,
            grid=(index.shape[0],),
            in_specs=[pl.BlockSpec(block, lambda i, index: (index[i], 0, 0))],
            out_specs=pl.BlockSpec(block, lambda i, index: (i, 0, 0)),
        ),
        out_shape=jax.ShapeDtypeStruct(index.shape + page_rows.shape[1:], page_rows.dtype),
    )(index, page_rows)


def pack_pages(keys_vals, live, page_table, capacity, position):
    devices = lax.axis_size("tensor")
    pages = keys_vals.shape[0] // PAGE
    owners = page_table[:, 0]
    numbers = jnp.arange(pages, dtype=jnp.int32)
    earlier = (owners[None, :] == owners[:, None]) & (numbers[None, :] < numbers[:, None])
    ranks = jnp.sum(earlier.astype(jnp.int32), axis=1)
    slot_ids = owners * capacity + ranks
    owner_order = position ^ jnp.arange(devices, dtype=jnp.int32)
    slots = owner_order[:, None] * capacity + jnp.arange(capacity, dtype=jnp.int32)[None, :]
    hits = slot_ids[None, :] == slots.reshape(-1)[:, None]
    source_page = jnp.sum(jnp.where(hits, numbers[None, :], 0), axis=1)
    live_pages = live.reshape(pages, PAGE).astype(jnp.int32)
    kept = jnp.sum(jnp.where(hits[:, :, None], live_pages[None], 0), axis=1) > 0
    page_rows = keys_vals.reshape(pages, PAGE, -1)
    taken = take_pages(page_rows, source_page)
    outgoing = jnp.where(kept[:, :, None], taken, 0).astype(jnp.bfloat16)
    return [
        lax.slice_in_dim(outgoing, apart * capacity, (apart + 1) * capacity, axis=0)
        for apart in range(devices)
    ]


def send_pages(pieces):
    devices = len(pieces)
    received = [pieces[0]]
    for apart in range(1, devices):
        hops = [(source, source ^ apart) for source in range(devices)]
        received.append(lax.ppermute(pieces[apart], "tensor", hops))
    return received


def lay_out_pages(received, position):
    devices = len(received)
    slots, page, width = received[0].shape
    laid = jnp.zeros((slots, page, devices * width), received[0].dtype)
    for apart in range(devices):
        laid = lax.dynamic_update_slice_in_dim(
            laid, received[apart], (position ^ apart) * width, axis=2
        )
    return laid


MESH = pl.DeviceIdType.MESH
SQUARE_LINE = (4, 8)
CHUNK = 32
TILE = 1024


def layer_norm(values, gain, shift):
    widened = values.astype(jnp.float32)
    center = jnp.mean(widened, axis=-1, keepdims=True)
    moved = widened - center
    spread = jnp.mean(moved * moved, axis=-1, keepdims=True)
    return moved * lax.rsqrt(spread + 1e-05) * gain + shift


def norm_rows(load, out, rows, gain_ref, shift_ref):
    @pl.loop(0, rows // 16, unroll=4)
    def _(i):
        part = pl.ds(pl.multiple_of(i * 16, 16), 16)
        out[part, :] = layer_norm(load(part), gain_ref[...], shift_ref[...]).astype(jnp.bfloat16)


def greet(me, chips, across=()):
    z, c = me // 2, lax.rem(me, 2)
    barrier = pltpu.get_barrier_semaphore()
    pl.semaphore_signal(barrier, inc=1, device_id={"tensor": 2 * z + 1 - c}, device_id_type=MESH)
    for column in across:
        pl.semaphore_signal(barrier, inc=1, device_id={"dp": column}, device_id_type=MESH)

    @pl.when(z > 0)
    def _():
        pl.semaphore_signal(barrier, inc=1, device_id={"tensor": me - 2}, device_id_type=MESH)

    @pl.when(z < chips - 1)
    def _():
        pl.semaphore_signal(barrier, inc=1, device_id={"tensor": me + 2}, device_id_type=MESH)

    peers = 1 + len(across) + (z > 0).astype(jnp.int32) + (z < chips - 1).astype(jnp.int32)
    pl.semaphore_wait(barrier, peers)


def gather_project_kernel(
    chips, hid, w_hbm, oshare, kshare, b_ref, gain_ref, shift_ref, hall_out, proj_out, oall, kall,
    buf, w_ref, nrm, pbuf, ssem, rsem, lsem, psem, wsem, share_s, share_r,
):
    me, p = lax.axis_index("tensor"), lax.axis_index("dp")
    z, c = me // 2, lax.rem(me, 2)
    twin = 2 * z + 1 - c
    beside, over, corner = p + 1 - 2 * lax.rem(p, 2), lax.rem(p + 2, 4), 3 - p
    rows, width = hid.shape
    cols = w_ref.shape[1]
    pair, own_share = (oall, kall), (oshare, kshare)
    load = pltpu.make_async_copy(w_hbm, w_ref, wsem.at[0])
    own = pltpu.make_async_copy(hid, buf.at[me], wsem.at[1])
    own_shares = [
        pltpu.make_async_copy(oshare, oall.at[p, me], wsem.at[2]),
        pltpu.make_async_copy(kshare, kall.at[p, me], wsem.at[3]),
    ]
    for copy in own_shares:
        copy.start()
    own.start()
    load.start()
    greet(me, chips, (beside, over))

    def share_copy(a, q, slot, way, own_from=False):
        device = [
            {"tensor": me - 2}, {"tensor": me + 2}, {"tensor": twin}, {"dp": beside}, {"dp": over},
        ][way]
        source = own_share[a] if own_from else pair[a].at[q, slot]
        return pltpu.make_async_remote_copy(
            src_ref=source, dst_ref=pair[a].at[q, slot],
            send_sem=share_s.at[a, q, slot, way], recv_sem=share_r.at[a, q, slot],
            device_id=device, device_id_type=MESH,
        )

    def share_send(q, slot, *ways):
        for a in range(2):
            for way in ways:
                share_copy(a, q, slot, way).start()

    def own_share_send(*ways):
        for a in range(2):
            for way in ways:
                share_copy(a, p, me, way, True).start()

    def share_arrived(q, slot):
        for a in range(2):
            share_copy(a, q, slot, 2).wait_recv()

    def share_line(hop):
        @pl.when(z - hop >= 0)
        def _():
            slot = me - 2 * hop
            share_arrived(p, slot)

            @pl.when(z < chips - 1)
            def _():
                share_send(p, slot, 1)

            share_send(p, slot, 3, 4, 2)

        @pl.when(z + hop < chips)
        def _():
            slot = me + 2 * hop
            share_arrived(p, slot)

            @pl.when(z > 0)
            def _():
                share_send(p, slot, 0)

            share_send(p, slot, 3, 4, 2)

    def at_slots(hop, run):
        if hop == 0:
            run(me)
        else:
            pl.when(z - hop >= 0)(lambda: run(me - 2 * hop))
            pl.when(z + hop < chips)(lambda: run(me + 2 * hop))

    def share_across(slot):
        share_arrived(over, slot)
        pl.when(c == 0)(lambda: share_send(over, slot, 3))
        share_arrived(beside, slot)
        pl.when(c == 1)(lambda: share_send(beside, slot, 4))
        share_send(over, slot, 2)
        share_send(beside, slot, 2)

    def share_corner(slot):
        share_arrived(corner, slot)
        share_send(corner, slot, 2)

    def send(slot, device, way):
        pltpu.make_async_remote_copy(
            src_ref=buf.at[slot], dst_ref=buf.at[slot], send_sem=ssem.at[slot, way],
            recv_sem=rsem.at[slot], device_id={"tensor": device}, device_id_type=MESH,
        ).start()

    def sent(slot, way):
        pltpu.make_async_remote_copy(
            src_ref=buf.at[slot], dst_ref=buf.at[slot], send_sem=ssem.at[slot, way],
            recv_sem=rsem.at[slot], device_id={"tensor": twin}, device_id_type=MESH,
        ).wait_send()

    def arrived(slot):
        pltpu.make_async_copy(hid, buf.at[slot], rsem.at[slot]).wait()

    def compute(slot):
        pltpu.make_async_copy(buf.at[slot], hall_out.at[slot], lsem.at[slot]).start()

        norm_rows(lambda part: buf[slot, part, :], nrm, rows, gain_ref, shift_ref)

        pbuf[slot] = (
            jnp.dot(nrm[...], w_ref[...], preferred_element_type=jnp.float32)
            + b_ref[...].astype(jnp.float32)
        ).astype(jnp.bfloat16)

        pltpu.make_async_copy(pbuf.at[slot], proj_out.at[slot], psem.at[slot]).start()

    def token_line(hop):
        @pl.when(z - hop >= 0)
        def _():
            slot = me - 2 * hop
            arrived(slot)

            @pl.when(z < chips - 1)
            def _():
                send(slot, me + 2, 1)

            send(slot, twin, 2)

        @pl.when(z + hop < chips)
        def _():
            slot = me + 2 * hop
            arrived(slot)

            @pl.when(z > 0)
            def _():
                send(slot, me - 2, 0)

            send(slot, twin, 2)

    def token_compute(hop):
        @pl.when(z - hop >= 0)
        def _():
            compute(me - 2 * hop)
            arrived(twin - 2 * hop)
            compute(twin - 2 * hop)

        @pl.when(z + hop < chips)
        def _():
            compute(me + 2 * hop)
            arrived(twin + 2 * hop)
            compute(twin + 2 * hop)

    pl.when(z > 0)(lambda: own_share_send(0))
    pl.when(z < chips - 1)(lambda: own_share_send(1))
    own_share_send(3, 4, 2)
    own.wait()
    load.wait()
    compute(me)
    for hop in range(1, chips - 1):
        share_line(hop)
        if hop == 1:
            at_slots(0, share_across)
    pl.when(z > 0)(lambda: send(me, me - 2, 0))
    pl.when(z < chips - 1)(lambda: send(me, me + 2, 1))
    send(me, twin, 2)
    share_line(chips - 1)
    arrived(twin)
    compute(twin)
    for hop in range(1, chips):
        at_slots(hop, share_across)
        at_slots(hop - 1, share_corner)
        token_line(hop)
        token_compute(hop)
    at_slots(chips - 1, share_corner)

    for copy in own_shares:
        copy.wait()
    for slot in range(2 * chips):
        pltpu.make_async_copy(buf.at[slot], hall_out.at[slot], lsem.at[slot]).wait()
        pltpu.make_async_copy(pbuf.at[slot], proj_out.at[slot], psem.at[slot]).wait()
    for origin in range(chips):
        slot = 2 * origin + c
        sent(slot, 2)
        for q in (beside, over, corner):
            share_arrived(q, 2 * origin + 1 - c)

        share_arrived(p, 2 * origin + 1 - c)

        @pl.when((origin >= z) & (z > 0))
        def _():
            sent(slot, 0)
            for a in range(2):
                share_copy(a, p, slot, 0).wait_send()

        @pl.when((origin <= z) & (z < chips - 1))
        def _():
            sent(slot, 1)
            for a in range(2):
                share_copy(a, p, slot, 1).wait_send()

        for a in range(2):
            for q in (p, beside, over, corner):
                share_copy(a, q, slot, 2).wait_send()
            share_copy(a, p, slot, 3).wait_send()
            share_copy(a, p, slot, 4).wait_send()

            @pl.when(c == 0)
            def _():
                share_copy(a, over, slot, 3).wait_send()

            @pl.when(c == 1)
            def _():
                share_copy(a, beside, slot, 4).wait_send()


def gather_project(
    hidden_in, qkv_weight, out_share, kv_share, qkv_bias, gain, shift, devices, columns
):
    rows, width = hidden_in.shape
    cols = qkv_weight.shape[1]
    hbm, vmem = pl.BlockSpec(memory_space=pl.ANY), pl.BlockSpec(memory_space=pltpu.VMEM)
    total = rows * devices
    dma = pltpu.SemaphoreType.DMA
    return pl.pallas_call(
        functools.partial(gather_project_kernel, devices // 2),
        in_specs=[hbm] * 4 + [vmem] * 3,
        out_specs=[hbm] * 4,
        out_shape=[
            jax.ShapeDtypeStruct((devices, rows, width), jnp.bfloat16),
            jax.ShapeDtypeStruct((devices, rows, cols), jnp.bfloat16),
            jax.ShapeDtypeStruct((columns, devices) + out_share.shape, jnp.bfloat16),
            jax.ShapeDtypeStruct((columns, devices) + kv_share.shape, jnp.bfloat16),
        ],
        scratch_shapes=[
            pltpu.VMEM((devices, rows, width), jnp.bfloat16),
            pltpu.VMEM((width, cols), jnp.bfloat16),
            pltpu.VMEM((rows, width), jnp.bfloat16),
            pltpu.VMEM((devices, rows, cols), jnp.bfloat16),
            dma((devices, 3)),
            dma((devices,)),
            dma((devices,)),
            dma((devices,)),
            dma((4,)),
            dma((2, columns, devices, 5)),
            dma((2, columns, devices)),
        ],
        compiler_params=pltpu.CompilerParams(
            collective_id=0, has_side_effects=True, vmem_limit_bytes=60 << 20
        ),
        cost_estimate=pl.CostEstimate(
            flops=2 * total * width * cols,
            bytes_accessed=2 * (total * (width + cols) + width * cols),
            transcendentals=0,
        ),
        name="gather_project",
    )(
        hidden_in, qkv_weight, out_share, kv_share, qkv_bias.reshape(1, cols),
        gain.reshape(1, width), shift.reshape(1, width),
    )


def mlp_kernel(
    chips, att, hall, outw_hbm, upw_hbm, dnw_hbm, outb_ref, gain_ref, shift_ref, upb_ref, dnb_ref,
    out_ref,
    ag, outw, upw, dnw, hbuf, res, nrm, exp_, own_res, par, tw, lin, rin,
    wsem, osem, hsem, ag_s, ag_r, tw_s, tw_r, rs_s, rs_r,
):
    me = lax.axis_index("tensor")
    z, c = me // 2, lax.rem(me, 2)
    twin = 2 * z + 1 - c
    devices = 2 * chips
    chunks = ag.shape[0]
    width = outw.shape[1]
    piece = att.shape[-1]
    hidden_units = upw.shape[1]
    rows = devices * CHUNK

    columns, _, out_rows, _ = outw_hbm.shape
    loads = [
        pltpu.make_async_copy(
            outw_hbm.at[p, d], outw.at[pl.ds((d * columns + p) * out_rows, out_rows)], wsem.at[2 + d * columns + p]
        )
        for d in range(devices)
        for p in range(columns)
    ] + [
        pltpu.make_async_copy(upw_hbm, upw, wsem.at[0]),
        pltpu.make_async_copy(dnw_hbm, dnw, wsem.at[1]),
    ]

    def place(k, device):
        return ag.at[k, :, :, pl.ds(pl.multiple_of(device * piece, piece), piece)]

    def own_piece(k):
        part = pl.ds(pl.multiple_of(k * CHUNK, CHUNK), CHUNK)
        return pltpu.make_async_copy(att.at[:, part, :], place(k, me), osem.at[k])

    def hidden_part(k):
        part = pl.ds(pl.multiple_of(k * CHUNK, CHUNK), CHUNK)
        return pltpu.make_async_copy(hall.at[:, part, :], hbuf.at[lax.rem(k, 2)], hsem.at[lax.rem(k, 2)])

    @pl.loop(0, chunks)
    def _(k):
        own_piece(k).start()

    for load in loads:
        load.start()
    greet(me, chips)

    def piece_copy(k, origin, device, way):
        return pltpu.make_async_remote_copy(
            src_ref=place(k, origin), dst_ref=place(k, origin), send_sem=ag_s.at[k, origin, way],
            recv_sem=ag_r.at[k, origin], device_id={"tensor": device}, device_id_type=MESH,
        )

    def piece_wait(k, origin):
        piece_copy(k, origin, twin, 2).wait_recv()

    def twin_copy(k, half):
        part = pl.ds(half * (width // 2), width // 2)
        return pltpu.make_async_remote_copy(
            src_ref=par.at[k, :, 1 - c, :, part], dst_ref=tw.at[k, :, :, part],
            send_sem=tw_s.at[k, half], recv_sem=tw_r.at[k, half],
            device_id={"tensor": twin}, device_id_type=MESH,
        )

    def right_copy(k, chip):
        return pltpu.make_async_remote_copy(
            src_ref=par.at[k, chip, c], dst_ref=lin.at[k, chip - 1],
            send_sem=rs_s.at[k, 0, chip], recv_sem=rs_r.at[k, 0, chip],
            device_id={"tensor": me + 2}, device_id_type=MESH,
        )

    def left_copy(k, chip):
        return pltpu.make_async_remote_copy(
            src_ref=par.at[k, chip, c], dst_ref=rin.at[k, chip],
            send_sem=rs_s.at[k, 1, chip], recv_sem=rs_r.at[k, 1, chip],
            device_id={"tensor": me - 2}, device_id_type=MESH,
        )

    def add_to(k, chip, more):
        par[k, chip, c] = (par[k, chip, c].astype(jnp.float32) + more.astype(jnp.float32)).astype(
            jnp.bfloat16
        )

    def at_chunk(k, run):
        pl.when((k >= 0) & (k < chunks))(lambda: run(k))

    def first_hop(k):
        own_piece(k).wait()

        @pl.when(z > 0)
        def _():
            piece_copy(k, me, me - 2, 0).start()

        @pl.when(z < chips - 1)
        def _():
            piece_copy(k, me, me + 2, 1).start()

        piece_copy(k, me, twin, 2).start()

    def later_hop(hop, k):
        @pl.when(z - hop >= 0)
        def _():
            origin = me - 2 * hop
            piece_wait(k, origin)

            @pl.when(z < chips - 1)
            def _():
                piece_copy(k, origin, me + 2, 1).start()

            piece_copy(k, origin, twin, 2).start()

        @pl.when(z + hop < chips)
        def _():
            origin = me + 2 * hop
            piece_wait(k, origin)

            @pl.when(z > 0)
            def _():
                piece_copy(k, origin, me - 2, 0).start()

            piece_copy(k, origin, twin, 2).start()

    def join_twins(k):
        for half in range(2):
            twin_copy(k, half).wait_recv()

        @pl.when(z < chips // 2)
        def _():
            for chip in reversed(range(chips)):
                add_to(k, chip, tw[k, chip])
                if chip > 0:
                    pl.when(z == 0)(lambda: right_copy(k, chip).start())

        @pl.when(z >= chips // 2)
        def _():
            for chip in range(chips):
                add_to(k, chip, tw[k, chip])
                if chip < chips - 1:
                    pl.when(z == chips - 1)(lambda: left_copy(k, chip).start())

    def add_left(k, at):
        for chip in reversed(range(at, chips)):
            right_copy(k, chip).wait_recv()
            add_to(k, chip, lin[k, chip - 1])
            if chip > at:
                right_copy(k, chip).start()

    def add_right(k, at):
        for chip in range(at + 1):
            left_copy(k, chip).wait_recv()
            add_to(k, chip, rin[k, chip])
            if chip < at:
                left_copy(k, chip).start()

    def pass_on(hop, k):
        for at in range(1, chips):
            if at == hop:

                @pl.when(z == at)
                def _():
                    add_left(k, at)

                @pl.when(z == chips - 1 - at)
                def _():
                    add_right(k, chips - 1 - at)

    def finish(k):
        part = pl.ds(pl.multiple_of(k * CHUNK, CHUNK), CHUNK)
        out_ref[part, :] = (
            own_res[part, :].astype(jnp.float32) + par[k, z, c].astype(jnp.float32) + dnb_ref[...]
        ).astype(jnp.bfloat16)

    def compute(k):
        for hop in range(1, chips):

            @pl.when(z - hop >= 0)
            def _():
                piece_wait(k, twin - 2 * hop)

            @pl.when(z + hop < chips)
            def _():
                piece_wait(k, twin + 2 * hop)

        piece_wait(k, twin)
        hidden_part(k).wait()
        slot = lax.rem(k, 2)

        @pl.when(k + 1 < chunks)
        def _():
            hidden_part(k + 1).start()

        @pl.when(k == 0)
        def _():
            for load in loads:
                load.wait()

        @pl.loop(0, width // TILE)
        def _(i):
            part = pl.ds(pl.multiple_of(i * TILE, TILE), TILE)
            terms = jnp.dot(
                ag[k].reshape(rows, width), outw[:, part], preferred_element_type=jnp.float32
            )
            res[:, part] = (
                hbuf[slot, :, :, part].reshape(rows, TILE).astype(jnp.float32)
                + terms
                + outb_ref[:, part]
            ).astype(jnp.bfloat16)

        norm_rows(lambda part: res[part, :], nrm, rows, gain_ref, shift_ref)
        own_res[pl.ds(pl.multiple_of(k * CHUNK, CHUNK), CHUNK), :] = res[
            pl.ds(pl.multiple_of(me * CHUNK, CHUNK), CHUNK), :
        ]

        for i in range(hidden_units // 256):
            part = slice(i * 256, (i + 1) * 256)
            lifted = (
                jnp.dot(nrm[...], upw[:, part], preferred_element_type=jnp.float32) + upb_ref[:, part]
            )
            exp_[:, part] = (0.5 * lifted * (1.0 + lax.erf(lifted * math.sqrt(0.5)))).astype(
                jnp.bfloat16
            )

        for half in range(2):
            part = slice(half * (width // 2), (half + 1) * (width // 2))
            par[k, :, :, :, part] = (
                jnp.dot(exp_[...], dnw[:, part], preferred_element_type=jnp.float32)
                .astype(jnp.bfloat16)
                .reshape(chips, 2, CHUNK, width // 2)
            )
            twin_copy(k, half).start()

    hidden_part(0).start()

    @pl.loop(0, chunks + 2 * chips - 2)
    def _(s):
        at_chunk(s, first_hop)
        for hop in range(1, chips):
            at_chunk(s - hop, functools.partial(later_hop, hop))
        at_chunk(s - chips + 1, compute)
        at_chunk(s - chips + 1, join_twins)
        for hop in range(1, chips):
            at_chunk(s - chips + 1 - hop, functools.partial(pass_on, hop))
        at_chunk(s - 2 * chips + 2, finish)

    @pl.loop(0, chunks)
    def _(k):
        for origin in range(chips):
            slot = 2 * origin + c
            piece_copy(k, slot, twin, 2).wait_send()

            @pl.when((origin >= z) & (z > 0))
            def _():
                piece_copy(k, slot, twin, 0).wait_send()

            @pl.when((origin <= z) & (z < chips - 1))
            def _():
                piece_copy(k, slot, twin, 1).wait_send()

        for half in range(2):
            twin_copy(k, half).wait_send()
        for chip in range(chips):
            pl.when(z < chip)(lambda: right_copy(k, chip).wait_send())
            pl.when(z > chip)(lambda: left_copy(k, chip).wait_send())


def mlp_layer(
    attended, hall, out_weight, up_weight, down_weight, out_bias, gain, shift, up_bias, down_bias
):
    devices, tok_rows, width = hall.shape
    chips, chunks = devices // 2, tok_rows // CHUNK
    piece, units = attended.shape[1], up_weight.shape[1]
    total = devices * tok_rows
    hbm, vmem = pl.BlockSpec(memory_space=pl.ANY), pl.BlockSpec(memory_space=pltpu.VMEM)
    dma = pltpu.SemaphoreType.DMA
    bf16 = jnp.bfloat16
    return pl.pallas_call(
        functools.partial(mlp_kernel, chips),
        in_specs=[hbm] * 5 + [vmem] * 5,
        out_specs=vmem,
        out_shape=jax.ShapeDtypeStruct((tok_rows, width), bf16),
        scratch_shapes=[
            pltpu.VMEM((chunks, devices, CHUNK, width), bf16),
            pltpu.VMEM((width, width), bf16),
            pltpu.VMEM((width, units), bf16),
            pltpu.VMEM((units, width), bf16),
            pltpu.VMEM((2, devices, CHUNK, width), bf16),
            pltpu.VMEM((devices * CHUNK, width), bf16),
            pltpu.VMEM((devices * CHUNK, width), bf16),
            pltpu.VMEM((devices * CHUNK, units), bf16),
            pltpu.VMEM((tok_rows, width), bf16),
            pltpu.VMEM((chunks, chips, 2, CHUNK, width), bf16),
            pltpu.VMEM((chunks, chips, CHUNK, width), bf16),
            pltpu.VMEM((chunks, chips - 1, CHUNK, width), bf16),
            pltpu.VMEM((chunks, chips - 1, CHUNK, width), bf16),
            dma((2 + devices * out_weight.shape[0],)),
            dma((chunks,)),
            dma((2,)),
            dma((chunks, devices, 3)),
            dma((chunks, devices)),
            dma((chunks, 2)),
            dma((chunks, 2)),
            dma((chunks, 2, chips)),
            dma((chunks, 2, chips)),
        ],
        compiler_params=pltpu.CompilerParams(
            collective_id=1, has_side_effects=True, vmem_limit_bytes=60 << 20
        ),
        cost_estimate=pl.CostEstimate(
            flops=2 * total * width * (width + 2 * units),
            bytes_accessed=2 * (2 * total * width + width * (width + 2 * units)),
            transcendentals=total * units,
        ),
        name="mlp_layer",
    )(
        attended.reshape(devices, tok_rows, piece),
        hall,
        out_weight,
        up_weight,
        down_weight,
        out_bias.reshape(1, width),
        gain.reshape(1, width),
        shift.reshape(1, width),
        up_bias.reshape(1, units),
        down_bias.reshape(1, width),
    )


def page_kernel(src_ref, hall, w_ref, gain_ref, shift_ref, live_ref, out_ref, raw, nrm, sem):
    slots = raw.shape[0] // PAGE

    @pl.when(pl.program_id(0) == 0)
    def _():
        copies = [
            pltpu.make_async_copy(hall.at[src_ref[i]], raw.at[pl.ds(i * PAGE, PAGE)], sem.at[i])
            for i in range(slots)
        ]
        for copy in copies:
            copy.start()
        for copy in copies:
            copy.wait()

        norm_rows(
            lambda part: raw[part, :], nrm, slots * PAGE, gain_ref, shift_ref
        )

    parts, depth = w_ref.shape[0], nrm.shape[1] // w_ref.shape[0]

    bias = w_ref[0, depth : depth + 1, :].astype(jnp.float32)
    sums = jnp.dot(
        nrm[...],
        w_ref[:, :depth, :].reshape(parts * depth, w_ref.shape[2]),
        preferred_element_type=jnp.float32,
    )
    made = jnp.where(live_ref[...] > 0, sums + bias, 0.0).astype(jnp.bfloat16)
    out_ref[...] = made.reshape(slots, PAGE, -1)


def own_pages(hall, kv_weights, gain, shift, page_table, prompt_lengths, seq_len, position):
    devices, tok_rows, width = hall.shape
    pages = devices * tok_rows // PAGE
    capacity = 2 * pages // devices
    owners = page_table[:, 0]
    numbers = jnp.arange(pages, dtype=jnp.int32)
    earlier = (owners[None, :] == owners[:, None]) & (numbers[None, :] < numbers[:, None])
    ranks = jnp.sum(earlier.astype(jnp.int32), axis=1)
    slots = jnp.arange(capacity, dtype=jnp.int32)
    hits = (owners[None, :] == position) & (ranks[None, :] == slots[:, None])
    source = jnp.sum(jnp.where(hits, numbers[None, :], 0), axis=1)
    taken = jnp.sum(hits.astype(jnp.int32), axis=1) > 0
    tokens = source[:, None] * PAGE + jnp.arange(PAGE, dtype=jnp.int32)[None, :]
    stream = tokens // seq_len
    limits = jnp.sum(
        jnp.where(
            stream[:, :, None] == jnp.arange(prompt_lengths.shape[0], dtype=jnp.int32),
            prompt_lengths, 0,
        ),
        axis=2,
    )
    live = (taken[:, None] & (tokens - stream * seq_len < limits)).astype(jnp.int32)
    parts, shards, depth, cols = kv_weights.shape
    total = capacity * PAGE
    return pl.pallas_call(
        page_kernel,
        grid_spec=pltpu.PrefetchScalarGridSpec(
            num_scalar_prefetch=1,
            grid=(shards,),
            in_specs=[
                pl.BlockSpec(memory_space=pl.ANY),
                pl.BlockSpec((parts, None, depth, cols), lambda t, src: (0, t, 0, 0)),
                pl.BlockSpec((1, width), lambda t, src: (0, 0)),
                pl.BlockSpec((1, width), lambda t, src: (0, 0)),
                pl.BlockSpec((total, 1), lambda t, src: (0, 0)),
            ],
            out_specs=pl.BlockSpec((capacity, PAGE, cols), lambda t, src: (0, 0, t)),
            scratch_shapes=[
                pltpu.VMEM((total, width), jnp.bfloat16),
                pltpu.VMEM((total, width), jnp.bfloat16),
                pltpu.SemaphoreType.DMA((capacity,)),
            ],
        ),
        out_shape=jax.ShapeDtypeStruct((capacity, PAGE, shards * cols), jnp.bfloat16),
        compiler_params=pltpu.CompilerParams(vmem_limit_bytes=60 << 20),
        cost_estimate=pl.CostEstimate(
            flops=2 * total * width * shards * cols,
            bytes_accessed=2 * (total * (width + shards * cols) + width * shards * cols),
            transcendentals=0,
        ),
        name="own_pages",
    )(
        source,
        hall.reshape(pages, PAGE, width),
        kv_weights,
        gain.reshape(1, width),
        shift.reshape(1, width),
        live.reshape(total, 1),
    )


def on_line(
    hidden_in, attn_gain, attn_shift, qkv_weight, qkv_bias, out_weight, out_bias, mlp_gain,
    mlp_shift, up_weight, up_bias, down_weight, down_bias, segment_ids, prompt_lengths, page_table,
):
    devices = lax.axis_size("tensor")
    columns = lax.axis_size("dp")
    position, column = lax.axis_index("tensor"), lax.axis_index("dp")
    width = hidden_in.shape[1]
    heads = qkv_weight.shape[1] // (3 * HD)

    out_rows = out_weight.shape[0] // columns
    out_share = lax.dynamic_slice_in_dim(out_weight, column * out_rows, out_rows, 0)
    kv_rows = width // columns
    share = lax.dynamic_slice_in_dim(qkv_weight, column * kv_rows, kv_rows, 0)
    share = jnp.concatenate(
        [share, jnp.broadcast_to(qkv_bias[None, :], (PAGE, qkv_bias.shape[0]))], axis=0
    )
    share = jnp.concatenate(
        [share[:, (3 * n + 1) * HD : (3 * n + 3) * HD] for n in range(heads)], axis=1
    )
    hall, projected, out_whole, kv_whole = gather_project(
        hidden_in, qkv_weight, out_share, share, qkv_bias, attn_gain, attn_shift, devices, columns
    )
    attended = attend(projected.reshape(-1, projected.shape[2]), segment_ids)
    layer_out = mlp_layer(
        attended, hall, out_whole, up_weight, down_weight, out_bias, mlp_gain, mlp_shift, up_bias,
        down_bias,
    )
    kv_pages = own_pages(
        hall, kv_whole, attn_gain, attn_shift, page_table, prompt_lengths, segment_ids.shape[1],
        position,
    )
    return (layer_out, kv_pages)


def on_device(
    hidden_in,
    attn_gain,
    attn_shift,
    qkv_weight,
    qkv_bias,
    out_weight,
    out_bias,
    mlp_gain,
    mlp_shift,
    up_weight,
    up_bias,
    down_weight,
    down_bias,
    segment_ids,
    prompt_lengths,
    page_table,
):
    devices = lax.axis_size("tensor")
    position = lax.axis_index("tensor")
    tok_rows, width = hidden_in.shape
    total_rows = tok_rows * devices
    streams, seq_len = segment_ids.shape
    whole_heads = qkv_weight.shape[1] % (3 * HD) == 0

    normed = normalize(hidden_in, attn_gain, attn_shift).astype(jnp.bfloat16)
    if not whole_heads:
        qkv_weight = join_pair(qkv_weight, 1, position)
        qkv_bias = join_pair(qkv_bias, 0, position)
    gathered = lax.all_gather(normed, "tensor", axis=0, tiled=True)
    projected = (
        jnp.dot(gathered, qkv_weight, preferred_element_type=jnp.float32)
        + qkv_bias.astype(jnp.float32)
    ).astype(jnp.bfloat16)
    heads_here = projected.shape[1] // (3 * HD)
    keys_vals = jnp.concatenate(
        [
            lax.slice_in_dim(projected, (3 * n + 1) * HD, (3 * n + 3) * HD, axis=1)
            for n in range(heads_here)
        ],
        axis=1,
    )
    if not whole_heads:
        half = keys_vals.shape[1] // 2
        keys_vals = lax.dynamic_slice_in_dim(keys_vals, position % 2 * half, half, 1)
    live = jnp.arange(seq_len, dtype=jnp.int32)[None, :] < prompt_lengths[:, None]
    pieces = pack_pages(
        keys_vals, live, page_table, 2 * (total_rows // PAGE) // devices, position
    )
    projected, pieces = lax.optimization_barrier((projected, pieces))
    received = send_pages(pieces)
    far, step = devices // 2, devices // 8
    attended = attend(projected, segment_ids)
    if not whole_heads:
        half = attended.shape[1] // 2
        attended = lax.dynamic_slice_in_dim(attended, position % 2 * half, half, 1)
    attended, received[far : far + step] = lax.optimization_barrier(
        (attended, received[far : far + step])
    )

    part = tok_rows // CHUNKS
    shaped = attended.reshape(devices, CHUNKS, part, attended.shape[1])
    sums = []
    for chunk in range(CHUNKS):
        rows = shaped[:, chunk].reshape(devices * part, -1)
        terms = jnp.dot(rows, out_weight, preferred_element_type=jnp.float32)
        sums.append(
            lax.psum_scatter(
                terms.astype(jnp.bfloat16), "tensor", scatter_dimension=0, tiled=True
            )
        )
    residuals, gathers = [], []
    for chunk in range(CHUNKS):
        hidden = lax.slice_in_dim(hidden_in, chunk * part, (chunk + 1) * part, axis=0)
        attn_sum = sums[chunk]
        if chunk == 0:
            attn_sum, received[far + step : far + 3 * step] = lax.optimization_barrier(
                (attn_sum, received[far + step : far + 3 * step])
            )
        else:
            attn_sum, residuals[-1], received, _ = lax.optimization_barrier(
                (attn_sum, residuals[-1], received, normed_mid)
            )
        residual_mid = (
            hidden.astype(jnp.float32) + attn_sum.astype(jnp.float32) + out_bias
        ).astype(jnp.bfloat16)
        normed_mid = normalize(residual_mid, mlp_gain, mlp_shift).astype(jnp.bfloat16)
        residuals.append(residual_mid)
        gathers.append(lax.all_gather(normed_mid, "tensor", axis=0, tiled=True))
    sums = []
    for chunk in range(CHUNKS):
        lifted = jnp.dot(gathers[chunk], up_weight, preferred_element_type=jnp.float32) + up_bias
        expanded = jax.nn.gelu(lifted, approximate=False).astype(jnp.bfloat16)
        expanded = lax.optimization_barrier(expanded)
        terms = jnp.dot(expanded, down_weight, preferred_element_type=jnp.float32)
        sums.append(
            lax.psum_scatter(
                terms.astype(jnp.bfloat16), "tensor", scatter_dimension=0, tiled=True
            )
        )
    kv_pages = lay_out_pages(received, position)
    outs = [
        (residual_mid.astype(jnp.float32) + mlp_sum.astype(jnp.float32) + down_bias).astype(
            jnp.bfloat16
        )
        for residual_mid, mlp_sum in zip(residuals, sums)
    ]
    layer_out = outs[0] if CHUNKS == 1 else jnp.concatenate(outs, axis=0)
    return (layer_out, kv_pages)


def solution(mesh):
    in_specs = (
        P(("dp", "tensor"), None),
        P(),
        P(),
        P(None, "tensor"),
        P("tensor"),
        P("tensor", None),
        P(),
        P(),
        P(),
        P(None, "tensor"),
        P("tensor"),
        P("tensor", None),
        P(),
        P("dp", None),
        P("dp"),
        P("dp", None),
    )
    out_specs = (P(("dp", "tensor"), None), P(("dp", "tensor"), None, None))
    body = on_line if (mesh.shape["dp"], mesh.shape["tensor"]) == SQUARE_LINE else on_device
    return jax.shard_map(
        body, mesh=mesh, in_specs=in_specs, out_specs=out_specs, check_vma=False
    )
```

```python
import functools
import math

import jax
import jax.numpy as jnp
from jax import lax
from jax.experimental import pallas as pl
from jax.experimental.pallas import tpu as pltpu
from jax.sharding import PartitionSpec as P

HD = 128
PAGE = 16
MAX_DOC = 1024
Q_BLOCK = 256
CHUNKS = 2


def normalize(values, norm_gain, norm_shift):
    widened = values.astype(jnp.float32)
    center = jnp.mean(widened, axis=-1, keepdims=True)
    spread = jnp.mean(jnp.square(widened - center), axis=-1, keepdims=True)
    return (widened - center) * lax.rsqrt(spread + 1e-05) * norm_gain + norm_shift


def attend_kernel(most, count_ref, proj_ref, kseg_ref, out_ref):
    stream, block = pl.program_id(0), pl.program_id(1)
    rows = out_ref.shape[0]
    heads = out_ref.shape[1] // HD
    count = count_ref[stream * pl.num_programs(1) + block]
    here = pl.ds(pl.multiple_of(block * rows, rows), rows)

    query_segments = jnp.transpose(jnp.broadcast_to(kseg_ref[0, :, here], (8, rows)))[:, :1]

    def over(blocks):
        window = blocks * rows
        start = pl.multiple_of((block - blocks + 1) * rows, rows)
        ahead = lax.broadcasted_iota(jnp.int32, (rows, window), 1) - lax.broadcasted_iota(
            jnp.int32, (rows, window), 0
        )
        allowed = (ahead <= window - rows) & (
            query_segments == kseg_ref[0, :, pl.ds(start, window)]
        )
        scores = [
            lax.dot_general(
                proj_ref[here, 3 * n * HD : (3 * n + 1) * HD],
                proj_ref[pl.ds(start, window), (3 * n + 1) * HD : (3 * n + 2) * HD],
                (((1,), (1,)), ((), ())),
                preferred_element_type=jnp.float32,
            )
            for n in range(heads)
        ]
        for n in range(heads):
            masked = jnp.where(allowed, scores[n] * (1.0 / math.sqrt(HD)), -1e30)
            expo = jnp.exp(masked - jnp.max(masked, axis=1, keepdims=True))
            weights = (expo * (1.0 / jnp.sum(expo, axis=1, keepdims=True))).astype(jnp.bfloat16)
            values = proj_ref[pl.ds(start, window), (3 * n + 2) * HD : (3 * n + 3) * HD]
            out_ref[:, n * HD : (n + 1) * HD] = jnp.dot(
                weights, values, preferred_element_type=jnp.float32
            ).astype(jnp.bfloat16)

    for blocks in range(1, most + 1):
        pl.when(count == blocks)(functools.partial(over, blocks))


def key_blocks(segment_ids):
    blocks = segment_ids.shape[1] // Q_BLOCK
    most = min(blocks, MAX_DOC // Q_BLOCK + 1)
    firsts = segment_ids[:, ::Q_BLOCK]
    begins = jnp.sum((segment_ids[:, None, :] < firsts[:, :, None]).astype(jnp.int32), axis=2)
    counts = jnp.arange(blocks, dtype=jnp.int32)[None, :] - begins // Q_BLOCK + 1
    return most, jnp.clip(counts, 1, most).reshape(-1)


def attend(projected, segment_ids):
    streams, seq_len = segment_ids.shape
    heads = projected.shape[1] // (3 * HD)
    blocks = seq_len // Q_BLOCK
    pairs = streams * heads * seq_len * 2 * Q_BLOCK
    most, counts = key_blocks(segment_ids)
    return pl.pallas_call(
        functools.partial(attend_kernel, most),
        grid_spec=pltpu.PrefetchScalarGridSpec(
            num_scalar_prefetch=1,
            grid=(streams, blocks),
            in_specs=[
                pl.BlockSpec((seq_len, 3 * heads * HD), lambda s, i, counts: (s, 0)),
                pl.BlockSpec((1, 1, seq_len), lambda s, i, counts: (s, 0, 0)),
            ],
            out_specs=pl.BlockSpec((Q_BLOCK, heads * HD), lambda s, i, counts: (s * blocks + i, 0)),
        ),
        out_shape=jax.ShapeDtypeStruct((streams * seq_len, heads * HD), jnp.bfloat16),
        compiler_params=pltpu.CompilerParams(vmem_limit_bytes=60 << 20),
        cost_estimate=pl.CostEstimate(
            flops=4 * pairs * HD,
            bytes_accessed=2 * projected.size * 2,
            transcendentals=pairs,
        ),
        name="attend",
    )(
        counts,
        projected,
        segment_ids.reshape(streams, 1, seq_len),
    )


def join_pair(value, axis, position):
    devices = lax.axis_size("tensor")
    other = lax.ppermute(value, "tensor", [(source, source ^ 1) for source in range(devices)])
    first = jnp.where(position % 2 == 0, value, other)
    second = jnp.where(position % 2 == 0, other, value)
    return jnp.concatenate([first, second], axis=axis)


def copy_page(index_ref, page_ref, out_ref):
    out_ref[...] = page_ref[...]


def take_pages(page_rows, index):
    block = (1,) + page_rows.shape[1:]
    return pl.pallas_call(
        copy_page,
        grid_spec=pltpu.PrefetchScalarGridSpec(
            num_scalar_prefetch=1,
            grid=(index.shape[0],),
            in_specs=[pl.BlockSpec(block, lambda i, index: (index[i], 0, 0))],
            out_specs=pl.BlockSpec(block, lambda i, index: (i, 0, 0)),
        ),
        out_shape=jax.ShapeDtypeStruct(index.shape + page_rows.shape[1:], page_rows.dtype),
    )(index, page_rows)


def pack_pages(keys_vals, live, page_table, capacity, position):
    devices = lax.axis_size("tensor")
    pages = keys_vals.shape[0] // PAGE
    owners = page_table[:, 0]
    numbers = jnp.arange(pages, dtype=jnp.int32)
    earlier = (owners[None, :] == owners[:, None]) & (numbers[None, :] < numbers[:, None])
    ranks = jnp.sum(earlier.astype(jnp.int32), axis=1)
    slot_ids = owners * capacity + ranks
    owner_order = position ^ jnp.arange(devices, dtype=jnp.int32)
    slots = owner_order[:, None] * capacity + jnp.arange(capacity, dtype=jnp.int32)[None, :]
    hits = slot_ids[None, :] == slots.reshape(-1)[:, None]
    source_page = jnp.sum(jnp.where(hits, numbers[None, :], 0), axis=1)
    live_pages = live.reshape(pages, PAGE).astype(jnp.int32)
    kept = jnp.sum(jnp.where(hits[:, :, None], live_pages[None], 0), axis=1) > 0
    page_rows = keys_vals.reshape(pages, PAGE, -1)
    taken = take_pages(page_rows, source_page)
    outgoing = jnp.where(kept[:, :, None], taken, 0).astype(jnp.bfloat16)
    return [
        lax.slice_in_dim(outgoing, apart * capacity, (apart + 1) * capacity, axis=0)
        for apart in range(devices)
    ]


def send_pages(pieces):
    devices = len(pieces)
    received = [pieces[0]]
    for apart in range(1, devices):
        hops = [(source, source ^ apart) for source in range(devices)]
        received.append(lax.ppermute(pieces[apart], "tensor", hops))
    return received


def lay_out_pages(received, position):
    devices = len(received)
    slots, page, width = received[0].shape
    laid = jnp.zeros((slots, page, devices * width), received[0].dtype)
    for apart in range(devices):
        laid = lax.dynamic_update_slice_in_dim(
            laid, received[apart], (position ^ apart) * width, axis=2
        )
    return laid


MESH = pl.DeviceIdType.MESH
SQUARE_LINE = (4, 8)
CHUNK = 32
TILE = 1024


def layer_norm(values, gain, shift):
    widened = values.astype(jnp.float32)
    center = jnp.mean(widened, axis=-1, keepdims=True)
    moved = widened - center
    spread = jnp.mean(moved * moved, axis=-1, keepdims=True)
    return moved * lax.rsqrt(spread + 1e-05) * gain + shift


def norm_rows(load, out, rows, gain_ref, shift_ref):
    @pl.loop(0, rows // 16, unroll=4)
    def _(i):
        part = pl.ds(pl.multiple_of(i * 16, 16), 16)
        out[part, :] = layer_norm(load(part), gain_ref[...], shift_ref[...]).astype(jnp.bfloat16)


def greet(me, chips, across=()):
    z, c = me // 2, lax.rem(me, 2)
    barrier = pltpu.get_barrier_semaphore()
    pl.semaphore_signal(barrier, inc=1, device_id={"tensor": 2 * z + 1 - c}, device_id_type=MESH)
    for column in across:
        pl.semaphore_signal(barrier, inc=1, device_id={"dp": column}, device_id_type=MESH)

    @pl.when(z > 0)
    def _():
        pl.semaphore_signal(barrier, inc=1, device_id={"tensor": me - 2}, device_id_type=MESH)

    @pl.when(z < chips - 1)
    def _():
        pl.semaphore_signal(barrier, inc=1, device_id={"tensor": me + 2}, device_id_type=MESH)

    peers = 1 + len(across) + (z > 0).astype(jnp.int32) + (z < chips - 1).astype(jnp.int32)
    pl.semaphore_wait(barrier, peers)


def gather_project_kernel(
    chips, hid, w_hbm, outw_hbm, kshare, b_ref, gain_ref, shift_ref, hall_out, proj_out, oall, kall,
    buf, w_ref, nrm, pbuf, ssem, rsem, lsem, psem, wsem, share_s, share_r,
):
    me, p = lax.axis_index("tensor"), lax.axis_index("dp")
    z, c = me // 2, lax.rem(me, 2)
    twin = 2 * z + 1 - c
    beside, over, corner = p + 1 - 2 * lax.rem(p, 2), lax.rem(p + 2, 4), 3 - p
    rows, width = hid.shape
    cols = w_ref.shape[1]
    out_rows = oall.shape[2]
    oshare = outw_hbm.at[pl.ds(pl.multiple_of(p * out_rows, out_rows), out_rows)]
    pair, own_share = (oall, kall), (oshare, kshare)
    load = pltpu.make_async_copy(w_hbm, w_ref, wsem.at[0])
    own = pltpu.make_async_copy(hid, buf.at[me], wsem.at[1])
    own_shares = [
        pltpu.make_async_copy(oshare, oall.at[p, me], wsem.at[2]),
        pltpu.make_async_copy(kshare, kall.at[p, me], wsem.at[3]),
    ]
    for copy in own_shares:
        copy.start()
    own.start()
    load.start()
    greet(me, chips, (beside, over))

    def share_copy(a, q, slot, way, own_from=False):
        device = [
            {"tensor": me - 2}, {"tensor": me + 2}, {"tensor": twin}, {"dp": beside}, {"dp": over},
        ][way]
        source = own_share[a] if own_from else pair[a].at[q, slot]
        return pltpu.make_async_remote_copy(
            src_ref=source, dst_ref=pair[a].at[q, slot],
            send_sem=share_s.at[a, q, slot, way], recv_sem=share_r.at[a, q, slot],
            device_id=device, device_id_type=MESH,
        )

    def share_send(q, slot, *ways):
        for a in range(2):
            for way in ways:
                share_copy(a, q, slot, way).start()

    def own_share_send(*ways):
        for a in range(2):
            for way in ways:
                share_copy(a, p, me, way, True).start()

    def share_arrived(q, slot):
        for a in range(2):
            share_copy(a, q, slot, 2).wait_recv()

    def share_line(hop):
        @pl.when(z - hop >= 0)
        def _():
            slot = me - 2 * hop
            share_arrived(p, slot)

            @pl.when(z < chips - 1)
            def _():
                share_send(p, slot, 1)

            share_send(p, slot, 3, 4, 2)

        @pl.when(z + hop < chips)
        def _():
            slot = me + 2 * hop
            share_arrived(p, slot)

            @pl.when(z > 0)
            def _():
                share_send(p, slot, 0)

            share_send(p, slot, 3, 4, 2)

    def at_slots(hop, run):
        if hop == 0:
            run(me)
        else:
            pl.when(z - hop >= 0)(lambda: run(me - 2 * hop))
            pl.when(z + hop < chips)(lambda: run(me + 2 * hop))

    def share_across(slot):
        share_arrived(over, slot)
        pl.when(c == 0)(lambda: share_send(over, slot, 3))
        share_arrived(beside, slot)
        pl.when(c == 1)(lambda: share_send(beside, slot, 4))
        share_send(over, slot, 2)
        share_send(beside, slot, 2)

    def share_corner(slot):
        share_arrived(corner, slot)
        share_send(corner, slot, 2)

    def send(slot, device, way):
        pltpu.make_async_remote_copy(
            src_ref=buf.at[slot], dst_ref=buf.at[slot], send_sem=ssem.at[slot, way],
            recv_sem=rsem.at[slot], device_id={"tensor": device}, device_id_type=MESH,
        ).start()

    def sent(slot, way):
        pltpu.make_async_remote_copy(
            src_ref=buf.at[slot], dst_ref=buf.at[slot], send_sem=ssem.at[slot, way],
            recv_sem=rsem.at[slot], device_id={"tensor": twin}, device_id_type=MESH,
        ).wait_send()

    def arrived(slot):
        pltpu.make_async_copy(hid, buf.at[slot], rsem.at[slot]).wait()

    def compute(slot):
        pltpu.make_async_copy(buf.at[slot], hall_out.at[slot], lsem.at[slot]).start()

        norm_rows(lambda part: buf[slot, part, :], nrm, rows, gain_ref, shift_ref)

        pbuf[slot] = (
            jnp.dot(nrm[...], w_ref[...], preferred_element_type=jnp.float32)
            + b_ref[...].astype(jnp.float32)
        ).astype(jnp.bfloat16)

        pltpu.make_async_copy(pbuf.at[slot], proj_out.at[slot], psem.at[slot]).start()

    def token_line(hop):
        @pl.when(z - hop >= 0)
        def _():
            slot = me - 2 * hop
            arrived(slot)

            @pl.when(z < chips - 1)
            def _():
                send(slot, me + 2, 1)

            send(slot, twin, 2)

        @pl.when(z + hop < chips)
        def _():
            slot = me + 2 * hop
            arrived(slot)

            @pl.when(z > 0)
            def _():
                send(slot, me - 2, 0)

            send(slot, twin, 2)

    def token_compute(hop):
        @pl.when(z - hop >= 0)
        def _():
            compute(me - 2 * hop)
            arrived(twin - 2 * hop)
            compute(twin - 2 * hop)

        @pl.when(z + hop < chips)
        def _():
            compute(me + 2 * hop)
            arrived(twin + 2 * hop)
            compute(twin + 2 * hop)

    pl.when(z > 0)(lambda: own_share_send(0))
    pl.when(z < chips - 1)(lambda: own_share_send(1))
    own_share_send(3, 4, 2)
    own.wait()
    load.wait()
    compute(me)
    for hop in range(1, chips - 1):
        share_line(hop)
        if hop == 1:
            at_slots(0, share_across)
    pl.when(z > 0)(lambda: send(me, me - 2, 0))
    pl.when(z < chips - 1)(lambda: send(me, me + 2, 1))
    send(me, twin, 2)
    share_line(chips - 1)
    arrived(twin)
    compute(twin)
    for hop in range(1, chips):
        at_slots(hop, share_across)
        at_slots(hop - 1, share_corner)
        token_line(hop)
        token_compute(hop)
    at_slots(chips - 1, share_corner)

    for copy in own_shares:
        copy.wait()
    for slot in range(2 * chips):
        pltpu.make_async_copy(buf.at[slot], hall_out.at[slot], lsem.at[slot]).wait()
        pltpu.make_async_copy(pbuf.at[slot], proj_out.at[slot], psem.at[slot]).wait()
    for origin in range(chips):
        slot = 2 * origin + c
        sent(slot, 2)
        for q in (beside, over, corner):
            share_arrived(q, 2 * origin + 1 - c)

        share_arrived(p, 2 * origin + 1 - c)

        @pl.when((origin >= z) & (z > 0))
        def _():
            sent(slot, 0)
            for a in range(2):
                share_copy(a, p, slot, 0).wait_send()

        @pl.when((origin <= z) & (z < chips - 1))
        def _():
            sent(slot, 1)
            for a in range(2):
                share_copy(a, p, slot, 1).wait_send()

        for a in range(2):
            for q in (p, beside, over, corner):
                share_copy(a, q, slot, 2).wait_send()
            share_copy(a, p, slot, 3).wait_send()
            share_copy(a, p, slot, 4).wait_send()

            @pl.when(c == 0)
            def _():
                share_copy(a, over, slot, 3).wait_send()

            @pl.when(c == 1)
            def _():
                share_copy(a, beside, slot, 4).wait_send()


def gather_project(
    hidden_in, qkv_weight, out_weight, kv_share, qkv_bias, gain, shift, devices, columns
):
    rows, width = hidden_in.shape
    cols = qkv_weight.shape[1]
    hbm, vmem = pl.BlockSpec(memory_space=pl.ANY), pl.BlockSpec(memory_space=pltpu.VMEM)
    total = rows * devices
    dma = pltpu.SemaphoreType.DMA
    return pl.pallas_call(
        functools.partial(gather_project_kernel, devices // 2),
        in_specs=[hbm] * 4 + [vmem] * 3,
        out_specs=[hbm] * 4,
        out_shape=[
            jax.ShapeDtypeStruct((devices, rows, width), jnp.bfloat16),
            jax.ShapeDtypeStruct((devices, rows, cols), jnp.bfloat16),
            jax.ShapeDtypeStruct(
                (columns, devices, out_weight.shape[0] // columns, width), jnp.bfloat16
            ),
            jax.ShapeDtypeStruct((columns, devices) + kv_share.shape, jnp.bfloat16),
        ],
        scratch_shapes=[
            pltpu.VMEM((devices, rows, width), jnp.bfloat16),
            pltpu.VMEM((width, cols), jnp.bfloat16),
            pltpu.VMEM((rows, width), jnp.bfloat16),
            pltpu.VMEM((devices, rows, cols), jnp.bfloat16),
            dma((devices, 3)),
            dma((devices,)),
            dma((devices,)),
            dma((devices,)),
            dma((4,)),
            dma((2, columns, devices, 5)),
            dma((2, columns, devices)),
        ],
        compiler_params=pltpu.CompilerParams(
            collective_id=0, has_side_effects=True, vmem_limit_bytes=60 << 20
        ),
        cost_estimate=pl.CostEstimate(
            flops=2 * total * width * cols,
            bytes_accessed=2 * (total * (width + cols) + width * cols),
            transcendentals=0,
        ),
        name="gather_project",
    )(
        hidden_in, qkv_weight, out_weight, kv_share, qkv_bias.reshape(1, cols),
        gain.reshape(1, width), shift.reshape(1, width),
    )


def mlp_kernel(
    chips, att, hall, outw_hbm, upw_hbm, dnw_hbm, pages, kvw_hbm, outb_ref, gain_ref, shift_ref,
    upb_ref, dnb_ref, live_ref,
    out_ref, kv_out,
    ag, outw, upw, dnw, hbuf, res, nrm, exp_, own_res, par, tw, lin, rin,
    pbuf, kvw, kvo, wsem, osem, hsem, ag_s, ag_r, tw_s, tw_r, rs_s, rs_r, psem,
):
    me = lax.axis_index("tensor")
    z, c = me // 2, lax.rem(me, 2)
    twin = 2 * z + 1 - c
    devices = 2 * chips
    chunks = ag.shape[0]
    width = outw.shape[1]
    piece = att.shape[-1]
    hidden_units = upw.shape[1]
    rows = devices * CHUNK

    columns, _, out_rows, _ = outw_hbm.shape
    loads = [
        pltpu.make_async_copy(
            outw_hbm.at[p, d], outw.at[pl.ds((d * columns + p) * out_rows, out_rows)], wsem.at[2 + d * columns + p]
        )
        for d in range(devices)
        for p in range(columns)
    ] + [
        pltpu.make_async_copy(upw_hbm, upw, wsem.at[0]),
        pltpu.make_async_copy(dnw_hbm, dnw, wsem.at[1]),
    ]

    def place(k, device):
        return ag.at[k, :, :, pl.ds(pl.multiple_of(device * piece, piece), piece)]

    def own_piece(k):
        part = pl.ds(pl.multiple_of(k * CHUNK, CHUNK), CHUNK)
        return pltpu.make_async_copy(att.at[:, part, :], place(k, me), osem.at[k])

    def hidden_part(k):
        part = pl.ds(pl.multiple_of(k * CHUNK, CHUNK), CHUNK)
        return pltpu.make_async_copy(hall.at[:, part, :], hbuf.at[lax.rem(k, 2)], hsem.at[lax.rem(k, 2)])

    @pl.loop(0, chunks)
    def _(k):
        own_piece(k).start()

    page_load = pltpu.make_async_copy(pages, pbuf, psem.at[4])
    page_load.start()

    def weight_load(t):
        return pltpu.make_async_copy(kvw_hbm.at[:, t], kvw.at[lax.rem(t, 2)], psem.at[lax.rem(t, 2)])

    def page_store(t):
        part = pl.ds(pl.multiple_of(t * kvo.shape[3], kvo.shape[3]), kvo.shape[3])
        return pltpu.make_async_copy(
            kvo.at[lax.rem(t, 2)], kv_out.at[:, :, part], psem.at[2 + lax.rem(t, 2)]
        )

    for t in range(2):
        weight_load(t).start()
    for load in loads:
        load.start()
    greet(me, chips)

    def page_step(t):
        slot = lax.rem(t, 2)
        depth = pbuf.shape[1] // columns
        pl.when(t == 0)(page_load.wait)
        weight_load(t).wait()
        pl.when(t >= 2)(lambda: page_store(t - 2).wait())
        sums = jnp.dot(
            pbuf[...],
            kvw[slot, :, :depth, :].reshape(pbuf.shape[1], kvw.shape[3]),
            preferred_element_type=jnp.float32,
        )
        bias = kvw[slot, 0, depth : depth + 1, :].astype(jnp.float32)
        made = jnp.where(live_ref[...] > 0, sums + bias, 0.0).astype(jnp.bfloat16)
        kvo[slot] = made.reshape(kvo.shape[1:])
        page_store(t).start()
        pl.when(t + 2 < devices)(lambda: weight_load(t + 2).start())

    drain = chunks + chips - 1
    turns = ((0, 1), (1, 1), (2, 2), (drain, 2), (drain + 1, 1), (drain + 2, 1))

    def pages_before(s):
        return sum(number * (s > at).astype(jnp.int32) for at, number in turns)

    def piece_copy(k, origin, device, way):
        return pltpu.make_async_remote_copy(
            src_ref=place(k, origin), dst_ref=place(k, origin), send_sem=ag_s.at[k, origin, way],
            recv_sem=ag_r.at[k, origin], device_id={"tensor": device}, device_id_type=MESH,
        )

    def piece_wait(k, origin):
        piece_copy(k, origin, twin, 2).wait_recv()

    def twin_copy(k, half):
        part = pl.ds(half * (width // 2), width // 2)
        return pltpu.make_async_remote_copy(
            src_ref=par.at[k, :, 1 - c, :, part], dst_ref=tw.at[k, :, :, part],
            send_sem=tw_s.at[k, half], recv_sem=tw_r.at[k, half],
            device_id={"tensor": twin}, device_id_type=MESH,
        )

    def right_copy(k, chip):
        return pltpu.make_async_remote_copy(
            src_ref=par.at[k, chip, c], dst_ref=lin.at[k, chip - 1],
            send_sem=rs_s.at[k, 0, chip], recv_sem=rs_r.at[k, 0, chip],
            device_id={"tensor": me + 2}, device_id_type=MESH,
        )

    def left_copy(k, chip):
        return pltpu.make_async_remote_copy(
            src_ref=par.at[k, chip, c], dst_ref=rin.at[k, chip],
            send_sem=rs_s.at[k, 1, chip], recv_sem=rs_r.at[k, 1, chip],
            device_id={"tensor": me - 2}, device_id_type=MESH,
        )

    def add_to(k, chip, more):
        par[k, chip, c] = (par[k, chip, c].astype(jnp.float32) + more.astype(jnp.float32)).astype(
            jnp.bfloat16
        )

    def at_chunk(k, run):
        pl.when((k >= 0) & (k < chunks))(lambda: run(k))

    def first_hop(k):
        own_piece(k).wait()

        @pl.when(z > 0)
        def _():
            piece_copy(k, me, me - 2, 0).start()

        @pl.when(z < chips - 1)
        def _():
            piece_copy(k, me, me + 2, 1).start()

        piece_copy(k, me, twin, 2).start()

    def later_hop(hop, k):
        @pl.when(z - hop >= 0)
        def _():
            origin = me - 2 * hop
            piece_wait(k, origin)

            @pl.when(z < chips - 1)
            def _():
                piece_copy(k, origin, me + 2, 1).start()

            piece_copy(k, origin, twin, 2).start()

        @pl.when(z + hop < chips)
        def _():
            origin = me + 2 * hop
            piece_wait(k, origin)

            @pl.when(z > 0)
            def _():
                piece_copy(k, origin, me - 2, 0).start()

            piece_copy(k, origin, twin, 2).start()

    def join_twins(k):
        for half in range(2):
            twin_copy(k, half).wait_recv()

        @pl.when(z < chips // 2)
        def _():
            for chip in reversed(range(chips)):
                add_to(k, chip, tw[k, chip])
                if chip > 0:
                    pl.when(z == 0)(lambda: right_copy(k, chip).start())

        @pl.when(z >= chips // 2)
        def _():
            for chip in range(chips):
                add_to(k, chip, tw[k, chip])
                if chip < chips - 1:
                    pl.when(z == chips - 1)(lambda: left_copy(k, chip).start())

    def add_left(k, at):
        for chip in reversed(range(at, chips)):
            right_copy(k, chip).wait_recv()
            add_to(k, chip, lin[k, chip - 1])
            if chip > at:
                right_copy(k, chip).start()

    def add_right(k, at):
        for chip in range(at + 1):
            left_copy(k, chip).wait_recv()
            add_to(k, chip, rin[k, chip])
            if chip < at:
                left_copy(k, chip).start()

    def pass_on(hop, k):
        for at in range(1, chips):
            if at == hop:

                @pl.when(z == at)
                def _():
                    add_left(k, at)

                @pl.when(z == chips - 1 - at)
                def _():
                    add_right(k, chips - 1 - at)

    def finish(k):
        part = pl.ds(pl.multiple_of(k * CHUNK, CHUNK), CHUNK)
        out_ref[part, :] = (
            own_res[part, :].astype(jnp.float32) + par[k, z, c].astype(jnp.float32) + dnb_ref[...]
        ).astype(jnp.bfloat16)

    def compute(k):
        for hop in range(1, chips):

            @pl.when(z - hop >= 0)
            def _():
                piece_wait(k, twin - 2 * hop)

            @pl.when(z + hop < chips)
            def _():
                piece_wait(k, twin + 2 * hop)

        piece_wait(k, twin)
        hidden_part(k).wait()
        slot = lax.rem(k, 2)

        @pl.when(k + 1 < chunks)
        def _():
            hidden_part(k + 1).start()

        @pl.when(k == 0)
        def _():
            for load in loads:
                load.wait()

        @pl.loop(0, width // TILE)
        def _(i):
            part = pl.ds(pl.multiple_of(i * TILE, TILE), TILE)
            terms = jnp.dot(
                ag[k].reshape(rows, width), outw[:, part], preferred_element_type=jnp.float32
            )
            res[:, part] = (
                hbuf[slot, :, :, part].reshape(rows, TILE).astype(jnp.float32)
                + terms
                + outb_ref[:, part]
            ).astype(jnp.bfloat16)

        norm_rows(lambda part: res[part, :], nrm, rows, gain_ref, shift_ref)
        own_res[pl.ds(pl.multiple_of(k * CHUNK, CHUNK), CHUNK), :] = res[
            pl.ds(pl.multiple_of(me * CHUNK, CHUNK), CHUNK), :
        ]

        for i in range(hidden_units // 256):
            part = slice(i * 256, (i + 1) * 256)
            lifted = (
                jnp.dot(nrm[...], upw[:, part], preferred_element_type=jnp.float32) + upb_ref[:, part]
            )
            exp_[:, part] = (0.5 * lifted * (1.0 + lax.erf(lifted * math.sqrt(0.5)))).astype(
                jnp.bfloat16
            )

        for half in range(2):
            part = slice(half * (width // 2), (half + 1) * (width // 2))
            par[k, :, :, :, part] = (
                jnp.dot(exp_[...], dnw[:, part], preferred_element_type=jnp.float32)
                .astype(jnp.bfloat16)
                .reshape(chips, 2, CHUNK, width // 2)
            )
            twin_copy(k, half).start()

    hidden_part(0).start()

    @pl.loop(0, chunks + 2 * chips - 2)
    def _(s):
        for hop in reversed(range(1, chips)):
            at_chunk(s - hop, functools.partial(later_hop, hop))
        at_chunk(s, first_hop)
        lax.fori_loop(pages_before(s), pages_before(s + 1), lambda t, _: page_step(t), None)
        at_chunk(s - chips + 1, compute)
        at_chunk(s - chips + 1, join_twins)
        for hop in reversed(range(1, chips)):
            at_chunk(s - chips + 1 - hop, functools.partial(pass_on, hop))
        at_chunk(s - 2 * chips + 2, finish)

    for t in range(devices - 2, devices):
        page_store(t).wait()

    @pl.loop(0, chunks)
    def _(k):
        for origin in range(chips):
            slot = 2 * origin + c
            piece_copy(k, slot, twin, 2).wait_send()

            @pl.when((origin >= z) & (z > 0))
            def _():
                piece_copy(k, slot, twin, 0).wait_send()

            @pl.when((origin <= z) & (z < chips - 1))
            def _():
                piece_copy(k, slot, twin, 1).wait_send()

        for half in range(2):
            twin_copy(k, half).wait_send()
        for chip in range(chips):
            pl.when(z < chip)(lambda: right_copy(k, chip).wait_send())
            pl.when(z > chip)(lambda: left_copy(k, chip).wait_send())


def mlp_layer(
    attended, hall, out_weight, up_weight, down_weight, pages, kv_weights, out_bias, gain, shift,
    up_bias, down_bias, live,
):
    devices, tok_rows, width = hall.shape
    chips, chunks = devices // 2, tok_rows // CHUNK
    piece, units = attended.shape[1], up_weight.shape[1]
    total = devices * tok_rows
    kept, kv_cols = pages.shape[0], kv_weights.shape[3]
    hbm, vmem = pl.BlockSpec(memory_space=pl.ANY), pl.BlockSpec(memory_space=pltpu.VMEM)
    dma = pltpu.SemaphoreType.DMA
    bf16 = jnp.bfloat16
    return pl.pallas_call(
        functools.partial(mlp_kernel, chips),
        in_specs=[hbm] * 7 + [vmem] * 6,
        out_specs=[vmem, hbm],
        out_shape=[
            jax.ShapeDtypeStruct((tok_rows, width), bf16),
            jax.ShapeDtypeStruct((kept // PAGE, PAGE, devices * kv_cols), bf16),
        ],
        scratch_shapes=[
            pltpu.VMEM((chunks, devices, CHUNK, width), bf16),
            pltpu.VMEM((width, width), bf16),
            pltpu.VMEM((width, units), bf16),
            pltpu.VMEM((units, width), bf16),
            pltpu.VMEM((2, devices, CHUNK, width), bf16),
            pltpu.VMEM((devices * CHUNK, width), bf16),
            pltpu.VMEM((devices * CHUNK, width), bf16),
            pltpu.VMEM((devices * CHUNK, units), bf16),
            pltpu.VMEM((tok_rows, width), bf16),
            pltpu.VMEM((chunks, chips, 2, CHUNK, width), bf16),
            pltpu.VMEM((chunks, chips, CHUNK, width), bf16),
            pltpu.VMEM((chunks, chips - 1, CHUNK, width), bf16),
            pltpu.VMEM((chunks, chips - 1, CHUNK, width), bf16),
            pltpu.VMEM(pages.shape, bf16),
            pltpu.VMEM((2,) + kv_weights.shape[:1] + kv_weights.shape[2:], bf16),
            pltpu.VMEM((2, kept // PAGE, PAGE, kv_cols), bf16),
            dma((2 + devices * out_weight.shape[0],)),
            dma((chunks,)),
            dma((2,)),
            dma((chunks, devices, 3)),
            dma((chunks, devices)),
            dma((chunks, 2)),
            dma((chunks, 2)),
            dma((chunks, 2, chips)),
            dma((chunks, 2, chips)),
            dma((5,)),
        ],
        compiler_params=pltpu.CompilerParams(
            collective_id=1, has_side_effects=True, vmem_limit_bytes=60 << 20
        ),
        cost_estimate=pl.CostEstimate(
            flops=2 * total * width * (width + 2 * units),
            bytes_accessed=2 * (2 * total * width + width * (width + 2 * units)),
            transcendentals=total * units,
        ),
        name="mlp_layer",
    )(
        attended.reshape(devices, tok_rows, piece),
        hall,
        out_weight,
        up_weight,
        down_weight,
        pages,
        kv_weights,
        out_bias.reshape(1, width),
        gain.reshape(1, width),
        shift.reshape(1, width),
        up_bias.reshape(1, units),
        down_bias.reshape(1, width),
        live,
    )


def attend_pages_kernel(
    most, count_ref, src_ref, proj_ref, kseg_ref, hall, gain_ref, shift_ref, out_ref, rows_ref,
    raw, sem,
):
    block = pl.program_id(1)
    slots = raw.shape[0] // PAGE
    copies = [
        pltpu.make_async_copy(hall.at[src_ref[i]], raw.at[pl.ds(i * PAGE, PAGE)], sem.at[i])
        for i in range(slots)
    ]

    @pl.when(block == 0)
    def _():
        for copy in copies:
            copy.start()

    attend_kernel(most, count_ref, proj_ref, kseg_ref, out_ref)

    @pl.when(block == pl.num_programs(1) - 1)
    def _():
        for copy in copies:
            copy.wait()
        norm_rows(lambda part: raw[part, :], rows_ref, slots * PAGE, gain_ref, shift_ref)


def attend_pages(projected, segment_ids, source, hall, gain, shift):
    streams, seq_len = segment_ids.shape
    heads = projected.shape[1] // (3 * HD)
    blocks = seq_len // Q_BLOCK
    width, total = hall.shape[2], source.shape[0] * PAGE
    most, counts = key_blocks(segment_ids)
    pairs = streams * heads * seq_len * 2 * Q_BLOCK
    whole = pl.BlockSpec((1, width), lambda s, i, counts, source: (0, 0))
    return pl.pallas_call(
        functools.partial(attend_pages_kernel, most),
        grid_spec=pltpu.PrefetchScalarGridSpec(
            num_scalar_prefetch=2,
            grid=(streams, blocks),
            in_specs=[
                pl.BlockSpec((seq_len, 3 * heads * HD), lambda s, i, counts, source: (s, 0)),
                pl.BlockSpec((1, 1, seq_len), lambda s, i, counts, source: (s, 0, 0)),
                pl.BlockSpec(memory_space=pl.ANY),
                whole,
                whole,
            ],
            out_specs=[
                pl.BlockSpec((Q_BLOCK, heads * HD), lambda s, i, counts, source: (s * blocks + i, 0)),
                pl.BlockSpec((total, width), lambda s, i, counts, source: (0, 0)),
            ],
            scratch_shapes=[
                pltpu.VMEM((total, width), jnp.bfloat16),
                pltpu.SemaphoreType.DMA((source.shape[0],)),
            ],
        ),
        out_shape=[
            jax.ShapeDtypeStruct((streams * seq_len, heads * HD), jnp.bfloat16),
            jax.ShapeDtypeStruct((total, width), jnp.bfloat16),
        ],
        compiler_params=pltpu.CompilerParams(vmem_limit_bytes=60 << 20),
        cost_estimate=pl.CostEstimate(
            flops=4 * pairs * HD,
            bytes_accessed=2 * projected.size * 2,
            transcendentals=pairs,
        ),
        name="attend",
    )(
        counts,
        source,
        projected,
        segment_ids.reshape(streams, 1, seq_len),
        hall.reshape(-1, PAGE, width),
        gain.reshape(1, width),
        shift.reshape(1, width),
    )


def own_pages(devices, page_table, prompt_lengths, seq_len, position):
    pages = page_table.shape[0]
    capacity = 2 * pages // devices
    owners = page_table[:, 0]
    numbers = jnp.arange(pages, dtype=jnp.int32)
    earlier = (owners[None, :] == owners[:, None]) & (numbers[None, :] < numbers[:, None])
    ranks = jnp.sum(earlier.astype(jnp.int32), axis=1)
    slots = jnp.arange(capacity, dtype=jnp.int32)
    hits = (owners[None, :] == position) & (ranks[None, :] == slots[:, None])
    source = jnp.sum(jnp.where(hits, numbers[None, :], 0), axis=1)
    taken = jnp.sum(hits.astype(jnp.int32), axis=1) > 0
    tokens = source[:, None] * PAGE + jnp.arange(PAGE, dtype=jnp.int32)[None, :]
    stream = tokens // seq_len
    limits = jnp.sum(
        jnp.where(
            stream[:, :, None] == jnp.arange(prompt_lengths.shape[0], dtype=jnp.int32),
            prompt_lengths, 0,
        ),
        axis=2,
    )
    live = (taken[:, None] & (tokens - stream * seq_len < limits)).astype(jnp.int32)
    return source, live.reshape(capacity * PAGE, 1)


def on_line(
    hidden_in, attn_gain, attn_shift, qkv_weight, qkv_bias, out_weight, out_bias, mlp_gain,
    mlp_shift, up_weight, up_bias, down_weight, down_bias, segment_ids, prompt_lengths, page_table,
):
    devices = lax.axis_size("tensor")
    columns = lax.axis_size("dp")
    position, column = lax.axis_index("tensor"), lax.axis_index("dp")
    width = hidden_in.shape[1]
    heads = qkv_weight.shape[1] // (3 * HD)

    kv_rows = width // columns
    share = lax.dynamic_slice_in_dim(qkv_weight, column * kv_rows, kv_rows, 0)
    share = jnp.concatenate(
        [share, jnp.broadcast_to(qkv_bias[None, :], (PAGE, qkv_bias.shape[0]))], axis=0
    )
    share = jnp.concatenate(
        [share[:, (3 * n + 1) * HD : (3 * n + 3) * HD] for n in range(heads)], axis=1
    )
    hall, projected, out_whole, kv_whole = gather_project(
        hidden_in, qkv_weight, out_weight, share, qkv_bias, attn_gain, attn_shift, devices, columns
    )
    source, live = own_pages(devices, page_table, prompt_lengths, segment_ids.shape[1], position)
    attended, pages = attend_pages(
        projected.reshape(-1, projected.shape[2]), segment_ids, source, hall, attn_gain, attn_shift
    )
    layer_out, kv_pages = mlp_layer(
        attended, hall, out_whole, up_weight, down_weight, pages, kv_whole, out_bias, mlp_gain,
        mlp_shift, up_bias, down_bias, live,
    )
    return (layer_out, kv_pages)


def on_device(
    hidden_in,
    attn_gain,
    attn_shift,
    qkv_weight,
    qkv_bias,
    out_weight,
    out_bias,
    mlp_gain,
    mlp_shift,
    up_weight,
    up_bias,
    down_weight,
    down_bias,
    segment_ids,
    prompt_lengths,
    page_table,
):
    devices = lax.axis_size("tensor")
    position = lax.axis_index("tensor")
    tok_rows, width = hidden_in.shape
    total_rows = tok_rows * devices
    streams, seq_len = segment_ids.shape
    whole_heads = qkv_weight.shape[1] % (3 * HD) == 0

    normed = normalize(hidden_in, attn_gain, attn_shift).astype(jnp.bfloat16)
    if not whole_heads:
        qkv_weight = join_pair(qkv_weight, 1, position)
        qkv_bias = join_pair(qkv_bias, 0, position)
    gathered = lax.all_gather(normed, "tensor", axis=0, tiled=True)
    projected = (
        jnp.dot(gathered, qkv_weight, preferred_element_type=jnp.float32)
        + qkv_bias.astype(jnp.float32)
    ).astype(jnp.bfloat16)
    heads_here = projected.shape[1] // (3 * HD)
    keys_vals = jnp.concatenate(
        [
            lax.slice_in_dim(projected, (3 * n + 1) * HD, (3 * n + 3) * HD, axis=1)
            for n in range(heads_here)
        ],
        axis=1,
    )
    if not whole_heads:
        half = keys_vals.shape[1] // 2
        keys_vals = lax.dynamic_slice_in_dim(keys_vals, position % 2 * half, half, 1)
    live = jnp.arange(seq_len, dtype=jnp.int32)[None, :] < prompt_lengths[:, None]
    pieces = pack_pages(
        keys_vals, live, page_table, 2 * (total_rows // PAGE) // devices, position
    )
    projected, pieces = lax.optimization_barrier((projected, pieces))
    received = send_pages(pieces)
    far, step = devices // 2, devices // 8
    attended = attend(projected, segment_ids)
    if not whole_heads:
        half = attended.shape[1] // 2
        attended = lax.dynamic_slice_in_dim(attended, position % 2 * half, half, 1)
    attended, received[far : far + step] = lax.optimization_barrier(
        (attended, received[far : far + step])
    )

    part = tok_rows // CHUNKS
    shaped = attended.reshape(devices, CHUNKS, part, attended.shape[1])
    sums = []
    for chunk in range(CHUNKS):
        rows = shaped[:, chunk].reshape(devices * part, -1)
        terms = jnp.dot(rows, out_weight, preferred_element_type=jnp.float32)
        sums.append(
            lax.psum_scatter(
                terms.astype(jnp.bfloat16), "tensor", scatter_dimension=0, tiled=True
            )
        )
    residuals, gathers = [], []
    for chunk in range(CHUNKS):
        hidden = lax.slice_in_dim(hidden_in, chunk * part, (chunk + 1) * part, axis=0)
        attn_sum = sums[chunk]
        if chunk == 0:
            attn_sum, received[far + step : far + 3 * step] = lax.optimization_barrier(
                (attn_sum, received[far + step : far + 3 * step])
            )
        else:
            attn_sum, residuals[-1], received, _ = lax.optimization_barrier(
                (attn_sum, residuals[-1], received, normed_mid)
            )
        residual_mid = (
            hidden.astype(jnp.float32) + attn_sum.astype(jnp.float32) + out_bias
        ).astype(jnp.bfloat16)
        normed_mid = normalize(residual_mid, mlp_gain, mlp_shift).astype(jnp.bfloat16)
        residuals.append(residual_mid)
        gathers.append(lax.all_gather(normed_mid, "tensor", axis=0, tiled=True))
    sums = []
    for chunk in range(CHUNKS):
        lifted = jnp.dot(gathers[chunk], up_weight, preferred_element_type=jnp.float32) + up_bias
        expanded = jax.nn.gelu(lifted, approximate=False).astype(jnp.bfloat16)
        expanded = lax.optimization_barrier(expanded)
        terms = jnp.dot(expanded, down_weight, preferred_element_type=jnp.float32)
        sums.append(
            lax.psum_scatter(
                terms.astype(jnp.bfloat16), "tensor", scatter_dimension=0, tiled=True
            )
        )
    kv_pages = lay_out_pages(received, position)
    outs = [
        (residual_mid.astype(jnp.float32) + mlp_sum.astype(jnp.float32) + down_bias).astype(
            jnp.bfloat16
        )
        for residual_mid, mlp_sum in zip(residuals, sums)
    ]
    layer_out = outs[0] if CHUNKS == 1 else jnp.concatenate(outs, axis=0)
    return (layer_out, kv_pages)


def solution(mesh):
    in_specs = (
        P(("dp", "tensor"), None),
        P(),
        P(),
        P(None, "tensor"),
        P("tensor"),
        P("tensor", None),
        P(),
        P(),
        P(),
        P(None, "tensor"),
        P("tensor"),
        P("tensor", None),
        P(),
        P("dp", None),
        P("dp"),
        P("dp", None),
    )
    out_specs = (P(("dp", "tensor"), None), P(("dp", "tensor"), None, None))
    body = on_line if (mesh.shape["dp"], mesh.shape["tensor"]) == SQUARE_LINE else on_device
    return jax.shard_map(
        body, mesh=mesh, in_specs=in_specs, out_specs=out_specs, check_vma=False
    )
```

```python
import functools
import math

import jax
import jax.numpy as jnp
from jax import lax
from jax.experimental import pallas as pl
from jax.experimental.pallas import tpu as pltpu
from jax.sharding import PartitionSpec as P

HD = 128
PAGE = 16
MAX_DOC = 1024
Q_BLOCK = 256
CHUNKS = 2


def normalize(values, norm_gain, norm_shift):
    widened = values.astype(jnp.float32)
    center = jnp.mean(widened, axis=-1, keepdims=True)
    spread = jnp.mean(jnp.square(widened - center), axis=-1, keepdims=True)
    return (widened - center) * lax.rsqrt(spread + 1e-05) * norm_gain + norm_shift


def attend_kernel(most, count_ref, proj_ref, kseg_ref, out_ref):
    block = pl.program_id(1)
    rows = out_ref.shape[0]
    heads = out_ref.shape[1] // HD
    count = count_ref[pl.program_id(0), block]
    here = pl.ds(pl.multiple_of(block * rows, rows), rows)

    query_segments = jnp.transpose(jnp.broadcast_to(kseg_ref[0, :, here], (8, rows)))[:, :1]

    def over(blocks):
        window = blocks * rows
        start = pl.multiple_of((block - blocks + 1) * rows, rows)
        ahead = lax.broadcasted_iota(jnp.int32, (rows, window), 1) - lax.broadcasted_iota(
            jnp.int32, (rows, window), 0
        )
        allowed = (ahead <= window - rows) & (
            query_segments == kseg_ref[0, :, pl.ds(start, window)]
        )
        scores = [
            lax.dot_general(
                proj_ref[here, 3 * n * HD : (3 * n + 1) * HD],
                proj_ref[pl.ds(start, window), (3 * n + 1) * HD : (3 * n + 2) * HD],
                (((1,), (1,)), ((), ())),
                preferred_element_type=jnp.float32,
            )
            for n in range(heads)
        ]
        for n in range(heads):
            masked = jnp.where(allowed, scores[n], -1e30)
            top = jnp.max(masked, axis=1, keepdims=True)
            expo = jnp.exp2((masked - top) * (math.log2(math.e) / math.sqrt(HD)))
            values = proj_ref[pl.ds(start, window), (3 * n + 2) * HD : (3 * n + 3) * HD]
            sums = jnp.dot(
                expo.astype(jnp.bfloat16), values, preferred_element_type=jnp.float32
            )
            out_ref[:, n * HD : (n + 1) * HD] = (
                sums * (1.0 / jnp.sum(expo, axis=1, keepdims=True))
            ).astype(jnp.bfloat16)

    for blocks in range(1, most + 1):
        pl.when(count == blocks)(functools.partial(over, blocks))


def key_blocks(segment_ids):
    blocks = segment_ids.shape[1] // Q_BLOCK
    most = min(blocks, MAX_DOC // Q_BLOCK + 1)
    firsts = segment_ids[:, ::Q_BLOCK]
    begins = jnp.sum((segment_ids[:, None, :] < firsts[:, :, None]).astype(jnp.int32), axis=2)
    counts = jnp.arange(blocks, dtype=jnp.int32)[None, :] - begins // Q_BLOCK + 1
    return most, jnp.clip(counts, 1, most)


def attend(projected, segment_ids):
    streams, seq_len = segment_ids.shape
    heads = projected.shape[1] // (3 * HD)
    blocks = seq_len // Q_BLOCK
    pairs = streams * heads * seq_len * 2 * Q_BLOCK
    most, counts = key_blocks(segment_ids)
    return pl.pallas_call(
        functools.partial(attend_kernel, most),
        grid_spec=pltpu.PrefetchScalarGridSpec(
            num_scalar_prefetch=1,
            grid=(streams, blocks),
            in_specs=[
                pl.BlockSpec((seq_len, 3 * heads * HD), lambda s, i, counts: (s, 0)),
                pl.BlockSpec((1, 1, seq_len), lambda s, i, counts: (s, 0, 0)),
            ],
            out_specs=pl.BlockSpec((Q_BLOCK, heads * HD), lambda s, i, counts: (s * blocks + i, 0)),
        ),
        out_shape=jax.ShapeDtypeStruct((streams * seq_len, heads * HD), jnp.bfloat16),
        compiler_params=pltpu.CompilerParams(vmem_limit_bytes=60 << 20),
        cost_estimate=pl.CostEstimate(
            flops=4 * pairs * HD,
            bytes_accessed=2 * projected.size * 2,
            transcendentals=pairs,
        ),
        name="attend",
    )(
        counts,
        projected,
        segment_ids.reshape(streams, 1, seq_len),
    )


def join_pair(value, axis, position):
    devices = lax.axis_size("tensor")
    other = lax.ppermute(value, "tensor", [(source, source ^ 1) for source in range(devices)])
    first = jnp.where(position % 2 == 0, value, other)
    second = jnp.where(position % 2 == 0, other, value)
    return jnp.concatenate([first, second], axis=axis)


def copy_page(index_ref, page_ref, out_ref):
    out_ref[...] = page_ref[...]


def take_pages(page_rows, index):
    block = (1,) + page_rows.shape[1:]
    return pl.pallas_call(
        copy_page,
        grid_spec=pltpu.PrefetchScalarGridSpec(
            num_scalar_prefetch=1,
            grid=(index.shape[0],),
            in_specs=[pl.BlockSpec(block, lambda i, index: (index[i], 0, 0))],
            out_specs=pl.BlockSpec(block, lambda i, index: (i, 0, 0)),
        ),
        out_shape=jax.ShapeDtypeStruct(index.shape + page_rows.shape[1:], page_rows.dtype),
    )(index, page_rows)


def pack_pages(keys_vals, live, page_table, capacity, position):
    devices = lax.axis_size("tensor")
    pages = keys_vals.shape[0] // PAGE
    owners = page_table[:, 0]
    numbers = jnp.arange(pages, dtype=jnp.int32)
    earlier = (owners[None, :] == owners[:, None]) & (numbers[None, :] < numbers[:, None])
    ranks = jnp.sum(earlier.astype(jnp.int32), axis=1)
    slot_ids = owners * capacity + ranks
    owner_order = position ^ jnp.arange(devices, dtype=jnp.int32)
    slots = owner_order[:, None] * capacity + jnp.arange(capacity, dtype=jnp.int32)[None, :]
    hits = slot_ids[None, :] == slots.reshape(-1)[:, None]
    source_page = jnp.sum(jnp.where(hits, numbers[None, :], 0), axis=1)
    live_pages = live.reshape(pages, PAGE).astype(jnp.int32)
    kept = jnp.sum(jnp.where(hits[:, :, None], live_pages[None], 0), axis=1) > 0
    page_rows = keys_vals.reshape(pages, PAGE, -1)
    taken = take_pages(page_rows, source_page)
    outgoing = jnp.where(kept[:, :, None], taken, 0).astype(jnp.bfloat16)
    return [
        lax.slice_in_dim(outgoing, apart * capacity, (apart + 1) * capacity, axis=0)
        for apart in range(devices)
    ]


def send_pages(pieces):
    devices = len(pieces)
    received = [pieces[0]]
    for apart in range(1, devices):
        hops = [(source, source ^ apart) for source in range(devices)]
        received.append(lax.ppermute(pieces[apart], "tensor", hops))
    return received


def lay_out_pages(received, position):
    devices = len(received)
    slots, page, width = received[0].shape
    laid = jnp.zeros((slots, page, devices * width), received[0].dtype)
    for apart in range(devices):
        laid = lax.dynamic_update_slice_in_dim(
            laid, received[apart], (position ^ apart) * width, axis=2
        )
    return laid


MESH = pl.DeviceIdType.MESH
SQUARE_LINE = (4, 8)
CHUNK = 32
TILE = 1024


def layer_norm(values, gain, shift):
    widened = values.astype(jnp.float32)
    center = jnp.mean(widened, axis=-1, keepdims=True)
    moved = widened - center
    spread = jnp.mean(moved * moved, axis=-1, keepdims=True)
    return moved * lax.rsqrt(spread + 1e-05) * gain + shift


def norm_rows(load, out, rows, gain_ref, shift_ref):
    @pl.loop(0, rows // 16, unroll=4)
    def _(i):
        part = pl.ds(pl.multiple_of(i * 16, 16), 16)
        out[part, :] = layer_norm(load(part), gain_ref[...], shift_ref[...]).astype(jnp.bfloat16)


def greet(me, chips, across=()):
    z, c = me // 2, lax.rem(me, 2)
    barrier = pltpu.get_barrier_semaphore()
    pl.semaphore_signal(barrier, inc=1, device_id={"tensor": 2 * z + 1 - c}, device_id_type=MESH)
    for column in across:
        pl.semaphore_signal(barrier, inc=1, device_id={"dp": column}, device_id_type=MESH)

    @pl.when(z > 0)
    def _():
        pl.semaphore_signal(barrier, inc=1, device_id={"tensor": me - 2}, device_id_type=MESH)

    @pl.when(z < chips - 1)
    def _():
        pl.semaphore_signal(barrier, inc=1, device_id={"tensor": me + 2}, device_id_type=MESH)

    peers = 1 + len(across) + (z > 0).astype(jnp.int32) + (z < chips - 1).astype(jnp.int32)
    pl.semaphore_wait(barrier, peers)


def page_tables(
    me, devices, seq_len, seg_ref, table_ref, limit_ref, count_ref, source_ref, live_ref
):
    blocks = seq_len // Q_BLOCK
    lanes = lax.broadcasted_iota(jnp.int32, (1, 128), 1)
    counts = jnp.ones((1, 128), jnp.int32)
    for i in range(blocks):
        first = seg_ref[:, i * Q_BLOCK : i * Q_BLOCK + 1]
        begin = jnp.sum((seg_ref[...] < first).astype(jnp.int32), axis=1, keepdims=True)
        counts = jnp.where(lanes == i, i + 1 - begin // Q_BLOCK, counts)
    count_ref[...] = jnp.clip(counts, 1, min(blocks, MAX_DOC // Q_BLOCK + 1))

    pages = table_ref.shape[0]
    owners = jnp.broadcast_to(table_ref[...], (pages, pages))
    row = lax.broadcasted_iota(jnp.int32, (pages, pages), 0)
    lane = lax.broadcasted_iota(jnp.int32, (pages, pages), 1)
    turned = jnp.transpose(owners)
    same = owners == turned
    ranks = jnp.sum((same & (lane < row)).astype(jnp.int32), axis=1, keepdims=True)
    here = (owners == me) & (ranks == lane)
    source_ref[...] = jnp.sum(jnp.where(here, row, 0), axis=0, keepdims=True)
    ranks_turned = jnp.sum((same & (row < lane)).astype(jnp.int32), axis=0, keepdims=True)
    tokens = live_ref.shape[0]
    at = lax.broadcasted_iota(jnp.int32, (tokens, pages), 0)
    number = lax.broadcasted_iota(jnp.int32, (tokens, pages), 1)
    spot = number * PAGE + lax.rem(at, PAGE)
    kept = (turned[:1] == me) & (ranks_turned == at // PAGE) & (spot < limit_ref[...])
    live_ref[...] = jnp.sum(kept.astype(jnp.int32), axis=1, keepdims=True)


def gather_project_kernel(
    chips, streams_len, hid, w_hbm, outw_hbm, b_ref, gain_ref, shift_ref, seg_ref, table_ref,
    limit_ref, hall_out, proj_out, oall, kall, count_ref, source_ref, live_ref,
    buf, w_ref, nrm, pbuf, kshare, ssem, rsem, lsem, psem, wsem, share_s, share_r,
):
    me, p = lax.axis_index("tensor"), lax.axis_index("dp")
    z, c = me // 2, lax.rem(me, 2)
    twin = 2 * z + 1 - c
    beside, over, corner = p + 1 - 2 * lax.rem(p, 2), lax.rem(p + 2, 4), 3 - p
    rows, width = hid.shape
    cols = w_ref.shape[1]
    out_rows = oall.shape[2]
    oshare = outw_hbm.at[pl.ds(pl.multiple_of(p * out_rows, out_rows), out_rows)]
    pair, own_share = (oall, kall), (oshare, kshare)
    load = pltpu.make_async_copy(w_hbm, w_ref, wsem.at[0])
    own = pltpu.make_async_copy(hid, buf.at[me], wsem.at[1])
    own_shares = [
        pltpu.make_async_copy(oshare, oall.at[p, me], wsem.at[2]),
        pltpu.make_async_copy(kshare, kall.at[p, me], wsem.at[3]),
    ]
    heads, kv_rows = cols // (3 * HD), kshare.shape[0] - PAGE
    cuts = [
        pltpu.make_async_copy(
            w_hbm.at[
                pl.ds(pl.multiple_of(p * kv_rows, kv_rows), kv_rows),
                pl.ds((3 * n + 1) * HD, 2 * HD),
            ],
            kshare.at[pl.ds(0, kv_rows), pl.ds(n * 2 * HD, 2 * HD)],
            wsem.at[4 + n],
        )
        for n in range(heads)
    ]
    for copy in cuts:
        copy.start()
    own_shares[0].start()
    own.start()
    load.start()
    for n in range(heads):
        kshare[kv_rows:, n * 2 * HD : (n + 1) * 2 * HD] = jnp.broadcast_to(
            b_ref[:, (3 * n + 1) * HD : (3 * n + 3) * HD].astype(jnp.bfloat16), (PAGE, 2 * HD)
        )
    greet(me, chips, (beside, over))
    for copy in cuts:
        copy.wait()
    own_shares[1].start()

    def share_copy(a, q, slot, way, own_from=False):
        device = [
            {"tensor": me - 2}, {"tensor": me + 2}, {"tensor": twin}, {"dp": beside}, {"dp": over},
        ][way]
        source = own_share[a] if own_from else pair[a].at[q, slot]
        return pltpu.make_async_remote_copy(
            src_ref=source, dst_ref=pair[a].at[q, slot],
            send_sem=share_s.at[a, q, slot, way], recv_sem=share_r.at[a, q, slot],
            device_id=device, device_id_type=MESH,
        )

    def share_send(q, slot, *ways):
        for a in range(2):
            for way in ways:
                share_copy(a, q, slot, way).start()

    def own_share_send(*ways):
        for a in range(2):
            for way in ways:
                share_copy(a, p, me, way, True).start()

    def share_arrived(q, slot):
        for a in range(2):
            share_copy(a, q, slot, 2).wait_recv()

    def share_line(hop):
        @pl.when(z - hop >= 0)
        def _():
            slot = me - 2 * hop
            share_arrived(p, slot)

            @pl.when(z < chips - 1)
            def _():
                share_send(p, slot, 1)

            share_send(p, slot, 3, 4, 2)

        @pl.when(z + hop < chips)
        def _():
            slot = me + 2 * hop
            share_arrived(p, slot)

            @pl.when(z > 0)
            def _():
                share_send(p, slot, 0)

            share_send(p, slot, 3, 4, 2)

    def at_slots(hop, run):
        if hop == 0:
            run(me)
        else:
            pl.when(z - hop >= 0)(lambda: run(me - 2 * hop))
            pl.when(z + hop < chips)(lambda: run(me + 2 * hop))

    def share_across(slot):
        share_arrived(over, slot)
        pl.when(c == 0)(lambda: share_send(over, slot, 3))
        share_arrived(beside, slot)
        pl.when(c == 1)(lambda: share_send(beside, slot, 4))
        share_send(over, slot, 2)
        share_send(beside, slot, 2)

    def share_corner(slot):
        share_arrived(corner, slot)
        share_send(corner, slot, 2)

    def token_copy(slot, half, device, way):
        part = pl.ds(half * (rows // 2), rows // 2)
        return pltpu.make_async_remote_copy(
            src_ref=buf.at[slot, part], dst_ref=buf.at[slot, part],
            send_sem=ssem.at[slot, way, half], recv_sem=rsem.at[slot, half],
            device_id={"tensor": device}, device_id_type=MESH,
        )

    def send(slot, device, way):
        for half in range(2):
            token_copy(slot, half, device, way).start()

    def sent(slot, way):
        for half in range(2):
            token_copy(slot, half, twin, way).wait_send()

    def compute(slot, arriving=False):
        for half in range(2):
            if arriving:
                token_copy(slot, half, twin, 2).wait_recv()
            part = pl.ds(half * (rows // 2), rows // 2)
            block = buf.at[slot, part]
            norm_rows(
                lambda inner: block[inner, :], nrm.at[part], rows // 2, gain_ref, shift_ref
            )
        pltpu.make_async_copy(buf.at[slot], hall_out.at[slot], lsem.at[slot]).start()

        pbuf[slot] = (
            jnp.dot(nrm[...], w_ref[...], preferred_element_type=jnp.float32)
            + b_ref[...].astype(jnp.float32)
        ).astype(jnp.bfloat16)

        pltpu.make_async_copy(pbuf.at[slot], proj_out.at[slot], psem.at[slot]).start()

    def token_line(hop):
        for half in range(2):

            @pl.when(z - hop >= 0)
            def _():
                slot = me - 2 * hop
                token_copy(slot, half, twin, 2).wait_recv()

                @pl.when(z < chips - 1)
                def _():
                    token_copy(slot, half, me + 2, 1).start()

                token_copy(slot, half, twin, 2).start()

            @pl.when(z + hop < chips)
            def _():
                slot = me + 2 * hop
                token_copy(slot, half, twin, 2).wait_recv()

                @pl.when(z > 0)
                def _():
                    token_copy(slot, half, me - 2, 0).start()

                token_copy(slot, half, twin, 2).start()

    def token_compute(hop):
        @pl.when(z - hop >= 0)
        def _():
            compute(me - 2 * hop)
            compute(twin - 2 * hop, True)

        @pl.when(z + hop < chips)
        def _():
            compute(me + 2 * hop)
            compute(twin + 2 * hop, True)

    pl.when(z > 0)(lambda: own_share_send(0))
    pl.when(z < chips - 1)(lambda: own_share_send(1))
    own_share_send(3, 4, 2)
    own.wait()
    load.wait()
    page_tables(
        me, 2 * chips, streams_len, seg_ref, table_ref, limit_ref, count_ref, source_ref, live_ref
    )
    compute(me)
    for hop in range(1, chips - 1):
        share_line(hop)
        if hop == 1:
            at_slots(0, share_across)
    pl.when(z > 0)(lambda: send(me, me - 2, 0))
    pl.when(z < chips - 1)(lambda: send(me, me + 2, 1))
    send(me, twin, 2)
    share_line(chips - 1)
    compute(twin, True)
    for hop in range(1, chips):
        at_slots(hop, share_across)
        at_slots(hop - 1, share_corner)
        token_line(hop)
        token_compute(hop)
    at_slots(chips - 1, share_corner)

    for copy in own_shares:
        copy.wait()
    for slot in range(2 * chips):
        pltpu.make_async_copy(buf.at[slot], hall_out.at[slot], lsem.at[slot]).wait()
        pltpu.make_async_copy(pbuf.at[slot], proj_out.at[slot], psem.at[slot]).wait()
    for origin in range(chips):
        slot = 2 * origin + c
        sent(slot, 2)
        for q in (beside, over, corner):
            share_arrived(q, 2 * origin + 1 - c)

        share_arrived(p, 2 * origin + 1 - c)

        @pl.when((origin >= z) & (z > 0))
        def _():
            sent(slot, 0)
            for a in range(2):
                share_copy(a, p, slot, 0).wait_send()

        @pl.when((origin <= z) & (z < chips - 1))
        def _():
            sent(slot, 1)
            for a in range(2):
                share_copy(a, p, slot, 1).wait_send()

        for a in range(2):
            for q in (p, beside, over, corner):
                share_copy(a, q, slot, 2).wait_send()
            share_copy(a, p, slot, 3).wait_send()
            share_copy(a, p, slot, 4).wait_send()

            @pl.when(c == 0)
            def _():
                share_copy(a, over, slot, 3).wait_send()

            @pl.when(c == 1)
            def _():
                share_copy(a, beside, slot, 4).wait_send()


def gather_project(
    hidden_in, qkv_weight, out_weight, qkv_bias, gain, shift, segment_ids, page_table,
    prompt_lengths, devices, columns,
):
    rows, width = hidden_in.shape
    cols = qkv_weight.shape[1]
    hbm, vmem = pl.BlockSpec(memory_space=pl.ANY), pl.BlockSpec(memory_space=pltpu.VMEM)
    total = rows * devices
    heads = cols // (3 * HD)
    kv_share = (width // columns + PAGE, 2 * heads * HD)
    dma = pltpu.SemaphoreType.DMA
    return pl.pallas_call(
        functools.partial(gather_project_kernel, devices // 2, segment_ids.shape[1]),
        in_specs=[hbm] * 3 + [vmem] * 6,
        out_specs=[hbm] * 4 + [vmem] * 3,
        out_shape=[
            jax.ShapeDtypeStruct((devices, rows, width), jnp.bfloat16),
            jax.ShapeDtypeStruct((devices, rows, cols), jnp.bfloat16),
            jax.ShapeDtypeStruct(
                (columns, devices, out_weight.shape[0] // columns, width), jnp.bfloat16
            ),
            jax.ShapeDtypeStruct((columns, devices) + kv_share, jnp.bfloat16),
            jax.ShapeDtypeStruct((1, 128), jnp.int32),
            jax.ShapeDtypeStruct((1, page_table.shape[0]), jnp.int32),
            jax.ShapeDtypeStruct((2 * total // devices, 1), jnp.int32),
        ],
        scratch_shapes=[
            pltpu.VMEM((devices, rows, width), jnp.bfloat16),
            pltpu.VMEM((width, cols), jnp.bfloat16),
            pltpu.VMEM((rows, width), jnp.bfloat16),
            pltpu.VMEM((devices, rows, cols), jnp.bfloat16),
            pltpu.VMEM(kv_share, jnp.bfloat16),
            dma((devices, 3, 2)),
            dma((devices, 2)),
            dma((devices,)),
            dma((devices,)),
            dma((4 + heads,)),
            dma((2, columns, devices, 5)),
            dma((2, columns, devices)),
        ],
        compiler_params=pltpu.CompilerParams(
            collective_id=0, has_side_effects=True, vmem_limit_bytes=60 << 20
        ),
        cost_estimate=pl.CostEstimate(
            flops=2 * total * width * cols,
            bytes_accessed=2 * (total * (width + cols) + width * cols),
            transcendentals=0,
        ),
        name="gather_project",
    )(
        hidden_in, qkv_weight, out_weight, qkv_bias.astype(jnp.float32).reshape(1, cols),
        gain.reshape(1, width), shift.reshape(1, width), segment_ids, page_table,
        prompt_lengths.reshape(1, 1),
    )


def mlp_kernel(
    chips, att, hall, outw_hbm, upw_hbm, dnw_hbm, pages, kvw_hbm, outb_ref, gain_ref, shift_ref,
    upb_ref, dnb_ref, live_ref, page_gain_ref, page_shift_ref,
    out_ref, kv_out,
    ag, outw, upw, dnw, hbuf, res, nrm, exp_, own_res, par, tw, lin, rin,
    pbuf, kvw, kvo, wsem, osem, hsem, ag_s, ag_r, tw_s, tw_r, rs_s, rs_r, psem,
):
    me = lax.axis_index("tensor")
    z, c = me // 2, lax.rem(me, 2)
    twin = 2 * z + 1 - c
    devices = 2 * chips
    chunks = ag.shape[0]
    width = outw.shape[1]
    piece = att.shape[-1]
    hidden_units = upw.shape[1]
    rows = devices * CHUNK

    columns, _, out_rows, _ = outw_hbm.shape
    loads = [
        pltpu.make_async_copy(
            outw_hbm.at[p, d], outw.at[pl.ds((d * columns + p) * out_rows, out_rows)], wsem.at[2 + d * columns + p]
        )
        for d in range(devices)
        for p in range(columns)
    ] + [
        pltpu.make_async_copy(upw_hbm, upw, wsem.at[0]),
        pltpu.make_async_copy(dnw_hbm, dnw, wsem.at[1]),
    ]

    def place(k, device):
        return ag.at[k, :, :, pl.ds(pl.multiple_of(device * piece, piece), piece)]

    def own_piece(k):
        part = pl.ds(pl.multiple_of(k * CHUNK, CHUNK), CHUNK)
        return pltpu.make_async_copy(att.at[:, part, :], place(k, me), osem.at[k])

    def hidden_part(k):
        part = pl.ds(pl.multiple_of(k * CHUNK, CHUNK), CHUNK)
        return pltpu.make_async_copy(hall.at[:, part, :], hbuf.at[lax.rem(k, 2)], hsem.at[lax.rem(k, 2)])

    @pl.loop(0, chunks)
    def _(k):
        own_piece(k).start()

    page_load = pltpu.make_async_copy(pages, pbuf, psem.at[4])
    page_load.start()

    def weight_load(t):
        return pltpu.make_async_copy(kvw_hbm.at[:, t], kvw.at[lax.rem(t, 2)], psem.at[lax.rem(t, 2)])

    def page_store(t):
        part = pl.ds(pl.multiple_of(t * kvo.shape[3], kvo.shape[3]), kvo.shape[3])
        return pltpu.make_async_copy(
            kvo.at[lax.rem(t, 2)], kv_out.at[:, :, part], psem.at[2 + lax.rem(t, 2)]
        )

    for t in range(2):
        weight_load(t).start()
    for load in loads:
        load.start()
    greet(me, chips)

    def page_step(t):
        slot = lax.rem(t, 2)
        depth = pbuf.shape[1] // columns

        weight_load(t).wait()
        pl.when(t >= 2)(lambda: page_store(t - 2).wait())
        sums = jnp.dot(
            pbuf[...],
            kvw[slot, :, :depth, :].reshape(pbuf.shape[1], kvw.shape[3]),
            preferred_element_type=jnp.float32,
        )
        bias = kvw[slot, 0, depth : depth + 1, :].astype(jnp.float32)
        made = jnp.where(live_ref[...] > 0, sums + bias, 0.0).astype(jnp.bfloat16)
        kvo[slot] = made.reshape(kvo.shape[1:])
        page_store(t).start()
        pl.when(t + 2 < devices)(lambda: weight_load(t + 2).start())

    drain = chunks + chips - 1
    turns = ((1, 1), (2, 1), (drain - 1, 1), (drain, 2), (drain + 1, 2), (drain + 2, 1))

    def pages_before(s):
        return sum(number * (s > at).astype(jnp.int32) for at, number in turns)

    def piece_copy(k, origin, device, way):
        return pltpu.make_async_remote_copy(
            src_ref=place(k, origin), dst_ref=place(k, origin), send_sem=ag_s.at[k, origin, way],
            recv_sem=ag_r.at[k, origin], device_id={"tensor": device}, device_id_type=MESH,
        )

    def piece_wait(k, origin):
        piece_copy(k, origin, twin, 2).wait_recv()

    def twin_copy(k, half):
        part = pl.ds(half * (width // 2), width // 2)
        return pltpu.make_async_remote_copy(
            src_ref=par.at[k, :, 1 - c, :, part], dst_ref=tw.at[k, :, :, part],
            send_sem=tw_s.at[k, half], recv_sem=tw_r.at[k, half],
            device_id={"tensor": twin}, device_id_type=MESH,
        )

    def right_copy(k, chip):
        return pltpu.make_async_remote_copy(
            src_ref=par.at[k, chip, c], dst_ref=lin.at[k, chip - 1],
            send_sem=rs_s.at[k, 0, chip], recv_sem=rs_r.at[k, 0, chip],
            device_id={"tensor": me + 2}, device_id_type=MESH,
        )

    def left_copy(k, chip):
        return pltpu.make_async_remote_copy(
            src_ref=par.at[k, chip, c], dst_ref=rin.at[k, chip],
            send_sem=rs_s.at[k, 1, chip], recv_sem=rs_r.at[k, 1, chip],
            device_id={"tensor": me - 2}, device_id_type=MESH,
        )

    def add_to(k, chip, more):
        par[k, chip, c] = (par[k, chip, c].astype(jnp.float32) + more.astype(jnp.float32)).astype(
            jnp.bfloat16
        )

    def at_chunk(k, run):
        pl.when((k >= 0) & (k < chunks))(lambda: run(k))

    def first_hop(k):
        own_piece(k).wait()

        @pl.when(z > 0)
        def _():
            piece_copy(k, me, me - 2, 0).start()

        @pl.when(z < chips - 1)
        def _():
            piece_copy(k, me, me + 2, 1).start()

        piece_copy(k, me, twin, 2).start()

    def later_hop(hop, k):
        @pl.when(z - hop >= 0)
        def _():
            origin = me - 2 * hop
            piece_wait(k, origin)

            @pl.when(z < chips - 1)
            def _():
                piece_copy(k, origin, me + 2, 1).start()

            piece_copy(k, origin, twin, 2).start()

        @pl.when(z + hop < chips)
        def _():
            origin = me + 2 * hop
            piece_wait(k, origin)

            @pl.when(z > 0)
            def _():
                piece_copy(k, origin, me - 2, 0).start()

            piece_copy(k, origin, twin, 2).start()

    def join_twins(k):
        for half in range(2):
            twin_copy(k, half).wait_recv()

        @pl.when(z < chips // 2)
        def _():
            for chip in reversed(range(chips)):
                add_to(k, chip, tw[k, chip])
                if chip > 0:
                    pl.when(z == 0)(lambda: right_copy(k, chip).start())

        @pl.when(z >= chips // 2)
        def _():
            for chip in range(chips):
                add_to(k, chip, tw[k, chip])
                if chip < chips - 1:
                    pl.when(z == chips - 1)(lambda: left_copy(k, chip).start())

    def add_left(k, at):
        for chip in reversed(range(at, chips)):
            right_copy(k, chip).wait_recv()
            add_to(k, chip, lin[k, chip - 1])
            if chip > at:
                right_copy(k, chip).start()

    def add_right(k, at):
        for chip in range(at + 1):
            left_copy(k, chip).wait_recv()
            add_to(k, chip, rin[k, chip])
            if chip < at:
                left_copy(k, chip).start()

    def pass_on(hop, k):
        for at in range(1, chips):
            if at == hop:

                @pl.when(z == at)
                def _():
                    add_left(k, at)

                @pl.when(z == chips - 1 - at)
                def _():
                    add_right(k, chips - 1 - at)

    def finish(k):
        part = pl.ds(pl.multiple_of(k * CHUNK, CHUNK), CHUNK)
        out_ref[part, :] = (
            own_res[part, :].astype(jnp.float32) + par[k, z, c].astype(jnp.float32) + dnb_ref[...]
        ).astype(jnp.bfloat16)

    def compute(k):
        for hop in range(1, chips):

            @pl.when(z - hop >= 0)
            def _():
                piece_wait(k, twin - 2 * hop)

            @pl.when(z + hop < chips)
            def _():
                piece_wait(k, twin + 2 * hop)

        piece_wait(k, twin)
        hidden_part(k).wait()
        slot = lax.rem(k, 2)

        @pl.when(k + 1 < chunks)
        def _():
            hidden_part(k + 1).start()

        @pl.when(k == 0)
        def _():
            for load in loads:
                load.wait()

        @pl.loop(0, width // TILE)
        def _(i):
            part = pl.ds(pl.multiple_of(i * TILE, TILE), TILE)
            terms = jnp.dot(
                ag[k].reshape(rows, width), outw[:, part], preferred_element_type=jnp.float32
            )
            res[:, part] = (
                hbuf[slot, :, :, part].reshape(rows, TILE).astype(jnp.float32)
                + terms
                + outb_ref[:, part]
            ).astype(jnp.bfloat16)

        norm_rows(lambda part: res[part, :], nrm, rows, gain_ref, shift_ref)
        own_res[pl.ds(pl.multiple_of(k * CHUNK, CHUNK), CHUNK), :] = res[
            pl.ds(pl.multiple_of(me * CHUNK, CHUNK), CHUNK), :
        ]

        for i in range(hidden_units // 256):
            part = slice(i * 256, (i + 1) * 256)
            lifted = (
                jnp.dot(nrm[...], upw[:, part], preferred_element_type=jnp.float32) + upb_ref[:, part]
            )
            exp_[:, part] = (0.5 * lifted * (1.0 + lax.erf(lifted * math.sqrt(0.5)))).astype(
                jnp.bfloat16
            )

        for half in range(2):
            part = slice(half * (width // 2), (half + 1) * (width // 2))
            par[k, :, :, :, part] = (
                jnp.dot(exp_[...], dnw[:, part], preferred_element_type=jnp.float32)
                .astype(jnp.bfloat16)
                .reshape(chips, 2, CHUNK, width // 2)
            )
            twin_copy(k, half).start()

    hidden_part(0).start()

    @pl.loop(0, chunks + 2 * chips - 2)
    def _(s):
        for hop in reversed(range(1, chips)):
            at_chunk(s - hop, functools.partial(later_hop, hop))
        at_chunk(s, first_hop)
        @pl.when(s == 0)
        def _():
            page_load.wait()
            norm_rows(
                lambda part: pbuf[part, :], pbuf, pbuf.shape[0], page_gain_ref, page_shift_ref
            )

        lax.fori_loop(pages_before(s), pages_before(s + 1), lambda t, _: page_step(t), None)
        at_chunk(s - chips + 1, compute)
        at_chunk(s - chips + 1, join_twins)
        for hop in reversed(range(1, chips)):
            at_chunk(s - chips + 1 - hop, functools.partial(pass_on, hop))
        at_chunk(s - 2 * chips + 2, finish)

    for t in range(devices - 2, devices):
        page_store(t).wait()

    @pl.loop(0, chunks)
    def _(k):
        for origin in range(chips):
            slot = 2 * origin + c
            piece_copy(k, slot, twin, 2).wait_send()

            @pl.when((origin >= z) & (z > 0))
            def _():
                piece_copy(k, slot, twin, 0).wait_send()

            @pl.when((origin <= z) & (z < chips - 1))
            def _():
                piece_copy(k, slot, twin, 1).wait_send()

        for half in range(2):
            twin_copy(k, half).wait_send()
        for chip in range(chips):
            pl.when(z < chip)(lambda: right_copy(k, chip).wait_send())
            pl.when(z > chip)(lambda: left_copy(k, chip).wait_send())


def mlp_layer(
    attended, hall, out_weight, up_weight, down_weight, pages, kv_weights, out_bias, gain, shift,
    up_bias, down_bias, live, page_gain, page_shift,
):
    devices, tok_rows, width = hall.shape
    chips, chunks = devices // 2, tok_rows // CHUNK
    piece, units = attended.shape[1], up_weight.shape[1]
    total = devices * tok_rows
    kept, kv_cols = pages.shape[0], kv_weights.shape[3]
    hbm, vmem = pl.BlockSpec(memory_space=pl.ANY), pl.BlockSpec(memory_space=pltpu.VMEM)
    dma = pltpu.SemaphoreType.DMA
    bf16 = jnp.bfloat16
    return pl.pallas_call(
        functools.partial(mlp_kernel, chips),
        in_specs=[hbm] * 7 + [vmem] * 8,
        out_specs=[vmem, hbm],
        out_shape=[
            jax.ShapeDtypeStruct((tok_rows, width), bf16),
            jax.ShapeDtypeStruct((kept // PAGE, PAGE, devices * kv_cols), bf16),
        ],
        scratch_shapes=[
            pltpu.VMEM((chunks, devices, CHUNK, width), bf16),
            pltpu.VMEM((width, width), bf16),
            pltpu.VMEM((width, units), bf16),
            pltpu.VMEM((units, width), bf16),
            pltpu.VMEM((2, devices, CHUNK, width), bf16),
            pltpu.VMEM((devices * CHUNK, width), bf16),
            pltpu.VMEM((devices * CHUNK, width), bf16),
            pltpu.VMEM((devices * CHUNK, units), bf16),
            pltpu.VMEM((tok_rows, width), bf16),
            pltpu.VMEM((chunks, chips, 2, CHUNK, width), bf16),
            pltpu.VMEM((chunks, chips, CHUNK, width), bf16),
            pltpu.VMEM((chunks, chips - 1, CHUNK, width), bf16),
            pltpu.VMEM((chunks, chips - 1, CHUNK, width), bf16),
            pltpu.VMEM(pages.shape, bf16),
            pltpu.VMEM((2,) + kv_weights.shape[:1] + kv_weights.shape[2:], bf16),
            pltpu.VMEM((2, kept // PAGE, PAGE, kv_cols), bf16),
            dma((2 + devices * out_weight.shape[0],)),
            dma((chunks,)),
            dma((2,)),
            dma((chunks, devices, 3)),
            dma((chunks, devices)),
            dma((chunks, 2)),
            dma((chunks, 2)),
            dma((chunks, 2, chips)),
            dma((chunks, 2, chips)),
            dma((5,)),
        ],
        compiler_params=pltpu.CompilerParams(
            collective_id=1, has_side_effects=True, vmem_limit_bytes=60 << 20
        ),
        cost_estimate=pl.CostEstimate(
            flops=2 * total * width * (width + 2 * units),
            bytes_accessed=2 * (2 * total * width + width * (width + 2 * units)),
            transcendentals=total * units,
        ),
        name="mlp_layer",
    )(
        attended.reshape(devices, tok_rows, piece),
        hall,
        out_weight,
        up_weight,
        down_weight,
        pages,
        kv_weights,
        out_bias.reshape(1, width),
        gain.reshape(1, width),
        shift.reshape(1, width),
        up_bias.reshape(1, units),
        down_bias.reshape(1, width),
        live,
        page_gain.reshape(1, width),
        page_shift.reshape(1, width),
    )


def attend_pages_kernel(
    most, count_ref, src_ref, proj_ref, kseg_ref, hall, out_ref, rows_ref, sem,
):
    block = pl.program_id(1)
    slots = rows_ref.shape[0] // PAGE
    copies = [
        pltpu.make_async_copy(hall.at[src_ref[0, i]], rows_ref.at[pl.ds(i * PAGE, PAGE)], sem.at[i])
        for i in range(slots)
    ]

    @pl.when(block == 0)
    def _():
        for copy in copies:
            copy.start()

    attend_kernel(most, count_ref, proj_ref, kseg_ref, out_ref)

    @pl.when(block == pl.num_programs(1) - 1)
    def _():
        for copy in copies:
            copy.wait()


def attend_pages(projected, segment_ids, counts, source, hall):
    streams, seq_len = segment_ids.shape
    heads = projected.shape[1] // (3 * HD)
    blocks = seq_len // Q_BLOCK
    devices, tok_rows, width = hall.shape
    slots = 2 * tok_rows // PAGE
    total = slots * PAGE
    most = min(blocks, MAX_DOC // Q_BLOCK + 1)
    pairs = streams * heads * seq_len * 2 * Q_BLOCK
    return pl.pallas_call(
        functools.partial(attend_pages_kernel, most),
        grid_spec=pltpu.PrefetchScalarGridSpec(
            num_scalar_prefetch=2,
            grid=(streams, blocks),
            in_specs=[
                pl.BlockSpec((seq_len, 3 * heads * HD), lambda s, i, counts, source: (s, 0)),
                pl.BlockSpec((1, 1, seq_len), lambda s, i, counts, source: (s, 0, 0)),
                pl.BlockSpec(memory_space=pl.ANY),
            ],
            out_specs=[
                pl.BlockSpec((Q_BLOCK, heads * HD), lambda s, i, counts, source: (s * blocks + i, 0)),
                pl.BlockSpec((total, width), lambda s, i, counts, source: (0, 0)),
            ],
            scratch_shapes=[pltpu.SemaphoreType.DMA((slots,))],
        ),
        out_shape=[
            jax.ShapeDtypeStruct((streams * seq_len, heads * HD), jnp.bfloat16),
            jax.ShapeDtypeStruct((total, width), jnp.bfloat16),
        ],
        compiler_params=pltpu.CompilerParams(vmem_limit_bytes=60 << 20),
        cost_estimate=pl.CostEstimate(
            flops=4 * pairs * HD,
            bytes_accessed=2 * projected.size * 2,
            transcendentals=pairs,
        ),
        name="attend",
    )(
        counts,
        source,
        projected,
        segment_ids.reshape(streams, 1, seq_len),
        hall.reshape(-1, PAGE, width),
    )


def on_line(
    hidden_in, attn_gain, attn_shift, qkv_weight, qkv_bias, out_weight, out_bias, mlp_gain,
    mlp_shift, up_weight, up_bias, down_weight, down_bias, segment_ids, prompt_lengths, page_table,
):
    devices = lax.axis_size("tensor")
    columns = lax.axis_size("dp")
    hall, projected, out_whole, kv_whole, counts, source, live = gather_project(
        hidden_in, qkv_weight, out_weight, qkv_bias, attn_gain, attn_shift, segment_ids,
        page_table, prompt_lengths, devices, columns,
    )
    attended, pages = attend_pages(
        projected.reshape(-1, projected.shape[2]), segment_ids, counts, source, hall
    )
    layer_out, kv_pages = mlp_layer(
        attended, hall, out_whole, up_weight, down_weight, pages, kv_whole, out_bias, mlp_gain,
        mlp_shift, up_bias, down_bias, live, attn_gain, attn_shift,
    )
    return (layer_out, kv_pages)


def on_device(
    hidden_in,
    attn_gain,
    attn_shift,
    qkv_weight,
    qkv_bias,
    out_weight,
    out_bias,
    mlp_gain,
    mlp_shift,
    up_weight,
    up_bias,
    down_weight,
    down_bias,
    segment_ids,
    prompt_lengths,
    page_table,
):
    devices = lax.axis_size("tensor")
    position = lax.axis_index("tensor")
    tok_rows, width = hidden_in.shape
    total_rows = tok_rows * devices
    streams, seq_len = segment_ids.shape
    whole_heads = qkv_weight.shape[1] % (3 * HD) == 0

    normed = normalize(hidden_in, attn_gain, attn_shift).astype(jnp.bfloat16)
    if not whole_heads:
        qkv_weight = join_pair(qkv_weight, 1, position)
        qkv_bias = join_pair(qkv_bias, 0, position)
    gathered = lax.all_gather(normed, "tensor", axis=0, tiled=True)
    projected = (
        jnp.dot(gathered, qkv_weight, preferred_element_type=jnp.float32)
        + qkv_bias.astype(jnp.float32)
    ).astype(jnp.bfloat16)
    heads_here = projected.shape[1] // (3 * HD)
    keys_vals = jnp.concatenate(
        [
            lax.slice_in_dim(projected, (3 * n + 1) * HD, (3 * n + 3) * HD, axis=1)
            for n in range(heads_here)
        ],
        axis=1,
    )
    if not whole_heads:
        half = keys_vals.shape[1] // 2
        keys_vals = lax.dynamic_slice_in_dim(keys_vals, position % 2 * half, half, 1)
    live = jnp.arange(seq_len, dtype=jnp.int32)[None, :] < prompt_lengths[:, None]
    pieces = pack_pages(
        keys_vals, live, page_table, 2 * (total_rows // PAGE) // devices, position
    )
    projected, pieces = lax.optimization_barrier((projected, pieces))
    received = send_pages(pieces)
    far, step = devices // 2, devices // 8
    attended = attend(projected, segment_ids)
    if not whole_heads:
        half = attended.shape[1] // 2
        attended = lax.dynamic_slice_in_dim(attended, position % 2 * half, half, 1)
    attended, received[far : far + step] = lax.optimization_barrier(
        (attended, received[far : far + step])
    )

    part = tok_rows // CHUNKS
    shaped = attended.reshape(devices, CHUNKS, part, attended.shape[1])
    sums = []
    for chunk in range(CHUNKS):
        rows = shaped[:, chunk].reshape(devices * part, -1)
        terms = jnp.dot(rows, out_weight, preferred_element_type=jnp.float32)
        sums.append(
            lax.psum_scatter(
                terms.astype(jnp.bfloat16), "tensor", scatter_dimension=0, tiled=True
            )
        )
    residuals, gathers = [], []
    for chunk in range(CHUNKS):
        hidden = lax.slice_in_dim(hidden_in, chunk * part, (chunk + 1) * part, axis=0)
        attn_sum = sums[chunk]
        if chunk == 0:
            attn_sum, received[far + step : far + 3 * step] = lax.optimization_barrier(
                (attn_sum, received[far + step : far + 3 * step])
            )
        else:
            attn_sum, residuals[-1], received, _ = lax.optimization_barrier(
                (attn_sum, residuals[-1], received, normed_mid)
            )
        residual_mid = (
            hidden.astype(jnp.float32) + attn_sum.astype(jnp.float32) + out_bias
        ).astype(jnp.bfloat16)
        normed_mid = normalize(residual_mid, mlp_gain, mlp_shift).astype(jnp.bfloat16)
        residuals.append(residual_mid)
        gathers.append(lax.all_gather(normed_mid, "tensor", axis=0, tiled=True))
    sums = []
    for chunk in range(CHUNKS):
        lifted = jnp.dot(gathers[chunk], up_weight, preferred_element_type=jnp.float32) + up_bias
        expanded = jax.nn.gelu(lifted, approximate=False).astype(jnp.bfloat16)
        expanded = lax.optimization_barrier(expanded)
        terms = jnp.dot(expanded, down_weight, preferred_element_type=jnp.float32)
        sums.append(
            lax.psum_scatter(
                terms.astype(jnp.bfloat16), "tensor", scatter_dimension=0, tiled=True
            )
        )
    kv_pages = lay_out_pages(received, position)
    outs = [
        (residual_mid.astype(jnp.float32) + mlp_sum.astype(jnp.float32) + down_bias).astype(
            jnp.bfloat16
        )
        for residual_mid, mlp_sum in zip(residuals, sums)
    ]
    layer_out = outs[0] if CHUNKS == 1 else jnp.concatenate(outs, axis=0)
    return (layer_out, kv_pages)


def solution(mesh):
    in_specs = (
        P(("dp", "tensor"), None),
        P(),
        P(),
        P(None, "tensor"),
        P("tensor"),
        P("tensor", None),
        P(),
        P(),
        P(),
        P(None, "tensor"),
        P("tensor"),
        P("tensor", None),
        P(),
        P("dp", None),
        P("dp"),
        P("dp", None),
    )
    out_specs = (P(("dp", "tensor"), None), P(("dp", "tensor"), None, None))
    body = on_line if (mesh.shape["dp"], mesh.shape["tensor"]) == SQUARE_LINE else on_device
    return jax.shard_map(
        body, mesh=mesh, in_specs=in_specs, out_specs=out_specs, check_vma=False
    )
```

```python
import functools
import math

import jax
import jax.numpy as jnp
from jax import lax
from jax.experimental import pallas as pl
from jax.experimental.pallas import tpu as pltpu
from jax.sharding import PartitionSpec as P

HD = 128
PAGE = 16
MAX_DOC = 1024
Q_BLOCK = 256
CHUNKS = 2


def normalize(values, norm_gain, norm_shift):
    widened = values.astype(jnp.float32)
    center = jnp.mean(widened, axis=-1, keepdims=True)
    spread = jnp.mean(jnp.square(widened - center), axis=-1, keepdims=True)
    return (widened - center) * lax.rsqrt(spread + 1e-05) * norm_gain + norm_shift


def attend_kernel(most, count_ref, proj_ref, kseg_ref, out_ref):
    block = pl.program_id(1)
    rows = out_ref.shape[0]
    heads = out_ref.shape[1] // HD
    count = count_ref[pl.program_id(0), block]
    here = pl.ds(pl.multiple_of(block * rows, rows), rows)

    query_segments = jnp.transpose(jnp.broadcast_to(kseg_ref[0, :, here], (8, rows)))[:, :1]

    def over(blocks):
        window = blocks * rows
        start = pl.multiple_of((block - blocks + 1) * rows, rows)
        ahead = lax.broadcasted_iota(jnp.int32, (rows, window), 1) - lax.broadcasted_iota(
            jnp.int32, (rows, window), 0
        )
        allowed = (ahead <= window - rows) & (
            query_segments == kseg_ref[0, :, pl.ds(start, window)]
        )
        scores = [
            lax.dot_general(
                proj_ref[here, 3 * n * HD : (3 * n + 1) * HD],
                proj_ref[pl.ds(start, window), (3 * n + 1) * HD : (3 * n + 2) * HD],
                (((1,), (1,)), ((), ())),
                preferred_element_type=jnp.float32,
            )
            for n in range(heads)
        ]
        for n in range(heads):
            masked = jnp.where(allowed, scores[n], -1e30)
            top = jnp.max(masked, axis=1, keepdims=True)
            expo = jnp.exp2((masked - top) * (math.log2(math.e) / math.sqrt(HD)))
            values = proj_ref[pl.ds(start, window), (3 * n + 2) * HD : (3 * n + 3) * HD]
            sums = jnp.dot(
                expo.astype(jnp.bfloat16), values, preferred_element_type=jnp.float32
            )
            out_ref[:, n * HD : (n + 1) * HD] = (
                sums * (1.0 / jnp.sum(expo, axis=1, keepdims=True))
            ).astype(jnp.bfloat16)

    for blocks in range(1, most + 1):
        pl.when(count == blocks)(functools.partial(over, blocks))


def key_blocks(segment_ids):
    blocks = segment_ids.shape[1] // Q_BLOCK
    most = min(blocks, MAX_DOC // Q_BLOCK + 1)
    firsts = segment_ids[:, ::Q_BLOCK]
    begins = jnp.sum((segment_ids[:, None, :] < firsts[:, :, None]).astype(jnp.int32), axis=2)
    counts = jnp.arange(blocks, dtype=jnp.int32)[None, :] - begins // Q_BLOCK + 1
    return most, jnp.clip(counts, 1, most)


def attend(projected, segment_ids):
    streams, seq_len = segment_ids.shape
    heads = projected.shape[1] // (3 * HD)
    blocks = seq_len // Q_BLOCK
    pairs = streams * heads * seq_len * 2 * Q_BLOCK
    most, counts = key_blocks(segment_ids)
    return pl.pallas_call(
        functools.partial(attend_kernel, most),
        grid_spec=pltpu.PrefetchScalarGridSpec(
            num_scalar_prefetch=1,
            grid=(streams, blocks),
            in_specs=[
                pl.BlockSpec((seq_len, 3 * heads * HD), lambda s, i, counts: (s, 0)),
                pl.BlockSpec((1, 1, seq_len), lambda s, i, counts: (s, 0, 0)),
            ],
            out_specs=pl.BlockSpec((Q_BLOCK, heads * HD), lambda s, i, counts: (s * blocks + i, 0)),
        ),
        out_shape=jax.ShapeDtypeStruct((streams * seq_len, heads * HD), jnp.bfloat16),
        compiler_params=pltpu.CompilerParams(vmem_limit_bytes=60 << 20),
        cost_estimate=pl.CostEstimate(
            flops=4 * pairs * HD,
            bytes_accessed=2 * projected.size * 2,
            transcendentals=pairs,
        ),
        name="attend",
    )(
        counts,
        projected,
        segment_ids.reshape(streams, 1, seq_len),
    )


def join_pair(value, axis, position):
    devices = lax.axis_size("tensor")
    other = lax.ppermute(value, "tensor", [(source, source ^ 1) for source in range(devices)])
    first = jnp.where(position % 2 == 0, value, other)
    second = jnp.where(position % 2 == 0, other, value)
    return jnp.concatenate([first, second], axis=axis)


def copy_page(index_ref, page_ref, out_ref):
    out_ref[...] = page_ref[...]


def take_pages(page_rows, index):
    block = (1,) + page_rows.shape[1:]
    return pl.pallas_call(
        copy_page,
        grid_spec=pltpu.PrefetchScalarGridSpec(
            num_scalar_prefetch=1,
            grid=(index.shape[0],),
            in_specs=[pl.BlockSpec(block, lambda i, index: (index[i], 0, 0))],
            out_specs=pl.BlockSpec(block, lambda i, index: (i, 0, 0)),
        ),
        out_shape=jax.ShapeDtypeStruct(index.shape + page_rows.shape[1:], page_rows.dtype),
    )(index, page_rows)


def pack_pages(keys_vals, live, page_table, capacity, position):
    devices = lax.axis_size("tensor")
    pages = keys_vals.shape[0] // PAGE
    owners = page_table[:, 0]
    numbers = jnp.arange(pages, dtype=jnp.int32)
    earlier = (owners[None, :] == owners[:, None]) & (numbers[None, :] < numbers[:, None])
    ranks = jnp.sum(earlier.astype(jnp.int32), axis=1)
    slot_ids = owners * capacity + ranks
    owner_order = position ^ jnp.arange(devices, dtype=jnp.int32)
    slots = owner_order[:, None] * capacity + jnp.arange(capacity, dtype=jnp.int32)[None, :]
    hits = slot_ids[None, :] == slots.reshape(-1)[:, None]
    source_page = jnp.sum(jnp.where(hits, numbers[None, :], 0), axis=1)
    live_pages = live.reshape(pages, PAGE).astype(jnp.int32)
    kept = jnp.sum(jnp.where(hits[:, :, None], live_pages[None], 0), axis=1) > 0
    page_rows = keys_vals.reshape(pages, PAGE, -1)
    taken = take_pages(page_rows, source_page)
    outgoing = jnp.where(kept[:, :, None], taken, 0).astype(jnp.bfloat16)
    return [
        lax.slice_in_dim(outgoing, apart * capacity, (apart + 1) * capacity, axis=0)
        for apart in range(devices)
    ]


def send_pages(pieces):
    devices = len(pieces)
    received = [pieces[0]]
    for apart in range(1, devices):
        hops = [(source, source ^ apart) for source in range(devices)]
        received.append(lax.ppermute(pieces[apart], "tensor", hops))
    return received


def lay_out_pages(received, position):
    devices = len(received)
    slots, page, width = received[0].shape
    laid = jnp.zeros((slots, page, devices * width), received[0].dtype)
    for apart in range(devices):
        laid = lax.dynamic_update_slice_in_dim(
            laid, received[apart], (position ^ apart) * width, axis=2
        )
    return laid


MESH = pl.DeviceIdType.MESH
SQUARE_LINE = (4, 8)
CHUNK = 32
TILE = 1024


def layer_norm(values, gain, shift):
    widened = values.astype(jnp.float32)
    center = jnp.mean(widened, axis=-1, keepdims=True)
    moved = widened - center
    spread = jnp.mean(moved * moved, axis=-1, keepdims=True)
    return moved * lax.rsqrt(spread + 1e-05) * gain + shift


def norm_rows(load, out, rows, gain_ref, shift_ref):
    @pl.loop(0, rows // 16, unroll=4)
    def _(i):
        part = pl.ds(pl.multiple_of(i * 16, 16), 16)
        out[part, :] = layer_norm(load(part), gain_ref[...], shift_ref[...]).astype(jnp.bfloat16)


def greet(me, chips, across=()):
    z, c = me // 2, lax.rem(me, 2)
    barrier = pltpu.get_barrier_semaphore()
    pl.semaphore_signal(barrier, inc=1, device_id={"tensor": 2 * z + 1 - c}, device_id_type=MESH)
    for column in across:
        pl.semaphore_signal(barrier, inc=1, device_id={"dp": column}, device_id_type=MESH)

    @pl.when(z > 0)
    def _():
        pl.semaphore_signal(barrier, inc=1, device_id={"tensor": me - 2}, device_id_type=MESH)

    @pl.when(z < chips - 1)
    def _():
        pl.semaphore_signal(barrier, inc=1, device_id={"tensor": me + 2}, device_id_type=MESH)

    peers = 1 + len(across) + (z > 0).astype(jnp.int32) + (z < chips - 1).astype(jnp.int32)
    pl.semaphore_wait(barrier, peers)


def page_tables(
    me, devices, seq_len, seg_ref, table_ref, limit_ref, count_ref, source_ref, live_ref
):
    blocks = seq_len // Q_BLOCK
    lanes = lax.broadcasted_iota(jnp.int32, (1, 128), 1)
    counts = jnp.ones((1, 128), jnp.int32)
    for i in range(blocks):
        first = seg_ref[:, i * Q_BLOCK : i * Q_BLOCK + 1]
        begin = jnp.sum((seg_ref[...] < first).astype(jnp.int32), axis=1, keepdims=True)
        counts = jnp.where(lanes == i, i + 1 - begin // Q_BLOCK, counts)
    count_ref[...] = jnp.clip(counts, 1, min(blocks, MAX_DOC // Q_BLOCK + 1))

    pages = table_ref.shape[1]
    turned = jnp.broadcast_to(table_ref[...], (pages, pages))
    owners = jnp.transpose(turned)
    row = lax.broadcasted_iota(jnp.int32, (pages, pages), 0)
    lane = lax.broadcasted_iota(jnp.int32, (pages, pages), 1)
    same = owners == turned
    ranks = jnp.sum((same & (lane < row)).astype(jnp.int32), axis=1, keepdims=True)
    here = (owners == me) & (ranks == lane)
    source_ref[...] = jnp.sum(jnp.where(here, row, 0), axis=0, keepdims=True)
    ranks_turned = jnp.sum((same & (row < lane)).astype(jnp.int32), axis=0, keepdims=True)
    tokens = live_ref.shape[0]
    at = lax.broadcasted_iota(jnp.int32, (tokens, pages), 0)
    number = lax.broadcasted_iota(jnp.int32, (tokens, pages), 1)
    spot = number * PAGE + lax.rem(at, PAGE)
    kept = (turned[:1] == me) & (ranks_turned == at // PAGE) & (spot < limit_ref[...])
    live_ref[...] = jnp.sum(kept.astype(jnp.int32), axis=1, keepdims=True)


def gather_project_kernel(
    chips, streams_len, hid, w_hbm, outw_hbm, b_ref, gain_ref, shift_ref, seg_ref, table_ref,
    limit_ref, hall_out, proj_out, oall, kall, count_ref, source_ref, live_ref,
    buf, w_ref, nrm, pbuf, kshare, ssem, rsem, lsem, psem, wsem, share_s, share_r,
):
    me, p = lax.axis_index("tensor"), lax.axis_index("dp")
    z, c = me // 2, lax.rem(me, 2)
    twin = 2 * z + 1 - c
    beside, over, corner = p + 1 - 2 * lax.rem(p, 2), lax.rem(p + 2, 4), 3 - p
    rows, width = hid.shape
    cols = w_ref.shape[1]
    out_rows = oall.shape[2]
    oshare = outw_hbm.at[pl.ds(pl.multiple_of(p * out_rows, out_rows), out_rows)]
    pair, own_share = (oall, kall), (oshare, kshare)
    load = pltpu.make_async_copy(w_hbm, w_ref, wsem.at[0])
    own = pltpu.make_async_copy(hid, buf.at[me], wsem.at[1])
    own_shares = [
        pltpu.make_async_copy(oshare, oall.at[p, me], wsem.at[2]),
        pltpu.make_async_copy(kshare, kall.at[p, me], wsem.at[3]),
    ]
    heads, kv_rows = cols // (3 * HD), kshare.shape[0] - PAGE
    cuts = [
        pltpu.make_async_copy(
            w_hbm.at[
                pl.ds(pl.multiple_of(p * kv_rows, kv_rows), kv_rows),
                pl.ds((3 * n + 1) * HD, 2 * HD),
            ],
            kshare.at[pl.ds(0, kv_rows), pl.ds(n * 2 * HD, 2 * HD)],
            wsem.at[4 + n],
        )
        for n in range(heads)
    ]
    for copy in cuts:
        copy.start()
    own_shares[0].start()
    own.start()
    load.start()
    for n in range(heads):
        kshare[kv_rows:, n * 2 * HD : (n + 1) * 2 * HD] = jnp.broadcast_to(
            b_ref[:, (3 * n + 1) * HD : (3 * n + 3) * HD].astype(jnp.bfloat16), (PAGE, 2 * HD)
        )
    greet(me, chips, (beside, over))
    for copy in cuts:
        copy.wait()
    own_shares[1].start()

    def share_copy(a, q, slot, way, own_from=False):
        device = [
            {"tensor": me - 2}, {"tensor": me + 2}, {"tensor": twin}, {"dp": beside}, {"dp": over},
        ][way]
        source = own_share[a] if own_from else pair[a].at[q, slot]
        return pltpu.make_async_remote_copy(
            src_ref=source, dst_ref=pair[a].at[q, slot],
            send_sem=share_s.at[a, q, slot, way], recv_sem=share_r.at[a, q, slot],
            device_id=device, device_id_type=MESH,
        )

    def share_send(q, slot, *ways):
        for a in range(2):
            for way in ways:
                share_copy(a, q, slot, way).start()

    def own_share_send(*ways):
        for a in range(2):
            for way in ways:
                share_copy(a, p, me, way, True).start()

    def share_arrived(q, slot):
        for a in range(2):
            share_copy(a, q, slot, 2).wait_recv()

    def share_line(hop):
        @pl.when(z - hop >= 0)
        def _():
            slot = me - 2 * hop
            share_arrived(p, slot)

            @pl.when(z < chips - 1)
            def _():
                share_send(p, slot, 1)

            share_send(p, slot, 3, 4, 2)

        @pl.when(z + hop < chips)
        def _():
            slot = me + 2 * hop
            share_arrived(p, slot)

            @pl.when(z > 0)
            def _():
                share_send(p, slot, 0)

            share_send(p, slot, 3, 4, 2)

    def at_slots(hop, run):
        if hop == 0:
            run(me)
        else:
            pl.when(z - hop >= 0)(lambda: run(me - 2 * hop))
            pl.when(z + hop < chips)(lambda: run(me + 2 * hop))

    def share_across(slot):
        share_arrived(over, slot)
        pl.when(c == 0)(lambda: share_send(over, slot, 3))
        share_arrived(beside, slot)
        pl.when(c == 1)(lambda: share_send(beside, slot, 4))
        share_send(over, slot, 2)
        share_send(beside, slot, 2)

    def share_corner(slot):
        share_arrived(corner, slot)
        share_send(corner, slot, 2)

    def token_copy(slot, half, device, way):
        part = pl.ds(half * (rows // 2), rows // 2)
        return pltpu.make_async_remote_copy(
            src_ref=buf.at[slot, part], dst_ref=buf.at[slot, part],
            send_sem=ssem.at[slot, way, half], recv_sem=rsem.at[slot, half],
            device_id={"tensor": device}, device_id_type=MESH,
        )

    def send(slot, device, way):
        for half in range(2):
            token_copy(slot, half, device, way).start()

    def sent(slot, way):
        for half in range(2):
            token_copy(slot, half, twin, way).wait_send()

    def compute(slot, arriving=False):
        for half in range(2):
            if arriving:
                token_copy(slot, half, twin, 2).wait_recv()
            part = pl.ds(half * (rows // 2), rows // 2)
            block = buf.at[slot, part]
            norm_rows(
                lambda inner: block[inner, :], nrm.at[part], rows // 2, gain_ref, shift_ref
            )
        pltpu.make_async_copy(buf.at[slot], hall_out.at[slot], lsem.at[slot]).start()

        pbuf[slot] = (
            jnp.dot(nrm[...], w_ref[...], preferred_element_type=jnp.float32)
            + b_ref[...].astype(jnp.float32)
        ).astype(jnp.bfloat16)

        pltpu.make_async_copy(pbuf.at[slot], proj_out.at[slot], psem.at[slot]).start()

    def token_line(hop):
        for half in range(2):

            @pl.when(z - hop >= 0)
            def _():
                slot = me - 2 * hop
                token_copy(slot, half, twin, 2).wait_recv()

                @pl.when(z < chips - 1)
                def _():
                    token_copy(slot, half, me + 2, 1).start()

                token_copy(slot, half, twin, 2).start()

            @pl.when(z + hop < chips)
            def _():
                slot = me + 2 * hop
                token_copy(slot, half, twin, 2).wait_recv()

                @pl.when(z > 0)
                def _():
                    token_copy(slot, half, me - 2, 0).start()

                token_copy(slot, half, twin, 2).start()

    def token_compute(hop):
        @pl.when(z - hop >= 0)
        def _():
            compute(me - 2 * hop)
            compute(twin - 2 * hop, True)

        @pl.when(z + hop < chips)
        def _():
            compute(me + 2 * hop)
            compute(twin + 2 * hop, True)

    pl.when(z > 0)(lambda: own_share_send(0))
    pl.when(z < chips - 1)(lambda: own_share_send(1))
    own_share_send(3, 4, 2)
    own.wait()
    load.wait()
    page_tables(
        me, 2 * chips, streams_len, seg_ref, table_ref, limit_ref, count_ref, source_ref, live_ref
    )
    compute(me)
    for hop in range(1, chips - 1):
        share_line(hop)
        if hop == 1:
            at_slots(0, share_across)
    pl.when(z > 0)(lambda: send(me, me - 2, 0))
    pl.when(z < chips - 1)(lambda: send(me, me + 2, 1))
    send(me, twin, 2)
    share_line(chips - 1)
    compute(twin, True)
    for hop in range(1, chips):
        at_slots(hop, share_across)
        at_slots(hop - 1, share_corner)
        token_line(hop)
        token_compute(hop)
    at_slots(chips - 1, share_corner)

    for copy in own_shares:
        copy.wait()
    for slot in range(2 * chips):
        pltpu.make_async_copy(buf.at[slot], hall_out.at[slot], lsem.at[slot]).wait()
        pltpu.make_async_copy(pbuf.at[slot], proj_out.at[slot], psem.at[slot]).wait()
    for origin in range(chips):
        slot = 2 * origin + c
        sent(slot, 2)
        for q in (beside, over, corner):
            share_arrived(q, 2 * origin + 1 - c)

        share_arrived(p, 2 * origin + 1 - c)

        @pl.when((origin >= z) & (z > 0))
        def _():
            sent(slot, 0)
            for a in range(2):
                share_copy(a, p, slot, 0).wait_send()

        @pl.when((origin <= z) & (z < chips - 1))
        def _():
            sent(slot, 1)
            for a in range(2):
                share_copy(a, p, slot, 1).wait_send()

        for a in range(2):
            for q in (p, beside, over, corner):
                share_copy(a, q, slot, 2).wait_send()
            share_copy(a, p, slot, 3).wait_send()
            share_copy(a, p, slot, 4).wait_send()

            @pl.when(c == 0)
            def _():
                share_copy(a, over, slot, 3).wait_send()

            @pl.when(c == 1)
            def _():
                share_copy(a, beside, slot, 4).wait_send()


def gather_project(
    hidden_in, qkv_weight, out_weight, qkv_bias, gain, shift, segment_ids, page_table,
    prompt_lengths, devices, columns,
):
    rows, width = hidden_in.shape
    cols = qkv_weight.shape[1]
    hbm, vmem = pl.BlockSpec(memory_space=pl.ANY), pl.BlockSpec(memory_space=pltpu.VMEM)
    total = rows * devices
    heads = cols // (3 * HD)
    kv_share = (width // columns + PAGE, 2 * heads * HD)
    dma = pltpu.SemaphoreType.DMA
    return pl.pallas_call(
        functools.partial(gather_project_kernel, devices // 2, segment_ids.shape[1]),
        in_specs=[hbm] * 3 + [vmem] * 6,
        out_specs=[hbm] * 4 + [vmem] * 3,
        out_shape=[
            jax.ShapeDtypeStruct((devices, rows, width), jnp.bfloat16),
            jax.ShapeDtypeStruct((devices, rows, cols), jnp.bfloat16),
            jax.ShapeDtypeStruct(
                (columns, devices, out_weight.shape[0] // columns, width), jnp.bfloat16
            ),
            jax.ShapeDtypeStruct((columns, devices) + kv_share, jnp.bfloat16),
            jax.ShapeDtypeStruct((1, 128), jnp.int32),
            jax.ShapeDtypeStruct((1, page_table.shape[0]), jnp.int32),
            jax.ShapeDtypeStruct((2 * total // devices, 1), jnp.int32),
        ],
        scratch_shapes=[
            pltpu.VMEM((devices, rows, width), jnp.bfloat16),
            pltpu.VMEM((width, cols), jnp.bfloat16),
            pltpu.VMEM((rows, width), jnp.bfloat16),
            pltpu.VMEM((devices, rows, cols), jnp.bfloat16),
            pltpu.VMEM(kv_share, jnp.bfloat16),
            dma((devices, 3, 2)),
            dma((devices, 2)),
            dma((devices,)),
            dma((devices,)),
            dma((4 + heads,)),
            dma((2, columns, devices, 5)),
            dma((2, columns, devices)),
        ],
        compiler_params=pltpu.CompilerParams(
            collective_id=0, has_side_effects=True, vmem_limit_bytes=60 << 20
        ),
        cost_estimate=pl.CostEstimate(
            flops=2 * total * width * cols,
            bytes_accessed=2 * (total * (width + cols) + width * cols),
            transcendentals=0,
        ),
        name="gather_project",
    )(
        hidden_in, qkv_weight, out_weight, qkv_bias.astype(jnp.float32).reshape(1, cols),
        gain.reshape(1, width), shift.reshape(1, width), segment_ids, page_table.reshape(1, -1),
        prompt_lengths.reshape(1, 1),
    )


def mlp_kernel(
    chips, att, hall, outw_hbm, upw_hbm, dnw_hbm, pages, kvw_hbm, outb_ref, gain_ref, shift_ref,
    upb_ref, dnb_ref, live_ref, page_gain_ref, page_shift_ref,
    out_ref, kv_out,
    ag, outw, upw, dnw, hbuf, res, nrm, exp_, own_res, par, tw, lin, rin,
    pbuf, kvw, kvo, wsem, osem, hsem, ag_s, ag_r, tw_s, tw_r, rs_s, rs_r, psem,
):
    me = lax.axis_index("tensor")
    z, c = me // 2, lax.rem(me, 2)
    twin = 2 * z + 1 - c
    devices = 2 * chips
    chunks = ag.shape[0]
    width = outw.shape[1]
    piece = att.shape[-1]
    hidden_units = upw.shape[1]
    rows = devices * CHUNK

    columns, _, out_rows, _ = outw_hbm.shape
    loads = [
        pltpu.make_async_copy(
            outw_hbm.at[p, d], outw.at[pl.ds((d * columns + p) * out_rows, out_rows)], wsem.at[2 + d * columns + p]
        )
        for d in range(devices)
        for p in range(columns)
    ] + [
        pltpu.make_async_copy(upw_hbm, upw, wsem.at[0]),
        pltpu.make_async_copy(dnw_hbm, dnw, wsem.at[1]),
    ]

    def place(k, device):
        return ag.at[k, :, :, pl.ds(pl.multiple_of(device * piece, piece), piece)]

    def own_piece(k):
        part = pl.ds(pl.multiple_of(k * CHUNK, CHUNK), CHUNK)
        return pltpu.make_async_copy(att.at[:, part, :], place(k, me), osem.at[k])

    def hidden_part(k):
        part = pl.ds(pl.multiple_of(k * CHUNK, CHUNK), CHUNK)
        return pltpu.make_async_copy(hall.at[:, part, :], hbuf.at[lax.rem(k, 2)], hsem.at[lax.rem(k, 2)])

    @pl.loop(0, chunks)
    def _(k):
        own_piece(k).start()

    page_load = pltpu.make_async_copy(pages, pbuf, psem.at[4])
    page_load.start()

    def weight_load(t):
        return pltpu.make_async_copy(kvw_hbm.at[:, t], kvw.at[lax.rem(t, 2)], psem.at[lax.rem(t, 2)])

    def page_store(t):
        part = pl.ds(pl.multiple_of(t * kvo.shape[3], kvo.shape[3]), kvo.shape[3])
        return pltpu.make_async_copy(
            kvo.at[lax.rem(t, 2)], kv_out.at[:, :, part], psem.at[2 + lax.rem(t, 2)]
        )

    for t in range(2):
        weight_load(t).start()
    for load in loads:
        load.start()
    greet(me, chips)

    def page_step(t):
        slot = lax.rem(t, 2)
        depth = pbuf.shape[1] // columns

        weight_load(t).wait()
        pl.when(t >= 2)(lambda: page_store(t - 2).wait())
        sums = jnp.dot(
            pbuf[...],
            kvw[slot, :, :depth, :].reshape(pbuf.shape[1], kvw.shape[3]),
            preferred_element_type=jnp.float32,
        )
        bias = kvw[slot, 0, depth : depth + 1, :].astype(jnp.float32)
        made = jnp.where(live_ref[...] > 0, sums + bias, 0.0).astype(jnp.bfloat16)
        kvo[slot] = made.reshape(kvo.shape[1:])
        page_store(t).start()
        pl.when(t + 2 < devices)(lambda: weight_load(t + 2).start())

    drain = chunks + chips - 1
    turns = ((1, 1), (2, 1), (drain - 1, 1), (drain, 2), (drain + 1, 2), (drain + 2, 1))

    def pages_before(s):
        return sum(number * (s > at).astype(jnp.int32) for at, number in turns)

    def piece_copy(k, origin, device, way):
        return pltpu.make_async_remote_copy(
            src_ref=place(k, origin), dst_ref=place(k, origin), send_sem=ag_s.at[k, origin, way],
            recv_sem=ag_r.at[k, origin], device_id={"tensor": device}, device_id_type=MESH,
        )

    def piece_wait(k, origin):
        piece_copy(k, origin, twin, 2).wait_recv()

    def twin_copy(k, half):
        part = pl.ds(half * (width // 2), width // 2)
        return pltpu.make_async_remote_copy(
            src_ref=par.at[k, :, 1 - c, :, part], dst_ref=tw.at[k, :, :, part],
            send_sem=tw_s.at[k, half], recv_sem=tw_r.at[k, half],
            device_id={"tensor": twin}, device_id_type=MESH,
        )

    def right_copy(k, chip):
        return pltpu.make_async_remote_copy(
            src_ref=par.at[k, chip, c], dst_ref=lin.at[k, chip - 1],
            send_sem=rs_s.at[k, 0, chip], recv_sem=rs_r.at[k, 0, chip],
            device_id={"tensor": me + 2}, device_id_type=MESH,
        )

    def left_copy(k, chip):
        return pltpu.make_async_remote_copy(
            src_ref=par.at[k, chip, c], dst_ref=rin.at[k, chip],
            send_sem=rs_s.at[k, 1, chip], recv_sem=rs_r.at[k, 1, chip],
            device_id={"tensor": me - 2}, device_id_type=MESH,
        )

    def add_to(k, chip, more):
        par[k, chip, c] = (par[k, chip, c].astype(jnp.float32) + more.astype(jnp.float32)).astype(
            jnp.bfloat16
        )

    def at_chunk(k, run):
        pl.when((k >= 0) & (k < chunks))(lambda: run(k))

    def first_hop(k):
        own_piece(k).wait()

        @pl.when(z > 0)
        def _():
            piece_copy(k, me, me - 2, 0).start()

        @pl.when(z < chips - 1)
        def _():
            piece_copy(k, me, me + 2, 1).start()

        piece_copy(k, me, twin, 2).start()

    def later_hop(hop, k):
        @pl.when(z - hop >= 0)
        def _():
            origin = me - 2 * hop
            piece_wait(k, origin)

            @pl.when(z < chips - 1)
            def _():
                piece_copy(k, origin, me + 2, 1).start()

            piece_copy(k, origin, twin, 2).start()

        @pl.when(z + hop < chips)
        def _():
            origin = me + 2 * hop
            piece_wait(k, origin)

            @pl.when(z > 0)
            def _():
                piece_copy(k, origin, me - 2, 0).start()

            piece_copy(k, origin, twin, 2).start()

    def join_twins(k):
        for half in range(2):
            twin_copy(k, half).wait_recv()

        @pl.when(z < chips // 2)
        def _():
            for chip in reversed(range(chips)):
                add_to(k, chip, tw[k, chip])
                if chip > 0:
                    pl.when(z == 0)(lambda: right_copy(k, chip).start())

        @pl.when(z >= chips // 2)
        def _():
            for chip in range(chips):
                add_to(k, chip, tw[k, chip])
                if chip < chips - 1:
                    pl.when(z == chips - 1)(lambda: left_copy(k, chip).start())

    def add_left(k, at):
        for chip in reversed(range(at, chips)):
            right_copy(k, chip).wait_recv()
            add_to(k, chip, lin[k, chip - 1])
            if chip > at:
                right_copy(k, chip).start()

    def add_right(k, at):
        for chip in range(at + 1):
            left_copy(k, chip).wait_recv()
            add_to(k, chip, rin[k, chip])
            if chip < at:
                left_copy(k, chip).start()

    def pass_on(hop, k):
        for at in range(1, chips):
            if at == hop:

                @pl.when(z == at)
                def _():
                    add_left(k, at)

                @pl.when(z == chips - 1 - at)
                def _():
                    add_right(k, chips - 1 - at)

    def finish(k):
        part = pl.ds(pl.multiple_of(k * CHUNK, CHUNK), CHUNK)
        out_ref[part, :] = (
            own_res[part, :].astype(jnp.float32) + par[k, z, c].astype(jnp.float32) + dnb_ref[...]
        ).astype(jnp.bfloat16)

    def compute(k):
        for hop in range(1, chips):

            @pl.when(z - hop >= 0)
            def _():
                piece_wait(k, twin - 2 * hop)

            @pl.when(z + hop < chips)
            def _():
                piece_wait(k, twin + 2 * hop)

        piece_wait(k, twin)
        hidden_part(k).wait()
        slot = lax.rem(k, 2)

        @pl.when(k + 1 < chunks)
        def _():
            hidden_part(k + 1).start()

        @pl.when(k == 0)
        def _():
            for load in loads:
                load.wait()

        @pl.loop(0, width // TILE)
        def _(i):
            part = pl.ds(pl.multiple_of(i * TILE, TILE), TILE)
            terms = jnp.dot(
                ag[k].reshape(rows, width), outw[:, part], preferred_element_type=jnp.float32
            )
            res[:, part] = (
                hbuf[slot, :, :, part].reshape(rows, TILE).astype(jnp.float32)
                + terms
                + outb_ref[:, part]
            ).astype(jnp.bfloat16)

        norm_rows(lambda part: res[part, :], nrm, rows, gain_ref, shift_ref)
        own_res[pl.ds(pl.multiple_of(k * CHUNK, CHUNK), CHUNK), :] = res[
            pl.ds(pl.multiple_of(me * CHUNK, CHUNK), CHUNK), :
        ]

        for i in range(hidden_units // 256):
            part = slice(i * 256, (i + 1) * 256)
            lifted = (
                jnp.dot(nrm[...], upw[:, part], preferred_element_type=jnp.float32) + upb_ref[:, part]
            )
            exp_[:, part] = (0.5 * lifted * (1.0 + lax.erf(lifted * math.sqrt(0.5)))).astype(
                jnp.bfloat16
            )

        for half in range(2):
            part = slice(half * (width // 2), (half + 1) * (width // 2))
            par[k, :, :, :, part] = (
                jnp.dot(exp_[...], dnw[:, part], preferred_element_type=jnp.float32)
                .astype(jnp.bfloat16)
                .reshape(chips, 2, CHUNK, width // 2)
            )
            twin_copy(k, half).start()

    hidden_part(0).start()

    @pl.loop(0, chunks + 2 * chips - 2)
    def _(s):
        for hop in reversed(range(1, chips)):
            at_chunk(s - hop, functools.partial(later_hop, hop))
        at_chunk(s, first_hop)
        @pl.when(s == 0)
        def _():
            page_load.wait()
            norm_rows(
                lambda part: pbuf[part, :], pbuf, pbuf.shape[0], page_gain_ref, page_shift_ref
            )

        lax.fori_loop(pages_before(s), pages_before(s + 1), lambda t, _: page_step(t), None)
        at_chunk(s - chips + 1, compute)
        at_chunk(s - chips + 1, join_twins)
        for hop in reversed(range(1, chips)):
            at_chunk(s - chips + 1 - hop, functools.partial(pass_on, hop))
        at_chunk(s - 2 * chips + 2, finish)

    for t in range(devices - 2, devices):
        page_store(t).wait()

    @pl.loop(0, chunks)
    def _(k):
        for origin in range(chips):
            slot = 2 * origin + c
            piece_copy(k, slot, twin, 2).wait_send()

            @pl.when((origin >= z) & (z > 0))
            def _():
                piece_copy(k, slot, twin, 0).wait_send()

            @pl.when((origin <= z) & (z < chips - 1))
            def _():
                piece_copy(k, slot, twin, 1).wait_send()

        for half in range(2):
            twin_copy(k, half).wait_send()
        for chip in range(chips):
            if chip > 0:
                pl.when(z < chip)(lambda: right_copy(k, chip).wait_send())
            if chip < chips - 1:
                pl.when(z > chip)(lambda: left_copy(k, chip).wait_send())


def mlp_layer(
    attended, hall, out_weight, up_weight, down_weight, pages, kv_weights, out_bias, gain, shift,
    up_bias, down_bias, live, page_gain, page_shift,
):
    devices, tok_rows, width = hall.shape
    chips, chunks = devices // 2, tok_rows // CHUNK
    piece, units = attended.shape[1], up_weight.shape[1]
    total = devices * tok_rows
    kept, kv_cols = pages.shape[0], kv_weights.shape[3]
    hbm, vmem = pl.BlockSpec(memory_space=pl.ANY), pl.BlockSpec(memory_space=pltpu.VMEM)
    dma = pltpu.SemaphoreType.DMA
    bf16 = jnp.bfloat16
    return pl.pallas_call(
        functools.partial(mlp_kernel, chips),
        in_specs=[hbm] * 7 + [vmem] * 8,
        out_specs=[vmem, hbm],
        out_shape=[
            jax.ShapeDtypeStruct((tok_rows, width), bf16),
            jax.ShapeDtypeStruct((kept // PAGE, PAGE, devices * kv_cols), bf16),
        ],
        scratch_shapes=[
            pltpu.VMEM((chunks, devices, CHUNK, width), bf16),
            pltpu.VMEM((width, width), bf16),
            pltpu.VMEM((width, units), bf16),
            pltpu.VMEM((units, width), bf16),
            pltpu.VMEM((2, devices, CHUNK, width), bf16),
            pltpu.VMEM((devices * CHUNK, width), bf16),
            pltpu.VMEM((devices * CHUNK, width), bf16),
            pltpu.VMEM((devices * CHUNK, units), bf16),
            pltpu.VMEM((tok_rows, width), bf16),
            pltpu.VMEM((chunks, chips, 2, CHUNK, width), bf16),
            pltpu.VMEM((chunks, chips, CHUNK, width), bf16),
            pltpu.VMEM((chunks, chips - 1, CHUNK, width), bf16),
            pltpu.VMEM((chunks, chips - 1, CHUNK, width), bf16),
            pltpu.VMEM(pages.shape, bf16),
            pltpu.VMEM((2,) + kv_weights.shape[:1] + kv_weights.shape[2:], bf16),
            pltpu.VMEM((2, kept // PAGE, PAGE, kv_cols), bf16),
            dma((2 + devices * out_weight.shape[0],)),
            dma((chunks,)),
            dma((2,)),
            dma((chunks, devices, 3)),
            dma((chunks, devices)),
            dma((chunks, 2)),
            dma((chunks, 2)),
            dma((chunks, 2, chips)),
            dma((chunks, 2, chips)),
            dma((5,)),
        ],
        compiler_params=pltpu.CompilerParams(
            collective_id=1, has_side_effects=True, vmem_limit_bytes=60 << 20
        ),
        cost_estimate=pl.CostEstimate(
            flops=2 * total * width * (width + 2 * units),
            bytes_accessed=2 * (2 * total * width + width * (width + 2 * units)),
            transcendentals=total * units,
        ),
        name="mlp_layer",
    )(
        attended.reshape(devices, tok_rows, piece),
        hall,
        out_weight,
        up_weight,
        down_weight,
        pages,
        kv_weights,
        out_bias.reshape(1, width),
        gain.reshape(1, width),
        shift.reshape(1, width),
        up_bias.reshape(1, units),
        down_bias.reshape(1, width),
        live,
        page_gain.reshape(1, width),
        page_shift.reshape(1, width),
    )


def attend_pages_kernel(
    most, count_ref, src_ref, proj_ref, kseg_ref, hall, out_ref, rows_ref, sem,
):
    block = pl.program_id(1)
    slots = rows_ref.shape[0] // PAGE
    copies = [
        pltpu.make_async_copy(hall.at[src_ref[0, i]], rows_ref.at[pl.ds(i * PAGE, PAGE)], sem.at[i])
        for i in range(slots)
    ]

    @pl.when(block == 0)
    def _():
        for copy in copies:
            copy.start()

    attend_kernel(most, count_ref, proj_ref, kseg_ref, out_ref)

    @pl.when(block == pl.num_programs(1) - 1)
    def _():
        for copy in copies:
            copy.wait()


def attend_pages(projected, segment_ids, counts, source, hall):
    streams, seq_len = segment_ids.shape
    heads = projected.shape[1] // (3 * HD)
    blocks = seq_len // Q_BLOCK
    devices, tok_rows, width = hall.shape
    slots = 2 * tok_rows // PAGE
    total = slots * PAGE
    most = min(blocks, MAX_DOC // Q_BLOCK + 1)
    pairs = streams * heads * seq_len * 2 * Q_BLOCK
    return pl.pallas_call(
        functools.partial(attend_pages_kernel, most),
        grid_spec=pltpu.PrefetchScalarGridSpec(
            num_scalar_prefetch=2,
            grid=(streams, blocks),
            in_specs=[
                pl.BlockSpec((seq_len, 3 * heads * HD), lambda s, i, counts, source: (s, 0)),
                pl.BlockSpec((1, 1, seq_len), lambda s, i, counts, source: (s, 0, 0)),
                pl.BlockSpec(memory_space=pl.ANY),
            ],
            out_specs=[
                pl.BlockSpec((Q_BLOCK, heads * HD), lambda s, i, counts, source: (s * blocks + i, 0)),
                pl.BlockSpec((total, width), lambda s, i, counts, source: (0, 0)),
            ],
            scratch_shapes=[pltpu.SemaphoreType.DMA((slots,))],
        ),
        out_shape=[
            jax.ShapeDtypeStruct((streams * seq_len, heads * HD), jnp.bfloat16),
            jax.ShapeDtypeStruct((total, width), jnp.bfloat16),
        ],
        compiler_params=pltpu.CompilerParams(vmem_limit_bytes=60 << 20),
        cost_estimate=pl.CostEstimate(
            flops=4 * pairs * HD,
            bytes_accessed=2 * projected.size * 2,
            transcendentals=pairs,
        ),
        name="attend",
    )(
        counts,
        source,
        projected,
        segment_ids.reshape(streams, 1, seq_len),
        hall.reshape(-1, PAGE, width),
    )


def on_line(
    hidden_in, attn_gain, attn_shift, qkv_weight, qkv_bias, out_weight, out_bias, mlp_gain,
    mlp_shift, up_weight, up_bias, down_weight, down_bias, segment_ids, prompt_lengths, page_table,
):
    devices = lax.axis_size("tensor")
    columns = lax.axis_size("dp")
    hall, projected, out_whole, kv_whole, counts, source, live = gather_project(
        hidden_in, qkv_weight, out_weight, qkv_bias, attn_gain, attn_shift, segment_ids,
        page_table, prompt_lengths, devices, columns,
    )
    attended, pages = attend_pages(
        projected.reshape(-1, projected.shape[2]), segment_ids, counts, source, hall
    )
    layer_out, kv_pages = mlp_layer(
        attended, hall, out_whole, up_weight, down_weight, pages, kv_whole, out_bias, mlp_gain,
        mlp_shift, up_bias, down_bias, live, attn_gain, attn_shift,
    )
    return (layer_out, kv_pages)


def on_device(
    hidden_in,
    attn_gain,
    attn_shift,
    qkv_weight,
    qkv_bias,
    out_weight,
    out_bias,
    mlp_gain,
    mlp_shift,
    up_weight,
    up_bias,
    down_weight,
    down_bias,
    segment_ids,
    prompt_lengths,
    page_table,
):
    devices = lax.axis_size("tensor")
    position = lax.axis_index("tensor")
    tok_rows, width = hidden_in.shape
    total_rows = tok_rows * devices
    streams, seq_len = segment_ids.shape
    whole_heads = qkv_weight.shape[1] % (3 * HD) == 0

    normed = normalize(hidden_in, attn_gain, attn_shift).astype(jnp.bfloat16)
    if not whole_heads:
        qkv_weight = join_pair(qkv_weight, 1, position)
        qkv_bias = join_pair(qkv_bias, 0, position)
    gathered = lax.all_gather(normed, "tensor", axis=0, tiled=True)
    projected = (
        jnp.dot(gathered, qkv_weight, preferred_element_type=jnp.float32)
        + qkv_bias.astype(jnp.float32)
    ).astype(jnp.bfloat16)
    heads_here = projected.shape[1] // (3 * HD)
    keys_vals = jnp.concatenate(
        [
            lax.slice_in_dim(projected, (3 * n + 1) * HD, (3 * n + 3) * HD, axis=1)
            for n in range(heads_here)
        ],
        axis=1,
    )
    if not whole_heads:
        half = keys_vals.shape[1] // 2
        keys_vals = lax.dynamic_slice_in_dim(keys_vals, position % 2 * half, half, 1)
    live = jnp.arange(seq_len, dtype=jnp.int32)[None, :] < prompt_lengths[:, None]
    pieces = pack_pages(
        keys_vals, live, page_table, 2 * (total_rows // PAGE) // devices, position
    )
    projected, pieces = lax.optimization_barrier((projected, pieces))
    received = send_pages(pieces)
    far, step = devices // 2, devices // 8
    attended = attend(projected, segment_ids)
    if not whole_heads:
        half = attended.shape[1] // 2
        attended = lax.dynamic_slice_in_dim(attended, position % 2 * half, half, 1)
    attended, received[far : far + step] = lax.optimization_barrier(
        (attended, received[far : far + step])
    )

    part = tok_rows // CHUNKS
    shaped = attended.reshape(devices, CHUNKS, part, attended.shape[1])
    sums = []
    for chunk in range(CHUNKS):
        rows = shaped[:, chunk].reshape(devices * part, -1)
        terms = jnp.dot(rows, out_weight, preferred_element_type=jnp.float32)
        sums.append(
            lax.psum_scatter(
                terms.astype(jnp.bfloat16), "tensor", scatter_dimension=0, tiled=True
            )
        )
    residuals, gathers = [], []
    for chunk in range(CHUNKS):
        hidden = lax.slice_in_dim(hidden_in, chunk * part, (chunk + 1) * part, axis=0)
        attn_sum = sums[chunk]
        if chunk == 0:
            attn_sum, received[far + step : far + 3 * step] = lax.optimization_barrier(
                (attn_sum, received[far + step : far + 3 * step])
            )
        else:
            attn_sum, residuals[-1], received, _ = lax.optimization_barrier(
                (attn_sum, residuals[-1], received, normed_mid)
            )
        residual_mid = (
            hidden.astype(jnp.float32) + attn_sum.astype(jnp.float32) + out_bias
        ).astype(jnp.bfloat16)
        normed_mid = normalize(residual_mid, mlp_gain, mlp_shift).astype(jnp.bfloat16)
        residuals.append(residual_mid)
        gathers.append(lax.all_gather(normed_mid, "tensor", axis=0, tiled=True))
    sums = []
    for chunk in range(CHUNKS):
        lifted = jnp.dot(gathers[chunk], up_weight, preferred_element_type=jnp.float32) + up_bias
        expanded = jax.nn.gelu(lifted, approximate=False).astype(jnp.bfloat16)
        expanded = lax.optimization_barrier(expanded)
        terms = jnp.dot(expanded, down_weight, preferred_element_type=jnp.float32)
        sums.append(
            lax.psum_scatter(
                terms.astype(jnp.bfloat16), "tensor", scatter_dimension=0, tiled=True
            )
        )
    kv_pages = lay_out_pages(received, position)
    outs = [
        (residual_mid.astype(jnp.float32) + mlp_sum.astype(jnp.float32) + down_bias).astype(
            jnp.bfloat16
        )
        for residual_mid, mlp_sum in zip(residuals, sums)
    ]
    layer_out = outs[0] if CHUNKS == 1 else jnp.concatenate(outs, axis=0)
    return (layer_out, kv_pages)


def solution(mesh):
    in_specs = (
        P(("dp", "tensor"), None),
        P(),
        P(),
        P(None, "tensor"),
        P("tensor"),
        P("tensor", None),
        P(),
        P(),
        P(),
        P(None, "tensor"),
        P("tensor"),
        P("tensor", None),
        P(),
        P("dp", None),
        P("dp"),
        P("dp", None),
    )
    out_specs = (P(("dp", "tensor"), None), P(("dp", "tensor"), None, None))
    body = on_line if (mesh.shape["dp"], mesh.shape["tensor"]) == SQUARE_LINE else on_device
    return jax.shard_map(
        body, mesh=mesh, in_specs=in_specs, out_specs=out_specs, check_vma=False
    )
```
